512 devices in a mesh: dp: 16 (over z_lo, y), mp: 8 (over z_hi, core), section: 4 (over x).
Axes of the slice: x: 4, y: 8, z: 8 (z_hi: 4, z_lo: 2; z = z_hi * 2 + z_lo), core: 2. Of those that a mesh axis runs over, the one named last changes fastest.
Arguments:
- states: bfloat16 [16384, 8192], P(('dp', 'section'), 'mp'), may hold values from -6 to 6
- direction: bfloat16 [16384, 1024], P(('dp', 'section'), 'mp'), may hold values from -0.09375 to 0.09375
- old_logp: bfloat16 [16384], P(('dp', 'section')), may hold values from -4 to -0.049804688
- lengths: int32 [128], P(('dp', 'section')), may hold values from 1 to 128, as said below
- group_ids: int32 [128], P(('dp', 'section')), may hold values from 0 to 15, as said below
- routes: int32 [16384, 1], P(('dp', 'section')), may hold values from 0 to 15; in each aligned block of 256 rows (0 to 255, 256 to 511, ...) at most 20 rows name the same one
- reward_head: bfloat16 [8192], P('mp'), may hold values from -0.0625 to 0.0625
- policy_k: bfloat16 [8192, 1024], P(('dp', 'section'), 'mp'), may hold values from -0.0625 to 0.0625
- reference_k: bfloat16 [8192, 1024], P(('dp', 'section'), 'mp'), may hold values from -0.0625 to 0.0625
Outputs:
- grad_k: float32 [8192, 1024], P(('dp', 'section'), 'mp')
- packed_logp: float32 [16, 4, 320], P('dp', 'section')
The draws below stay inside these ranges and needn't reach their ends.
Inputs may be any that keep to these rules, and one draw needn't show every extreme that they name: `lengths`: some response has all 128 tokens valid. `group_ids`: each prompt id is held by exactly 8 responses. `routes`: among the rows of one rollout device at most 20 name the same learner shard, a bound that some block reaches of them.
All inputs are finite; a program needn't handle non-finite values.
Results may differ from the reference program's by a relative error of at most 0.004.
Values may be sent and summed in bfloat16 or wider, within the bound.
No kernel may reach another device: no remote copies, remote signals or barrier semaphores. Data moves between devices by JAX's collectives and lax.ppermute only.
A program may use at most 64 MiB of HBM per device.

```python
import math
import jax
import jax.numpy as jnp
import numpy as np
from jax import lax

D = 8192
SEQ_LEN = 128
GROUP = 8
KVW = 1024
TOK_DEV = 256
NSEQ = 128
ROWS = 16384
NGROUPS = 16
CAP = 20
N_DP = 16
N_SECTION = 4


def draw_lengths(key, part):
    key_values, key_spot = jax.random.split(key)
    values = jax.random.randint(key_values, (NSEQ,), 1, SEQ_LEN + 1)
    spot = jax.random.randint(key_spot, (), 0, NSEQ)
    return values.at[spot].set(SEQ_LEN).astype(jnp.int32)


def draw_group_ids(key, part):
    return (jax.random.permutation(key, NSEQ) // GROUP).astype(jnp.int32)


def block_levels(key, dims, shards, least, high):
    factor_of = 1.0
    for axis_at, shards_of in shards:
        heights = jax.random.uniform(jax.random.fold_in(jax.random.fold_in(key, 6), axis_at), (shards_of,), jnp.float32, least / len(shards), high / len(shards))
        factor_of = factor_of * jnp.repeat(jnp.exp(heights), dims[axis_at] // shards_of).reshape((-1,) + (1,) * (len(dims) - 1 - axis_at))
    return factor_of


def shared_out(stream_key, own, number, rows, amount, top, limit, lean):
    ranking = jax.random.permutation(stream_key, amount)
    heavy_load, common = load_shares(amount, rows * top, limit, lean, True), load_shares(amount, rows * top, limit, lean, False)
    places = jnp.arange(amount)

    def named(tallies, offset_by):
        used = int((tallies > 0).sum())
        fixed = max(1, used // 4)
        shifted = fixed + (places - fixed + offset_by * (used - fixed)) % max(1, amount - fixed)
        return jnp.zeros((amount,), jnp.int32).at[ranking[jnp.where(places < fixed, places, shifted)]].set(jnp.asarray(tallies, jnp.int32))

    tallies = jnp.where(number % 4 == 0, named(heavy_load, number // 4), named(common, number - number // 4 - 1))
    mixed = jax.random.permutation(jax.random.fold_in(own, 3), amount)
    source_of, receiver = mixed[0:amount // 2 * 2:2], mixed[1:amount // 2 * 2:2]
    room = jnp.minimum(tallies[source_of] - 1, limit - tallies[receiver]) // 2
    room = jnp.where((source_of == ranking[0]) | (receiver == ranking[0]) | (tallies[receiver] == 0), 0, jnp.maximum(room, 0))
    shifted = jax.random.randint(jax.random.fold_in(own, 4), (amount // 2,), 0, 1 << 20) % (room + 1)
    tallies = tallies.at[source_of].add(-shifted).at[receiver].add(shifted)
    items = jnp.searchsorted(jnp.cumsum(tallies), jnp.arange(rows * top), side="right").astype(jnp.int32)
    listing = items.reshape(top, rows).T
    listing = listing[jax.random.permutation(jax.random.fold_in(own, 1), rows)]
    offset_by = jax.random.randint(jax.random.fold_in(own, 2), (rows, 1), 0, top)
    return jnp.take_along_axis(listing, (jnp.arange(top)[None, :] + offset_by) % top, axis=1)


def load_shares(amount, total, bound, slope, full):
    portions = [(1 << 20) // math.isqrt(grade ** slope) + 1 for grade in range(1, amount + 1)]
    largest = bound if full else min(bound, max(-(-total // amount), total * portions[0] // sum(portions)))
    least = 1 if total - largest >= amount - 1 else 0
    holding, spare = [largest] + [least] * (amount - 1), total - largest - least * (amount - 1)
    while spare > 0:
        free = [i for i in range(1, amount) if holding[i] < largest] or [i for i in range(1, amount) if holding[i] < bound]
        mass, remaining = sum([portions[i] for i in free]), spare
        for i in free:
            more = min(bound - holding[i], max(1, remaining * portions[i] // mass), spare)
            holding[i] = holding[i] + more
            spare = spare - more
    return np.array(holding)


def centred(stream_key, shape, deviation, bound, cuts=(), held_as=jnp.bfloat16):
    array = deviation * jax.random.normal(stream_key, shape, jnp.float32)
    if cuts:
        array = array * block_levels(stream_key, shape, cuts, -0.22, 0.18)
    return jnp.clip(array, -bound, bound).astype(held_as)


def setup_inputs(seed: int = 0) -> dict:
    arg_keys = jax.random.split(jax.random.key(seed), 10)
    states = centred(arg_keys[0], (ROWS, D), 1.0, 6.0, ((0, 64), (1, 8)))
    direction = centred(arg_keys[1], (ROWS, KVW), (4 * KVW) ** -0.5, 0.09375, ((0, 64), (1, 8)))
    old_logp = jnp.clip(-4.0 + 3.9501953 * jax.random.uniform(arg_keys[2], (ROWS,), jnp.float32) ** block_levels(arg_keys[2], (ROWS,), ((0, 64),), -0.2, 0.2), -4.0, -0.049804688).astype(jnp.bfloat16)
    lengths = draw_lengths(jax.random.fold_in(arg_keys[9], 71), 0)
    group_ids = draw_group_ids(jax.random.fold_in(arg_keys[9], 71), 0)
    routes_keys = jax.random.split(jax.random.fold_in(arg_keys[5], 1), ROWS // TOK_DEV)
    routes_turns = jax.random.permutation(jax.random.fold_in(arg_keys[5], 3), ROWS // TOK_DEV)
    routes = jax.vmap(lambda own, number: shared_out(jax.random.fold_in(arg_keys[5], 2), own, number, TOK_DEV, N_DP, 1, CAP, 2))(routes_keys, routes_turns).reshape((ROWS, 1))
    reward_head = centred(arg_keys[6], (D,), D ** -0.5, 0.0625, ((0, 8),))
    policy_k = centred(arg_keys[7], (D, KVW), D ** -0.5, 0.0625, ((0, 64), (1, 8)))
    reference_k = centred(arg_keys[8], (D, KVW), D ** -0.5, 0.0625, ((0, 64), (1, 8)))
    return dict(states=states, direction=direction, old_logp=old_logp, lengths=lengths, group_ids=group_ids, routes=routes, reward_head=reward_head, policy_k=policy_k, reference_k=reference_k)


kl_weight = 0.4
var_offset = 0.25

def reference(states, direction, old_logp, lengths, group_ids, routes, reward_head, policy_k, reference_k):
    score = jnp.dot(states, reward_head, preferred_element_type=jnp.float32)
    valid = (jnp.arange(SEQ_LEN, dtype=jnp.int32)[None, :] < lengths[:, None]).astype(jnp.float32)
    reward = lax.optimization_barrier(jnp.sum(score.reshape(NSEQ, SEQ_LEN) * valid, axis=1)) / jnp.sqrt(lengths.astype(jnp.float32))
    member = (group_ids[:, None] == jnp.arange(NGROUPS, dtype=jnp.int32)[None, :]).astype(jnp.float32)
    totals = lax.optimization_barrier(jnp.sum(member * reward[:, None], axis=0))
    squares = lax.optimization_barrier(jnp.sum(member * (reward * reward)[:, None], axis=0))
    center = totals / GROUP
    spread = squares / GROUP - center * center
    own_center = lax.optimization_barrier(jnp.sum(member * center[None, :], axis=1))
    own_spread = lax.optimization_barrier(jnp.sum(member * spread[None, :], axis=1))
    advantage = ((reward - own_center) / jnp.sqrt(own_spread + var_offset)).astype(jnp.bfloat16)
    key_policy = jnp.dot(states, policy_k, preferred_element_type=jnp.float32)
    key_reference = jnp.dot(states, reference_k, preferred_element_type=jnp.float32)
    dir_wide = direction.astype(jnp.float32)
    term_policy = lax.optimization_barrier(jnp.sum(dir_wide * key_policy, axis=1))
    term_reference = lax.optimization_barrier(jnp.sum(dir_wide * key_reference, axis=1))
    logp = old_logp.astype(jnp.float32) + term_policy
    adv_rows = jnp.repeat(advantage.astype(jnp.float32), SEQ_LEN)
    valid_rows = valid.reshape(ROWS)
    coef = valid_rows * (-adv_rows * jnp.exp(term_policy) + kl_weight * (1.0 - jnp.exp(term_reference - term_policy)))
    change = (coef[:, None] * dir_wide).astype(jnp.bfloat16)
    grad_k = jnp.dot(states.T, change, preferred_element_type=jnp.float32)
    target = routes[:, 0]
    blocks = N_DP * N_SECTION
    choose = (target.reshape(blocks, TOK_DEV)[:, :, None] == jnp.arange(N_DP, dtype=jnp.int32)[None, None, :]).astype(jnp.int32)
    ranked = jnp.cumsum(choose, axis=1) - 1
    within = lax.optimization_barrier(jnp.sum(ranked * choose, axis=2)).reshape(ROWS)
    block_of = jnp.arange(ROWS, dtype=jnp.int32) // TOK_DEV
    source_dp = block_of // N_SECTION
    section_of = block_of % N_SECTION
    packed_logp = jnp.zeros((N_DP, N_SECTION, N_DP * CAP), jnp.float32)
    packed_logp = packed_logp.at[target, section_of, source_dp * CAP + within].set(logp)
    return (grad_k, packed_logp)
```

```python
import jax
import jax.numpy as jnp
from jax import lax
from jax.experimental import pallas as pl
from jax.experimental.pallas import tpu as pltpu
from jax.sharding import Mesh
from jax.sharding import PartitionSpec as P

GROUP = 8
NGROUPS = 16
CAP = 20
SLOT = 32

kl_weight = 0.4
var_offset = 0.25

DP = ("zl", "y")
ALL = ("zl", "y", "zh", "core", "sec")
BF = jnp.bfloat16
F32 = jnp.float32
NT = (((1,), (1,)), ((), ()))


def split3(x):
    hi = x.astype(BF).astype(F32)
    rest = x - hi
    mid = rest.astype(BF).astype(F32)
    return hi, mid, rest - mid


def dp_index():
    return lax.axis_index("zl") * 8 + lax.axis_index("y")


def prepare_kernel(
    lengths, group_ids, states, direction, head, routes, wp, wr,
    quarters, dir_t, w_t, extra, slots,
):
    for k in range(4):
        quarters[k] = states[:, 256 * k : 256 * (k + 1)]
    dir_t[...] = direction[...].astype(F32).T.astype(BF)
    w_t[0:128, :] = wp[...].astype(F32).T.astype(BF)
    w_t[128:256, :] = wr[...].astype(F32).T.astype(BF)
    score = lax.dot_general(
        jnp.broadcast_to(head[...], (8, 1024)), states[...], NT, preferred_element_type=F32
    )
    lane = lax.broadcasted_iota(jnp.int32, (1, 128), 1)
    rows = []
    for q in range(2):
        valid = (lane < lengths[q]).astype(F32)
        part = jnp.sum(score[0:1, 128 * q : 128 * (q + 1)] * valid, axis=1, keepdims=True)
        rows.extend(split3(part))
    for values in (group_ids, lengths):
        for q in range(2):
            rows.append(jnp.full((1, 1), values[q], jnp.int32).astype(F32))
    at = lax.broadcasted_iota(jnp.int32, (16, 128), 0)
    block = jnp.zeros((16, 128), F32)
    for n, row in enumerate(rows):
        block = jnp.where(at == n, row, block)
    extra[...] = block.astype(BF)
    target = routes[...]
    choose = (lax.broadcasted_iota(jnp.int32, (16, 256), 0) == target).astype(F32)
    before = (
        lax.broadcasted_iota(jnp.int32, (256, 256), 0)
        < lax.broadcasted_iota(jnp.int32, (256, 256), 1)
    ).astype(F32)
    ranked = jnp.dot(choose.astype(BF), before.astype(BF), preferred_element_type=F32)
    rank = jnp.sum(choose * ranked, axis=0, keepdims=True)
    slots[...] = target * SLOT + rank.astype(jnp.int32)


def terms_kernel(own, other, weights, dir_t, out, pay):
    core = lax.axis_index("core")
    acc = [jnp.zeros((2, 256), F32) for _ in range(4)]
    for z in range(4):
        mats = []
        for u in (core, 1 - core):
            mats.append(
                jnp.concatenate(
                    [weights[u * 8 + z, 0:256, :], weights[u * 8 + 4 + z, 0:256, :]], axis=1
                )
            )
        for s in range(4):
            key = lax.dot_general(mats[0], own[s], NT, preferred_element_type=F32)
            key += lax.dot_general(mats[1], other[s], NT, preferred_element_type=F32)
            wide = dir_t[z, s].astype(F32)
            acc[s] += jnp.concatenate(
                [
                    jnp.sum(wide * key[0:128], axis=0, keepdims=True),
                    jnp.sum(wide * key[128:256], axis=0, keepdims=True),
                ],
                axis=0,
            )
    for s in range(4):
        for p in range(2):
            for q in range(2):
                n = 8 * p + 2 * s + q
                pay[n : n + 1, :] = acc[s][p : p + 1, 128 * q : 128 * (q + 1)]
    lane = lax.broadcasted_iota(jnp.int32, (16, 128), 1)
    block = jnp.zeros((16, 128), F32)
    for i in range(16):
        block = jnp.where(lane == i, weights[i, 256:272, :].astype(F32), block)
    pay[16:17, :] = block[0:1] + block[1:2] + block[2:3]
    pay[17:18, :] = block[3:4] + block[4:5] + block[5:6]
    pay[18:22, :] = block[6:10]
    pay[22:24, :] = jnp.zeros((2, 128), F32)
    whole = pay[...]
    for d in range(32):
        out[d] = whole


def grads_kernel(pays, own, other, dir_t, old_logp, slots, out, change):
    core, dp, sec = lax.axis_index("core"), dp_index(), lax.axis_index("sec")
    terms = pays[0, 0:16, :]
    for d in range(1, 32):
        terms = terms + pays[d, 0:16, :]
    tp, tr = terms[0:8], terms[8:16]
    facts = []
    for s in range(4):
        fact = pays[s, 16:24, :]
        for d in range(1, 8):
            fact = fact + pays[4 * d + s, 16:24, :]
        facts.append(fact)
    lane = lax.broadcasted_iota(jnp.int32, (8, 128), 1)
    used = lane < 16
    sums = jnp.concatenate([f[0:2] for f in facts], axis=0)
    ids = jnp.concatenate([f[2:4] for f in facts], axis=0) * 0.125
    lens = jnp.where(used, jnp.concatenate([f[4:6] for f in facts], axis=0) * 0.125, 1.0)
    reward = sums / jnp.sqrt(lens)
    center = jnp.zeros((8, 128), F32)
    spread = jnp.zeros((8, 128), F32)
    for g in range(NGROUPS):
        member = used & (ids == float(g))
        mine = jnp.where(member, reward, 0.0)
        total = jnp.sum(jnp.sum(mine, axis=0, keepdims=True), axis=1, keepdims=True)
        square = jnp.sum(jnp.sum(mine * mine, axis=0, keepdims=True), axis=1, keepdims=True)
        mid = total / GROUP
        center = jnp.where(member, mid, center)
        spread = jnp.where(member, square / GROUP - mid * mid, spread)
    advantage = ((reward - center) / jnp.sqrt(spread + var_offset)).astype(BF).astype(F32)
    here = lane == dp
    adv = jnp.sum(jnp.where(here, advantage, 0.0), axis=1, keepdims=True)
    length = jnp.sum(jnp.where(here, lens, 0.0), axis=1, keepdims=True)
    valid = (lane.astype(F32) < length).astype(F32)
    coef = valid * (-adv * jnp.exp(tp) + kl_weight * (1.0 - jnp.exp(tr - tp)))
    for z in range(4):
        for s in range(4):
            row = jnp.concatenate([coef[2 * s : 2 * s + 1], coef[2 * s + 1 : 2 * s + 2]], axis=1)
            change[128 * z : 128 * (z + 1), 256 * s : 256 * (s + 1)] = (
                dir_t[z, s].astype(F32) * row
            ).astype(BF)
    for u, part in ((core, own), (1 - core, other)):
        grad = jnp.dot(
            change[...], part[...].reshape(1024, 256), preferred_element_type=F32
        ).astype(BF)
        for v in range(2):
            for z in range(4):
                out[u * 8 + v * 4 + z, 0:128, :] = grad[
                    128 * z : 128 * (z + 1), 128 * v : 128 * (v + 1)
                ]
    at = lax.broadcasted_iota(jnp.int32, (8, 128), 0)
    halves = [
        jnp.sum(jnp.where(at == 2 * sec + q, tp, 0.0), axis=0, keepdims=True) for q in range(2)
    ]
    logp = old_logp[...].astype(F32) + jnp.concatenate(halves, axis=1)
    hi, mid, lo = split3(logp)
    rows = jnp.concatenate([hi, mid, lo, jnp.zeros((5, 256), F32)], axis=0).astype(BF)
    place = (lax.broadcasted_iota(jnp.int32, (16 * SLOT, 256), 0) == slots[...]).astype(F32)
    placed = lax.dot_general(rows, place.astype(BF), NT, preferred_element_type=F32)
    tail = jnp.concatenate(
        [placed[h : h + 1, 128 * a : 128 * (a + 1)] for h in range(3) for a in range(4)]
        + [jnp.zeros((4, 128), F32)],
        axis=0,
    ).astype(BF)
    for k in range(16):
        out[k, 128:144, :] = tail


def finish_kernel(parts, grad, packed):
    dp = dp_index()
    total = parts[0, 0:128, :].astype(F32)
    for i in range(1, 16):
        total = total + parts[i, 0:128, :].astype(F32)
    grad[...] = total.T
    at = lax.broadcasted_iota(jnp.int32, (16, 128), 0)
    mine = (at < 12) & (lax.rem(at, 4) == dp // 4)
    rows = []
    for i in range(16):
        tail = jnp.where(mine, parts[i, 128:144, :].astype(F32), 0.0)
        rows.append(jnp.sum(tail, axis=0, keepdims=True))
    table = jnp.concatenate(rows, axis=0)
    pick = jnp.zeros((16, SLOT), F32)
    for a in range(4):
        pick = jnp.where(lax.rem(dp, 4) == a, table[:, SLOT * a : SLOT * (a + 1)], pick)
    packed[...] = jnp.concatenate([pick[i : i + 1, 0:CAP] for i in range(16)], axis=1)


def cost(flops, size):
    return pl.CostEstimate(flops=flops, bytes_accessed=size, transcendentals=0)


def shape(dims, dtype):
    return jax.ShapeDtypeStruct(dims, dtype)


def call(kernel, outs, scratch=(), smem=0, inputs=0, flops=0, size=0):
    vmem = pl.BlockSpec(memory_space=pltpu.VMEM)
    scalar = pl.BlockSpec(memory_space=pltpu.SMEM)
    return pl.pallas_call(
        kernel,
        out_shape=outs,
        in_specs=[scalar] * smem + [vmem] * inputs,
        out_specs=jax.tree.map(lambda _: vmem, outs),
        scratch_shapes=list(scratch),
        cost_estimate=cost(flops, size),
    )


def flat(i, zh, core, sec):
    return ((i * 4 + zh) * 2 + core) * 4 + sec


TO_HANDLER = [
    (
        flat(i, zh, core, sec),
        flat(((i >> 1) & 1) * 8 + (sec & 1) * 4 + zh, i >> 2, core, 2 * (i & 1) + (sec >> 1)),
    )
    for i in range(16)
    for zh in range(4)
    for core in range(2)
    for sec in range(4)
]
TO_OWNER = [(b, a) for a, b in TO_HANDLER]


def body(
    states, direction, old_logp, lengths, group_ids, routes, reward_head, policy_k, reference_k
):
    quarters, dir_t, w_t, extra, slots = call(
        prepare_kernel,
        (
            shape((4, 256, 256), BF),
            shape((128, 256), BF),
            shape((256, 128), BF),
            shape((16, 128), BF),
            shape((1, 256), jnp.int32),
        ),
        smem=2,
        inputs=6,
        flops=8 * 256 * 1024 * 2,
        size=1 << 20,
    )(
        lengths,
        group_ids,
        states,
        direction,
        reward_head.reshape(1, 1024),
        routes.reshape(1, 256),
        policy_k,
        reference_k,
    )
    w_here = lax.ppermute(w_t, ALL, TO_HANDLER)
    own = lax.all_to_all(quarters, "sec", 0, 0, tiled=True)
    other = lax.ppermute(own, "core", [(0, 1), (1, 0)])
    dirs = lax.all_to_all(
        jnp.broadcast_to(dir_t[None], (16, 128, 256)), ("zh", "sec"), 0, 0, tiled=True
    ).reshape(4, 4, 128, 256)
    w_pack = jnp.concatenate([w_here, extra], axis=0)
    weights = lax.all_to_all(
        jnp.broadcast_to(w_pack[None], (16, 272, 128)), DP, 0, 0, tiled=True
    )
    pays = call(
        terms_kernel,
        shape((32, 24, 128), F32),
        scratch=[pltpu.VMEM((24, 128), F32)],
        inputs=4,
        flops=1 << 30,
        size=4 << 20,
    )(own, other, weights, dirs)
    pays = lax.all_to_all(pays, ("zh", "core", "sec"), 0, 0, tiled=True)
    parts = call(
        grads_kernel,
        shape((16, 144, 128), BF),
        scratch=[pltpu.VMEM((512, 1024), BF)],
        inputs=6,
        flops=1 << 29,
        size=4 << 20,
    )(pays, own, other, dirs, old_logp.reshape(1, 256), slots)
    parts = lax.all_to_all(parts, DP, 0, 0, tiled=True)
    grad, packed = call(
        finish_kernel,
        (shape((128, 128), F32), shape((1, 320), F32)),
        inputs=1,
        flops=1 << 20,
        size=1 << 20,
    )(parts)
    return lax.ppermute(grad, ALL, TO_OWNER), packed.reshape(1, 1, 320)


def solution(mesh):
    fine = Mesh(mesh.devices.reshape(2, 8, 4, 2, 4), ALL)
    rows, cols = ("zl", "y", "sec"), ("zh", "core")
    return jax.shard_map(
        body,
        mesh=fine,
        in_specs=(
            P(rows, cols),
            P(rows, cols),
            P(rows),
            P(rows),
            P(rows),
            P(rows, None),
            P(cols),
            P(rows, cols),
            P(rows, cols),
        ),
        out_specs=(P(rows, cols), P(DP, "sec", None)),
        check_vma=False,
    )
```

```python
import jax
import jax.numpy as jnp
from jax import lax
from jax.experimental import pallas as pl
from jax.experimental.pallas import tpu as pltpu
from jax.sharding import Mesh
from jax.sharding import PartitionSpec as P

GROUP = 8
NGROUPS = 16
CAP = 20
SLOT = 32

kl_weight = 0.4
var_offset = 0.25

DP = ("zl", "y")
ALL = ("zl", "y", "zh", "core", "sec")
BF = jnp.bfloat16
F32 = jnp.float32
NT = (((1,), (1,)), ((), ()))


def split3(x):
    hi = x.astype(BF).astype(F32)
    rest = x - hi
    mid = rest.astype(BF).astype(F32)
    return hi, mid, rest - mid


def dp_index():
    return lax.axis_index("zl") * 8 + lax.axis_index("y")


def prepare_kernel(
    lengths, group_ids, states, direction, head, routes, wp, wr,
    quarters, dir_t, w_t, extra, slots,
):
    sec = lax.axis_index("sec")
    for k in range(4):
        whole = states[:, 256 * k : 256 * (k + 1)]
        quarters[lax.rem(k - sec + 4, 4)] = whole
    turned = direction[...].astype(F32).T.astype(BF)
    for k in range(4):
        dir_t[k] = turned
    w_t[0:128, :] = wp[...].astype(F32).T.astype(BF)
    w_t[128:256, :] = wr[...].astype(F32).T.astype(BF)
    head_rows = head[...].astype(F32)
    wide_head = jnp.concatenate([head_rows[k : k + 1] for k in range(8)], axis=1).astype(BF)
    score = lax.dot_general(
        jnp.broadcast_to(wide_head, (8, 1024)), states[...], NT, preferred_element_type=F32
    )
    lane = lax.broadcasted_iota(jnp.int32, (1, 128), 1)
    rows = []
    for q in range(2):
        valid = (lane < lengths[q]).astype(F32)
        part = jnp.sum(score[0:1, 128 * q : 128 * (q + 1)] * valid, axis=1, keepdims=True)
        rows.extend(split3(part))
    for values in (group_ids, lengths):
        for q in range(2):
            rows.append(jnp.full((1, 1), values[q], jnp.int32).astype(F32))
    at = lax.broadcasted_iota(jnp.int32, (16, 128), 0)
    block = jnp.zeros((16, 128), F32)
    for n, row in enumerate(rows):
        block = jnp.where(at == n, row, block)
    extra[...] = block.astype(BF)
    target = routes[...]
    choose = (lax.broadcasted_iota(jnp.int32, (16, 256), 0) == target).astype(F32)
    before = (
        lax.broadcasted_iota(jnp.int32, (256, 256), 0)
        < lax.broadcasted_iota(jnp.int32, (256, 256), 1)
    ).astype(F32)
    ranked = jnp.dot(choose.astype(BF), before.astype(BF), preferred_element_type=F32)
    rank = jnp.sum(choose * ranked, axis=0, keepdims=True)
    slots[...] = target * SLOT + rank.astype(jnp.int32)


def terms_kernel(own, other, weights, dir_t, out, pay):
    core, sec = lax.axis_index("core"), lax.axis_index("sec")
    acc = [jnp.zeros((2, 256), F32) for _ in range(4)]
    for z in range(4):
        mats = []
        for u in (core, 1 - core):
            mats.append(
                jnp.concatenate(
                    [weights[u * 8 + z, 0:256, :], weights[u * 8 + 4 + z, 0:256, :]], axis=1
                )
            )
        for s in range(4):
            key = lax.dot_general(mats[0], own[s], NT, preferred_element_type=F32)
            key += lax.dot_general(mats[1], other[s], NT, preferred_element_type=F32)
            wide = dir_t[lax.rem(sec - s + 4, 4), z].astype(F32)
            acc[s] += jnp.concatenate(
                [
                    jnp.sum(wide * key[0:128], axis=0, keepdims=True),
                    jnp.sum(wide * key[128:256], axis=0, keepdims=True),
                ],
                axis=0,
            )
    for s in range(4):
        for p in range(2):
            for q in range(2):
                n = 8 * p + 2 * lax.rem(sec - s + 4, 4) + q
                pay[pl.ds(n, 1), :] = acc[s][p : p + 1, 128 * q : 128 * (q + 1)]
    lane = lax.broadcasted_iota(jnp.int32, (16, 128), 1)
    block = jnp.zeros((16, 128), F32)
    for i in range(16):
        block = jnp.where(lane == i, weights[i, 256:272, :].astype(F32), block)
    pay[16:17, :] = block[0:1] + block[1:2] + block[2:3]
    pay[17:18, :] = block[3:4] + block[4:5] + block[5:6]
    pay[18:22, :] = block[6:10]
    pay[22:24, :] = jnp.zeros((2, 128), F32)
    whole = pay[...]
    for d in range(32):
        out[d] = whole


def grads_kernel(pays, own, other, dir_t, old_logp, slots, out, change, coefs):
    core, dp, sec = lax.axis_index("core"), dp_index(), lax.axis_index("sec")
    terms = pays[0, 0:16, :]
    for d in range(1, 32):
        terms = terms + pays[d, 0:16, :]
    tp, tr = terms[0:8], terms[8:16]
    facts = []
    for s in range(4):
        fact = pays[s, 16:24, :]
        for d in range(1, 8):
            fact = fact + pays[4 * d + s, 16:24, :]
        facts.append(fact)
    lane = lax.broadcasted_iota(jnp.int32, (8, 128), 1)
    used = lane < 16
    sums = jnp.concatenate([f[0:2] for f in facts], axis=0)
    ids = jnp.concatenate([f[2:4] for f in facts], axis=0) * 0.125
    lens = jnp.where(used, jnp.concatenate([f[4:6] for f in facts], axis=0) * 0.125, 1.0)
    reward = sums / jnp.sqrt(lens)
    center = jnp.zeros((8, 128), F32)
    spread = jnp.zeros((8, 128), F32)
    for g in range(NGROUPS):
        member = used & (ids == float(g))
        mine = jnp.where(member, reward, 0.0)
        total = jnp.sum(jnp.sum(mine, axis=0, keepdims=True), axis=1, keepdims=True)
        square = jnp.sum(jnp.sum(mine * mine, axis=0, keepdims=True), axis=1, keepdims=True)
        mid = total / GROUP
        center = jnp.where(member, mid, center)
        spread = jnp.where(member, square / GROUP - mid * mid, spread)
    advantage = ((reward - center) / jnp.sqrt(spread + var_offset)).astype(BF).astype(F32)
    here = lane == dp
    adv = jnp.sum(jnp.where(here, advantage, 0.0), axis=1, keepdims=True)
    length = jnp.sum(jnp.where(here, lens, 0.0), axis=1, keepdims=True)
    valid = (lane.astype(F32) < length).astype(F32)
    coef = valid * (-adv * jnp.exp(tp) + kl_weight * (1.0 - jnp.exp(tr - tp)))
    coefs[...] = coef
    for s in range(4):
        at = lax.rem(sec - s + 4, 4)
        row = jnp.concatenate(
            [coefs[pl.ds(2 * at, 1), :], coefs[pl.ds(2 * at + 1, 1), :]], axis=1
        )
        for z in range(4):
            change[128 * z : 128 * (z + 1), 256 * s : 256 * (s + 1)] = (
                dir_t[at, z].astype(F32) * row
            ).astype(BF)
    for u, part in ((core, own), (1 - core, other)):
        grad = jnp.dot(
            change[...], part[...].reshape(1024, 256), preferred_element_type=F32
        ).astype(BF)
        for v in range(2):
            for z in range(4):
                out[u * 8 + v * 4 + z, 0:128, :] = grad[
                    128 * z : 128 * (z + 1), 128 * v : 128 * (v + 1)
                ]
    at = lax.broadcasted_iota(jnp.int32, (8, 128), 0)
    old = old_logp[...].astype(F32)
    logp = jnp.concatenate(
        [
            old[q : q + 1] + jnp.sum(jnp.where(at == 2 * sec + q, tp, 0.0), axis=0, keepdims=True)
            for q in range(2)
        ],
        axis=1,
    )
    hi, mid, lo = split3(logp)
    rows = jnp.concatenate([hi, mid, lo, jnp.zeros((5, 256), F32)], axis=0).astype(BF)
    place = (lax.broadcasted_iota(jnp.int32, (16 * SLOT, 256), 0) == slots[...]).astype(F32)
    placed = lax.dot_general(rows, place.astype(BF), NT, preferred_element_type=F32)
    tail = jnp.concatenate(
        [placed[h : h + 1, 128 * a : 128 * (a + 1)] for h in range(3) for a in range(4)]
        + [jnp.zeros((4, 128), F32)],
        axis=0,
    ).astype(BF)
    for k in range(16):
        out[k, 128:144, :] = tail


def finish_kernel(parts, grad, packed):
    dp = dp_index()
    total = parts[0, 0:128, :].astype(F32)
    for i in range(1, 16):
        total = total + parts[i, 0:128, :].astype(F32)
    grad[...] = total.T
    at = lax.broadcasted_iota(jnp.int32, (16, 128), 0)
    mine = (at < 12) & (lax.rem(at, 4) == dp // 4)
    rows = []
    for i in range(16):
        tail = jnp.where(mine, parts[i, 128:144, :].astype(F32), 0.0)
        rows.append(jnp.sum(tail, axis=0, keepdims=True))
    table = jnp.concatenate(rows, axis=0)
    pick = jnp.zeros((16, SLOT), F32)
    for a in range(4):
        pick = jnp.where(lax.rem(dp, 4) == a, table[:, SLOT * a : SLOT * (a + 1)], pick)
    packed[...] = jnp.concatenate([pick[i : i + 1, 0:CAP] for i in range(16)], axis=1)


def cost(flops, size):
    return pl.CostEstimate(flops=flops, bytes_accessed=size, transcendentals=0)


def shape(dims, dtype):
    return jax.ShapeDtypeStruct(dims, dtype)


def call(kernel, outs, scratch=(), smem=0, inputs=0, flops=0, size=0, vmem_mib=16):
    vmem = pl.BlockSpec(memory_space=pltpu.VMEM)
    scalar = pl.BlockSpec(memory_space=pltpu.SMEM)
    return pl.pallas_call(
        kernel,
        out_shape=outs,
        in_specs=[scalar] * smem + [vmem] * inputs,
        out_specs=jax.tree.map(lambda _: vmem, outs),
        scratch_shapes=list(scratch),
        cost_estimate=cost(flops, size),
        compiler_params=pltpu.CompilerParams(vmem_limit_bytes=vmem_mib << 20),
    )


def flat(i, zh, core, sec):
    return ((i * 4 + zh) * 2 + core) * 4 + sec


TO_HANDLER = [
    (
        flat(i, zh, core, sec),
        flat(((i >> 1) & 1) * 8 + (sec & 1) * 4 + zh, i >> 2, core, 2 * (i & 1) + (sec >> 1)),
    )
    for i in range(16)
    for zh in range(4)
    for core in range(2)
    for sec in range(4)
]
TO_OWNER = [(b, a) for a, b in TO_HANDLER]


def body(
    states, direction, old_logp, lengths, group_ids, routes, reward_head, policy_k, reference_k
):
    quarters, dir_t, w_t, extra, slots = call(
        prepare_kernel,
        (
            shape((4, 256, 256), BF),
            shape((4, 128, 256), BF),
            shape((256, 128), BF),
            shape((16, 128), BF),
            shape((1, 256), jnp.int32),
        ),
        smem=2,
        inputs=6,
        flops=8 * 256 * 1024 * 2,
        size=1 << 20,
        vmem_mib=60,
    )(
        lengths,
        group_ids,
        states,
        direction,
        reward_head.reshape(8, 128),
        routes.reshape(1, 256),
        policy_k,
        reference_k,
    )
    w_here = lax.ppermute(w_t, ALL, TO_HANDLER)
    dirs = lax.all_to_all(dir_t, "zh", 0, 0, tiled=True)
    dirs = lax.all_gather(dirs, "sec", axis=0, tiled=True).reshape(4, 4, 128, 256)
    own = [quarters[0]] + [
        lax.ppermute(quarters[k], "sec", [(j, (j + k) % 4) for j in range(4)]) for k in (1, 2, 3)
    ]
    own = jnp.stack(own)
    other = lax.ppermute(own, "core", [(0, 1), (1, 0)])
    w_pack = jnp.concatenate([w_here, extra], axis=0)
    weights = lax.all_to_all(
        jnp.broadcast_to(w_pack[None], (16, 272, 128)), DP, 0, 0, tiled=True
    )
    pays = call(
        terms_kernel,
        shape((32, 24, 128), F32),
        scratch=[pltpu.VMEM((24, 128), F32)],
        inputs=4,
        flops=1 << 30,
        size=4 << 20,
    )(own, other, weights, dirs)
    pays = lax.all_to_all(pays, ("zh", "core", "sec"), 0, 0, tiled=True)
    parts = call(
        grads_kernel,
        shape((16, 144, 128), BF),
        scratch=[pltpu.VMEM((512, 1024), BF), pltpu.VMEM((8, 128), F32)],
        inputs=6,
        flops=1 << 29,
        size=4 << 20,
    )(pays, own, other, dirs, old_logp.reshape(2, 128), slots)
    parts = lax.all_to_all(parts, DP, 0, 0, tiled=True)
    grad, packed = call(
        finish_kernel,
        (shape((128, 128), F32), shape((1, 320), F32)),
        inputs=1,
        flops=1 << 20,
        size=1 << 20,
    )(parts)
    return lax.ppermute(grad, ALL, TO_OWNER), packed.reshape(1, 1, 320)


def solution(mesh):
    fine = Mesh(mesh.devices.reshape(2, 8, 4, 2, 4), ALL)
    rows, cols = ("zl", "y", "sec"), ("zh", "core")
    return jax.shard_map(
        body,
        mesh=fine,
        in_specs=(
            P(rows, cols),
            P(rows, cols),
            P(rows),
            P(rows),
            P(rows),
            P(rows, None),
            P(cols),
            P(rows, cols),
            P(rows, cols),
        ),
        out_specs=(P(rows, cols), P(DP, "sec", None)),
        check_vma=False,
    )
```

```python
import jax
import jax.numpy as jnp
from jax import lax
from jax.experimental import pallas as pl
from jax.experimental.pallas import tpu as pltpu
from jax.sharding import Mesh
from jax.sharding import PartitionSpec as P

GROUP = 8
NGROUPS = 16
CAP = 20
SLOT = 32

kl_weight = 0.4
var_offset = 0.25

DP = ("zl", "y")
ALL = ("zl", "y", "zh", "core", "sec")
BF = jnp.bfloat16
F32 = jnp.float32
NT = (((1,), (1,)), ((), ()))


def split3(x):
    hi = x.astype(BF).astype(F32)
    rest = x - hi
    mid = rest.astype(BF).astype(F32)
    return hi, mid, rest - mid


def dp_index():
    return lax.axis_index("zl") * 8 + lax.axis_index("y")


def handler(zh, block, zz):
    turn = (zz - zh + (zh >> 1)) & 3
    zl = (turn & 1) ^ (turn >> 1)
    near = 4 * (zh & 1)
    y = near + block + (turn >> 1) * (7 - 2 * block)
    return zl * 8 + (y & 7)


def turn_kernel(direction, wp, wr, dir_t, w_t):
    dir_t[...] = direction[...].astype(F32).T.astype(BF)
    w_t[0:128, :] = wp[...].astype(F32).T.astype(BF)
    w_t[128:256, :] = wr[...].astype(F32).T.astype(BF)


def prepare_kernel(lengths, group_ids, states, head, routes, quarters, extra, slots):
    sec = lax.axis_index("sec")
    for k in range(4):
        to = lax.rem(k - sec + 4, 4)
        quarters[to, :, 0:128] = states[:, 128 * k : 128 * (k + 1)]
        quarters[to, :, 128:256] = states[:, 512 + 128 * k : 512 + 128 * (k + 1)]
    head_rows = head[...].astype(F32)
    wide_head = jnp.concatenate([head_rows[k : k + 1] for k in range(8)], axis=1).astype(BF)
    score = lax.dot_general(
        jnp.broadcast_to(wide_head, (8, 1024)), states[...], NT, preferred_element_type=F32
    )
    lane = lax.broadcasted_iota(jnp.int32, (1, 128), 1)
    rows = []
    for q in range(2):
        valid = (lane < lengths[q]).astype(F32)
        part = jnp.sum(score[0:1, 128 * q : 128 * (q + 1)] * valid, axis=1, keepdims=True)
        rows.extend(split3(part))
    for values in (group_ids, lengths):
        for q in range(2):
            rows.append(jnp.full((1, 1), values[q], jnp.int32).astype(F32))
    at = lax.broadcasted_iota(jnp.int32, (16, 128), 0)
    block = jnp.zeros((16, 128), F32)
    for n, row in enumerate(rows):
        block = jnp.where(at == n, row, block)
    extra[...] = block.astype(BF)
    target = routes[...]
    choose = (lax.broadcasted_iota(jnp.int32, (16, 256), 0) == target).astype(F32)
    before = (
        lax.broadcasted_iota(jnp.int32, (256, 256), 0)
        < lax.broadcasted_iota(jnp.int32, (256, 256), 1)
    ).astype(F32)
    ranked = jnp.dot(choose.astype(BF), before.astype(BF), preferred_element_type=F32)
    rank = jnp.sum(choose * ranked, axis=0, keepdims=True)
    slots[...] = target * SLOT + rank.astype(jnp.int32)


def pack_kernel(quarters, d0, d1, d2, d3, *outs):
    for k in range(4):
        outs[k][0:256, :] = quarters[k]
        for q, block in enumerate((d0, d1, d2, d3)):
            outs[k][256 + 128 * q : 384 + 128 * q, :] = block[...]


def terms_kernel(s0, s1, s2, s3, other, weights, out, pay):
    shares = (s0, s1, s2, s3)
    zh, core, sec = (lax.axis_index(name) for name in ("zh", "core", "sec"))
    acc = [jnp.zeros((2, 256), F32) for _ in range(4)]
    for q in range(4):
        zz = (zh - q) & 3
        mats = [
            jnp.concatenate(
                [weights[handler(zh, 2 * u + h, zz), 0:256, :] for h in range(2)], axis=1
            )
            for u in (core, 1 - core)
        ]
        for s, share in enumerate(shares):
            key = lax.dot_general(mats[0], share[0:256, :], NT, preferred_element_type=F32)
            key += lax.dot_general(
                mats[1], other[256 * s : 256 * (s + 1), :], NT, preferred_element_type=F32
            )
            wide = share[256 + 128 * q : 384 + 128 * q, :].astype(F32)
            acc[s] += jnp.concatenate(
                [
                    jnp.sum(wide * key[0:128], axis=0, keepdims=True),
                    jnp.sum(wide * key[128:256], axis=0, keepdims=True),
                ],
                axis=0,
            )
    for s in range(4):
        for p in range(2):
            for q in range(2):
                n = 8 * p + 2 * lax.rem(sec - s + 4, 4) + q
                pay[pl.ds(n, 1), :] = acc[s][p : p + 1, 128 * q : 128 * (q + 1)]
    lane = lax.broadcasted_iota(jnp.int32, (16, 128), 1)
    block = jnp.zeros((16, 128), F32)
    for i in range(16):
        block = jnp.where(lane == i, weights[i, 256:272, :].astype(F32), block)
    pay[16:17, :] = block[0:1] + block[1:2] + block[2:3]
    pay[17:18, :] = block[3:4] + block[4:5] + block[5:6]
    pay[18:22, :] = block[6:10]
    pay[22:24, :] = jnp.zeros((2, 128), F32)
    whole = pay[...]
    for d in range(32):
        out[d] = whole


def grads_kernel(pays, s0, s1, s2, s3, other, old_logp, slots, out, change, coefs):
    shares = (s0, s1, s2, s3)
    zh, core, sec = (lax.axis_index(name) for name in ("zh", "core", "sec"))
    dp = dp_index()
    terms = pays[0, 0:16, :]
    for d in range(1, 32):
        terms = terms + pays[d, 0:16, :]
    tp, tr = terms[0:8], terms[8:16]
    facts = []
    for s in range(4):
        fact = pays[s, 16:24, :]
        for d in range(1, 8):
            fact = fact + pays[4 * d + s, 16:24, :]
        facts.append(fact)
    lane = lax.broadcasted_iota(jnp.int32, (8, 128), 1)
    used = lane < 16
    sums = jnp.concatenate([f[0:2] for f in facts], axis=0)
    ids = jnp.concatenate([f[2:4] for f in facts], axis=0) * 0.125
    lens = jnp.where(used, jnp.concatenate([f[4:6] for f in facts], axis=0) * 0.125, 1.0)
    reward = sums / jnp.sqrt(lens)
    center = jnp.zeros((8, 128), F32)
    spread = jnp.zeros((8, 128), F32)
    for g in range(NGROUPS):
        member = used & (ids == float(g))
        mine = jnp.where(member, reward, 0.0)
        total = jnp.sum(jnp.sum(mine, axis=0, keepdims=True), axis=1, keepdims=True)
        square = jnp.sum(jnp.sum(mine * mine, axis=0, keepdims=True), axis=1, keepdims=True)
        mid = total / GROUP
        center = jnp.where(member, mid, center)
        spread = jnp.where(member, square / GROUP - mid * mid, spread)
    advantage = ((reward - center) / jnp.sqrt(spread + var_offset)).astype(BF).astype(F32)
    here = lane == dp
    adv = jnp.sum(jnp.where(here, advantage, 0.0), axis=1, keepdims=True)
    length = jnp.sum(jnp.where(here, lens, 0.0), axis=1, keepdims=True)
    valid = (lane.astype(F32) < length).astype(F32)
    coef = valid * (-adv * jnp.exp(tp) + kl_weight * (1.0 - jnp.exp(tr - tp)))
    coefs[...] = coef
    for s in range(4):
        at = lax.rem(sec - s + 4, 4)
        row = jnp.concatenate(
            [coefs[pl.ds(2 * at, 1), :], coefs[pl.ds(2 * at + 1, 1), :]], axis=1
        )
        for q in range(4):
            change[128 * q : 128 * (q + 1), 256 * s : 256 * (s + 1)] = (
                shares[s][256 + 128 * q : 384 + 128 * q, :].astype(F32) * row
            ).astype(BF)
    grads = [
        jnp.dot(change[:, 0:256], s0[0:256, :], preferred_element_type=F32),
        jnp.dot(change[...], other[...], preferred_element_type=F32),
    ]
    for s in range(1, 4):
        grads[0] += jnp.dot(
            change[:, 256 * s : 256 * (s + 1)], shares[s][0:256, :], preferred_element_type=F32
        )
    for u, grad in ((core, grads[0]), (1 - core, grads[1])):
        grad = grad.astype(BF)
        for h in range(2):
            for q in range(4):
                out[handler(zh, 2 * u + h, (zh - q) & 3), 0:128, :] = grad[
                    128 * q : 128 * (q + 1), 128 * h : 128 * (h + 1)
                ]
    at = lax.broadcasted_iota(jnp.int32, (8, 128), 0)
    old = old_logp[...].astype(F32)
    logp = jnp.concatenate(
        [
            old[q : q + 1] + jnp.sum(jnp.where(at == 2 * sec + q, tp, 0.0), axis=0, keepdims=True)
            for q in range(2)
        ],
        axis=1,
    )
    hi, mid, lo = split3(logp)
    rows = jnp.concatenate([hi, mid, lo, jnp.zeros((5, 256), F32)], axis=0).astype(BF)
    place = (lax.broadcasted_iota(jnp.int32, (16 * SLOT, 256), 0) == slots[...]).astype(F32)
    placed = lax.dot_general(rows, place.astype(BF), NT, preferred_element_type=F32)
    tail = jnp.concatenate(
        [placed[h : h + 1, 128 * a : 128 * (a + 1)] for h in range(3) for a in range(4)]
        + [jnp.zeros((4, 128), F32)],
        axis=0,
    ).astype(BF)
    for k in range(16):
        out[k, 128:144, :] = tail


def finish_kernel(parts, grad, packed):
    dp = dp_index()
    total = parts[0, 0:128, :].astype(F32)
    for i in range(1, 16):
        total = total + parts[i, 0:128, :].astype(F32)
    grad[...] = total.T
    at = lax.broadcasted_iota(jnp.int32, (16, 128), 0)
    mine = (at < 12) & (lax.rem(at, 4) == dp // 4)
    rows = []
    for i in range(16):
        tail = jnp.where(mine, parts[i, 128:144, :].astype(F32), 0.0)
        rows.append(jnp.sum(tail, axis=0, keepdims=True))
    table = jnp.concatenate(rows, axis=0)
    pick = jnp.zeros((16, SLOT), F32)
    for a in range(4):
        pick = jnp.where(lax.rem(dp, 4) == a, table[:, SLOT * a : SLOT * (a + 1)], pick)
    packed[...] = jnp.concatenate([pick[i : i + 1, 0:CAP] for i in range(16)], axis=1)


def cost(flops, size):
    return pl.CostEstimate(flops=flops, bytes_accessed=size, transcendentals=0)


def shape(dims, dtype):
    return jax.ShapeDtypeStruct(dims, dtype)


def call(kernel, outs, scratch=(), smem=0, inputs=0, flops=0, size=0, vmem_mib=16):
    vmem = pl.BlockSpec(memory_space=pltpu.VMEM)
    scalar = pl.BlockSpec(memory_space=pltpu.SMEM)
    return pl.pallas_call(
        kernel,
        out_shape=outs,
        in_specs=[scalar] * smem + [vmem] * inputs,
        out_specs=jax.tree.map(lambda _: vmem, outs),
        scratch_shapes=list(scratch),
        cost_estimate=cost(flops, size),
        compiler_params=pltpu.CompilerParams(vmem_limit_bytes=vmem_mib << 20),
    )


def flat(i, zh, core, sec):
    return ((i * 4 + zh) * 2 + core) * 4 + sec


TO_HANDLER = [
    (flat(i, zz, core, sec), flat(handler(i >> 2, i & 3, zz), i >> 2, core, sec))
    for i in range(16)
    for zz in range(4)
    for core in range(2)
    for sec in range(4)
]
TO_OWNER = [(b, a) for a, b in TO_HANDLER]


def ring(step):
    return [(j, (j + step) % 4) for j in range(4)]


def body(
    states, direction, old_logp, lengths, group_ids, routes, reward_head, policy_k, reference_k
):
    dir_t, w_t = call(
        turn_kernel,
        (shape((128, 256), BF), shape((256, 128), BF)),
        inputs=3,
        flops=1 << 16,
        size=1 << 18,
        vmem_mib=60,
    )(direction, policy_k, reference_k)
    w_here = lax.ppermute(w_t, ALL, TO_HANDLER)
    quarters, extra, slots = call(
        prepare_kernel,
        (shape((4, 256, 256), BF), shape((16, 128), BF), shape((1, 256), jnp.int32)),
        smem=2,
        inputs=3,
        flops=8 * 256 * 1024 * 2,
        size=1 << 20,
        vmem_mib=60,
    )(lengths, group_ids, states, reward_head.reshape(8, 128), routes.reshape(1, 256))
    weights = lax.all_to_all(
        jnp.broadcast_to(jnp.concatenate([w_here, extra], axis=0)[None], (16, 272, 128)),
        DP,
        0,
        0,
        tiled=True,
    )
    blocks = [dir_t] + [lax.ppermute(dir_t, "zh", ring(k)) for k in (1, 2, 3)]
    packs = call(
        pack_kernel, (shape((768, 256), BF),) * 4, inputs=5, flops=1 << 10, size=3 << 20
    )(quarters, *blocks)
    shares = [packs[0]] + [lax.ppermute(packs[k], "sec", ring(k)) for k in (1, 2, 3)]
    other = lax.ppermute(
        jnp.concatenate([share[0:256] for share in shares], axis=0), "core", [(0, 1), (1, 0)]
    )
    pays = call(
        terms_kernel,
        shape((32, 24, 128), F32),
        scratch=[pltpu.VMEM((24, 128), F32)],
        inputs=6,
        flops=1 << 30,
        size=4 << 20,
    )(*shares, other, weights)
    pays = lax.all_to_all(pays, ("zh", "core", "sec"), 0, 0, tiled=True)
    parts = call(
        grads_kernel,
        shape((16, 144, 128), BF),
        scratch=[pltpu.VMEM((512, 1024), BF), pltpu.VMEM((8, 128), F32)],
        inputs=8,
        flops=1 << 29,
        size=4 << 20,
    )(pays, *shares, other, old_logp.reshape(2, 128), slots)
    parts = lax.all_to_all(parts, DP, 0, 0, tiled=True)
    grad, packed = call(
        finish_kernel,
        (shape((128, 128), F32), shape((1, 320), F32)),
        inputs=1,
        flops=1 << 20,
        size=1 << 20,
    )(parts)
    return lax.ppermute(grad, ALL, TO_OWNER), packed.reshape(1, 1, 320)


def solution(mesh):
    fine = Mesh(mesh.devices.reshape(2, 8, 4, 2, 4), ALL)
    rows, cols = ("zl", "y", "sec"), ("zh", "core")
    return jax.shard_map(
        body,
        mesh=fine,
        in_specs=(
            P(rows, cols),
            P(rows, cols),
            P(rows),
            P(rows),
            P(rows),
            P(rows, None),
            P(cols),
            P(rows, cols),
            P(rows, cols),
        ),
        out_specs=(P(rows, cols), P(DP, "sec", None)),
        check_vma=False,
    )
```

```python
import jax
import jax.numpy as jnp
from jax import lax
from jax.experimental import pallas as pl
from jax.experimental.pallas import tpu as pltpu
from jax.sharding import Mesh
from jax.sharding import PartitionSpec as P

GROUP = 8
NGROUPS = 16
CAP = 20
SLOT = 32

kl_weight = 0.4
var_offset = 0.25

DP = ("zl", "y")
ALL = ("zl", "y", "zh", "core", "sec")
BF = jnp.bfloat16
F32 = jnp.float32
NT = (((1,), (1,)), ((), ()))


def split3(x):
    hi = x.astype(BF).astype(F32)
    rest = x - hi
    mid = rest.astype(BF).astype(F32)
    return hi, mid, rest - mid


def dp_index():
    return lax.axis_index("zl") * 8 + lax.axis_index("y")


def handler(zh, block, zz):
    turn = (zz - zh + (zh >> 1)) & 3
    zl = (turn & 1) ^ (turn >> 1)
    near = 4 * (zh & 1)
    y = near + block + (turn >> 1) * (7 - 2 * block)
    return zl * 8 + (y & 7)


def turn_kernel(direction, wp, wr, dir_t, w_t):
    dir_t[...] = direction[...].astype(F32).T.astype(BF)
    w_t[0:128, :] = wp[...].astype(F32).T.astype(BF)
    w_t[128:256, :] = wr[...].astype(F32).T.astype(BF)


def prepare_kernel(lengths, group_ids, states, head, routes, quarters, extra, slots):
    sec = lax.axis_index("sec")
    for k in range(4):
        to = lax.rem(k - sec + 4, 4)
        quarters[to, :, 0:128] = states[:, 128 * k : 128 * (k + 1)]
        quarters[to, :, 128:256] = states[:, 512 + 128 * k : 512 + 128 * (k + 1)]
    head_rows = head[...].astype(F32)
    wide_head = jnp.concatenate([head_rows[k : k + 1] for k in range(8)], axis=1).astype(BF)
    score = lax.dot_general(
        jnp.broadcast_to(wide_head, (8, 1024)), states[...], NT, preferred_element_type=F32
    )
    lane = lax.broadcasted_iota(jnp.int32, (1, 128), 1)
    rows = []
    for q in range(2):
        valid = (lane < lengths[q]).astype(F32)
        part = jnp.sum(score[0:1, 128 * q : 128 * (q + 1)] * valid, axis=1, keepdims=True)
        rows.extend(split3(part))
    for values in (group_ids, lengths):
        for q in range(2):
            rows.append(jnp.full((1, 1), values[q], jnp.int32).astype(F32))
    at = lax.broadcasted_iota(jnp.int32, (16, 128), 0)
    block = jnp.zeros((16, 128), F32)
    for n, row in enumerate(rows):
        block = jnp.where(at == n, row, block)
    extra[...] = block.astype(BF)
    target = routes[...]
    choose = (lax.broadcasted_iota(jnp.int32, (16, 256), 0) == target).astype(F32)
    before = (
        lax.broadcasted_iota(jnp.int32, (256, 256), 0)
        < lax.broadcasted_iota(jnp.int32, (256, 256), 1)
    ).astype(F32)
    ranked = jnp.dot(choose.astype(BF), before.astype(BF), preferred_element_type=F32)
    rank = jnp.sum(choose * ranked, axis=0, keepdims=True)
    slots[...] = target * SLOT + rank.astype(jnp.int32)


def pack_kernel(quarters, d0, d1, d2, d3, *outs):
    for k in range(4):
        outs[k][0:256, :] = quarters[k]
        for q, block in enumerate((d0, d1, d2, d3)):
            outs[k][256 + 128 * q : 384 + 128 * q, :] = block[...]


def spread_kernel(w, extra, out):
    for k in range(16):
        out[k, 0:256, :] = w[...]
        out[k, 256:272, :] = extra[...]


def terms_kernel(s0, s1, s2, s3, other, weights, out, pay):
    shares = (s0, s1, s2, s3)
    zh, core, sec = (lax.axis_index(name) for name in ("zh", "core", "sec"))
    acc = [jnp.zeros((2, 256), F32) for _ in range(4)]
    for q in range(4):
        zz = (zh - q) & 3
        mats = [
            jnp.concatenate(
                [weights[handler(zh, 2 * u + h, zz), 0:256, :] for h in range(2)], axis=1
            )
            for u in (core, 1 - core)
        ]
        for s, share in enumerate(shares):
            key = lax.dot_general(mats[0], share[0:256, :], NT, preferred_element_type=F32)
            key += lax.dot_general(
                mats[1], other[256 * s : 256 * (s + 1), :], NT, preferred_element_type=F32
            )
            wide = share[256 + 128 * q : 384 + 128 * q, :].astype(F32)
            acc[s] += jnp.concatenate(
                [
                    jnp.sum(wide * key[0:128], axis=0, keepdims=True),
                    jnp.sum(wide * key[128:256], axis=0, keepdims=True),
                ],
                axis=0,
            )
    for s in range(4):
        for p in range(2):
            pay[0:1, 1024 * p + 256 * s : 1024 * p + 256 * (s + 1)] = acc[s][p : p + 1]
    lane = lax.broadcasted_iota(jnp.int32, (16, 128), 1)
    block = jnp.zeros((16, 128), F32)
    for i in range(16):
        block = jnp.where((lane & 15) == i, weights[i, 256:272, :].astype(F32), block)
    fields = [block[0:1] + block[1:2] + block[2:3], block[3:4] + block[4:5] + block[5:6]]
    fields.extend(block[n : n + 1] for n in range(6, 10))
    facts = jnp.zeros((1, 128), F32)
    for n, field in enumerate(fields):
        facts = jnp.where((lane[0:1] >> 4) == n, field, facts)
    pay[0:1, 2048:2176] = facts
    whole = pay[...]
    for d in range(32):
        out[d] = whole


def grads_kernel(pays, s0, s1, s2, s3, other, old_logp, slots, out, sums, change, coefs):
    shares = (s0, s1, s2, s3)
    zh, core, sec = (lax.axis_index(name) for name in ("zh", "core", "sec"))
    dp = dp_index()
    for s in range(4):
        for p in range(2):
            total = jnp.zeros((1, 256), F32)
            for d in range(32):
                k = (d - s) & 3
                total += pays[d, 0:1, 1024 * p + 256 * k : 1024 * p + 256 * (k + 1)]
            for q in range(2):
                n = 8 * p + 4 * q + s
                sums[n : n + 1, :] = total[:, 128 * q : 128 * (q + 1)]
    tp, tr = sums[0:8, :], sums[8:16, :]
    facts = []
    for s in range(4):
        fact = pays[s, 0:1, 2048:2176]
        for d in range(1, 8):
            fact = fact + pays[4 * d + s, 0:1, 2048:2176]
        facts.append(fact)
    facts = jnp.concatenate(facts + facts, axis=0)
    lane = lax.broadcasted_iota(jnp.int32, (8, 128), 1)
    at = lax.broadcasted_iota(jnp.int32, (8, 128), 0)
    facts = jnp.where(at < 4, facts, pltpu.roll(facts, 112, 1))
    used = lane < 16
    ids = pltpu.roll(facts, 96, 1) * 0.125
    lens = jnp.where(used, pltpu.roll(facts, 64, 1) * 0.125, 1.0)
    reward = facts / jnp.sqrt(lens)
    center = jnp.zeros((8, 128), F32)
    spread = jnp.zeros((8, 128), F32)
    for g in range(NGROUPS):
        member = used & (ids == float(g))
        mine = jnp.where(member, reward, 0.0)
        total = jnp.sum(jnp.sum(mine, axis=0, keepdims=True), axis=1, keepdims=True)
        square = jnp.sum(jnp.sum(mine * mine, axis=0, keepdims=True), axis=1, keepdims=True)
        mid = total / GROUP
        center = jnp.where(member, mid, center)
        spread = jnp.where(member, square / GROUP - mid * mid, spread)
    advantage = ((reward - center) / jnp.sqrt(spread + var_offset)).astype(BF).astype(F32)
    here = lane == dp
    adv = jnp.sum(jnp.where(here, advantage, 0.0), axis=1, keepdims=True)
    length = jnp.sum(jnp.where(here, lens, 0.0), axis=1, keepdims=True)
    valid = (lane.astype(F32) < length).astype(F32)
    coef = valid * (-adv * jnp.exp(tp) + kl_weight * (1.0 - jnp.exp(tr - tp)))
    coefs[...] = coef
    for s in range(4):
        from_sec = (sec - s) & 3
        row = jnp.concatenate(
            [coefs[pl.ds(from_sec, 1), :], coefs[pl.ds(4 + from_sec, 1), :]], axis=1
        )
        for q in range(4):
            change[128 * q : 128 * (q + 1), 256 * s : 256 * (s + 1)] = (
                shares[s][256 + 128 * q : 384 + 128 * q, :].astype(F32) * row
            ).astype(BF)
    grads = [
        jnp.dot(change[:, 0:256], s0[0:256, :], preferred_element_type=F32),
        jnp.dot(change[...], other[...], preferred_element_type=F32),
    ]
    for s in range(1, 4):
        grads[0] += jnp.dot(
            change[:, 256 * s : 256 * (s + 1)], shares[s][0:256, :], preferred_element_type=F32
        )
    for u, grad in ((core, grads[0]), (1 - core, grads[1])):
        grad = grad.astype(BF)
        for h in range(2):
            for q in range(4):
                out[handler(zh, 2 * u + h, (zh - q) & 3), 0:128, :] = grad[
                    128 * q : 128 * (q + 1), 128 * h : 128 * (h + 1)
                ]
    old = old_logp[...].astype(F32)
    logp = jnp.concatenate(
        [
            old[q : q + 1] + jnp.sum(jnp.where(at == 4 * q + sec, tp, 0.0), axis=0, keepdims=True)
            for q in range(2)
        ],
        axis=1,
    )
    hi, mid, lo = split3(logp)
    rows = jnp.concatenate([hi, mid, lo, jnp.zeros((5, 256), F32)], axis=0).astype(BF)
    place = (lax.broadcasted_iota(jnp.int32, (16 * SLOT, 256), 0) == slots[...]).astype(F32)
    placed = lax.dot_general(rows, place.astype(BF), NT, preferred_element_type=F32)
    for a in range(4):
        tail = placed[:, 128 * a : 128 * (a + 1)].astype(BF)
        for k in range(4):
            out[4 * a + k, 128:136, :] = tail


def finish_kernel(parts, grad, packed):
    dp = dp_index()
    total = parts[0, 0:128, :].astype(F32)
    for i in range(1, 16):
        total = total + parts[i, 0:128, :].astype(F32)
    grad[...] = total.T
    rows = [
        jnp.sum(parts[i, 128:136, :].astype(F32), axis=0, keepdims=True) for i in range(16)
    ]
    table = jnp.concatenate(rows, axis=0)
    pick = jnp.zeros((16, SLOT), F32)
    for a in range(4):
        pick = jnp.where(lax.rem(dp, 4) == a, table[:, SLOT * a : SLOT * (a + 1)], pick)
    packed[...] = jnp.concatenate([pick[i : i + 1, 0:CAP] for i in range(16)], axis=1)


def cost(flops, size):
    return pl.CostEstimate(flops=flops, bytes_accessed=size, transcendentals=0)


def shape(dims, dtype):
    return jax.ShapeDtypeStruct(dims, dtype)


def call(kernel, outs, scratch=(), smem=0, inputs=0, flops=0, size=0, vmem_mib=16):
    vmem = pl.BlockSpec(memory_space=pltpu.VMEM)
    scalar = pl.BlockSpec(memory_space=pltpu.SMEM)
    return pl.pallas_call(
        kernel,
        out_shape=outs,
        in_specs=[scalar] * smem + [vmem] * inputs,
        out_specs=jax.tree.map(lambda _: vmem, outs),
        scratch_shapes=list(scratch),
        cost_estimate=cost(flops, size),
        compiler_params=pltpu.CompilerParams(vmem_limit_bytes=vmem_mib << 20),
    )


def flat(i, zh, core, sec):
    return ((i * 4 + zh) * 2 + core) * 4 + sec


TO_HANDLER = [
    (flat(i, zz, core, sec), flat(handler(i >> 2, i & 3, zz), i >> 2, core, sec))
    for i in range(16)
    for zz in range(4)
    for core in range(2)
    for sec in range(4)
]
TO_OWNER = [(b, a) for a, b in TO_HANDLER]


def ring(step):
    return [(j, (j + step) % 4) for j in range(4)]


def body(
    states, direction, old_logp, lengths, group_ids, routes, reward_head, policy_k, reference_k
):
    dir_t, w_t = call(
        turn_kernel,
        (shape((128, 256), BF), shape((256, 128), BF)),
        inputs=3,
        flops=1 << 16,
        size=1 << 18,
        vmem_mib=60,
    )(direction, policy_k, reference_k)
    w_here = lax.ppermute(w_t, ALL, TO_HANDLER)
    quarters, extra, slots = call(
        prepare_kernel,
        (shape((4, 256, 256), BF), shape((16, 128), BF), shape((1, 256), jnp.int32)),
        smem=2,
        inputs=3,
        flops=8 * 256 * 1024 * 2,
        size=1 << 20,
        vmem_mib=60,
    )(lengths, group_ids, states, reward_head.reshape(8, 128), routes.reshape(1, 256))
    blocks = [dir_t] + [lax.ppermute(dir_t, "zh", ring(k)) for k in (1, 2, 3)]
    w_here, *blocks = lax.optimization_barrier((w_here, *blocks))
    weights = call(
        spread_kernel, shape((16, 272, 128), BF), inputs=2, flops=1 << 10, size=1 << 20
    )(w_here, extra)
    weights = lax.all_to_all(weights, DP, 0, 0, tiled=True)
    packs = call(
        pack_kernel, (shape((768, 256), BF),) * 4, inputs=5, flops=1 << 10, size=3 << 20
    )(quarters, *blocks)
    shares = [packs[0]] + [lax.ppermute(packs[k], "sec", ring(k)) for k in (1, 2, 3)]
    other = lax.ppermute(
        jnp.concatenate([share[0:256] for share in shares], axis=0), "core", [(0, 1), (1, 0)]
    )
    pays = call(
        terms_kernel,
        shape((32, 1, 2176), F32),
        scratch=[pltpu.VMEM((1, 2176), F32)],
        inputs=6,
        flops=1 << 30,
        size=4 << 20,
    )(*shares, other, weights)
    pays = lax.all_to_all(pays, ("zh", "core", "sec"), 0, 0, tiled=True)
    parts = call(
        grads_kernel,
        shape((16, 136, 128), BF),
        scratch=[
            pltpu.VMEM((16, 128), F32),
            pltpu.VMEM((512, 1024), BF),
            pltpu.VMEM((8, 128), F32),
        ],
        inputs=8,
        flops=1 << 29,
        size=4 << 20,
    )(pays, *shares, other, old_logp.reshape(2, 128), slots)
    parts = lax.all_to_all(parts, DP, 0, 0, tiled=True)
    grad, packed = call(
        finish_kernel,
        (shape((128, 128), F32), shape((1, 320), F32)),
        inputs=1,
        flops=1 << 20,
        size=1 << 20,
    )(parts)
    return lax.ppermute(grad, ALL, TO_OWNER), packed.reshape(1, 1, 320)


def solution(mesh):
    fine = Mesh(mesh.devices.reshape(2, 8, 4, 2, 4), ALL)
    rows, cols = ("zl", "y", "sec"), ("zh", "core")
    return jax.shard_map(
        body,
        mesh=fine,
        in_specs=(
            P(rows, cols),
            P(rows, cols),
            P(rows),
            P(rows),
            P(rows),
            P(rows, None),
            P(cols),
            P(rows, cols),
            P(rows, cols),
        ),
        out_specs=(P(rows, cols), P(DP, "sec", None)),
        check_vma=False,
    )
```

```python
import jax
import jax.numpy as jnp
from jax import lax
from jax.experimental import pallas as pl
from jax.experimental.pallas import tpu as pltpu
from jax.sharding import Mesh
from jax.sharding import PartitionSpec as P

GROUP = 8
NGROUPS = 16
CAP = 20
SLOT = 32

kl_weight = 0.4
var_offset = 0.25

DP = ("zl", "y")
ALL = ("zl", "y", "zh", "core", "sec")
BF = jnp.bfloat16
F32 = jnp.float32
NT = (((1,), (1,)), ((), ()))


def split3(x):
    hi = x.astype(BF).astype(F32)
    rest = x - hi
    mid = rest.astype(BF).astype(F32)
    return hi, mid, rest - mid


def dp_index():
    return lax.axis_index("zl") * 8 + lax.axis_index("y")


def handler(zh, block, zz):
    turn = (zz - zh + (zh >> 1)) & 3
    zl = (turn & 1) ^ (turn >> 1)
    near = 4 * (zh & 1)
    y = near + block + (turn >> 1) * (7 - 2 * block)
    return zl * 8 + (y & 7)


def turn_kernel(direction, wp, wr, dir_t, w_t):
    turned = direction[...].astype(F32).T.astype(BF)
    for k in range(4):
        dir_t[k] = turned
    w_t[0:128, :] = wp[...].astype(F32).T.astype(BF)
    w_t[128:256, :] = wr[...].astype(F32).T.astype(BF)


def prepare_kernel(lengths, group_ids, states, head, routes, quarters, extra, slots):
    sec = lax.axis_index("sec")
    for k in range(4):
        to = lax.rem(k - sec + 4, 4)
        quarters[to, :, 0:128] = states[:, 128 * k : 128 * (k + 1)]
        quarters[to, :, 128:256] = states[:, 512 + 128 * k : 512 + 128 * (k + 1)]
    head_rows = head[...].astype(F32)
    wide_head = jnp.concatenate([head_rows[k : k + 1] for k in range(8)], axis=1).astype(BF)
    score = lax.dot_general(
        jnp.broadcast_to(wide_head, (8, 1024)), states[...], NT, preferred_element_type=F32
    )
    lane = lax.broadcasted_iota(jnp.int32, (1, 128), 1)
    rows = []
    for q in range(2):
        valid = (lane < lengths[q]).astype(F32)
        part = jnp.sum(score[0:1, 128 * q : 128 * (q + 1)] * valid, axis=1, keepdims=True)
        rows.extend(split3(part))
    for values in (group_ids, lengths):
        for q in range(2):
            rows.append(jnp.full((1, 1), values[q], jnp.int32).astype(F32))
    at = lax.broadcasted_iota(jnp.int32, (16, 128), 0)
    block = jnp.zeros((16, 128), F32)
    for n, row in enumerate(rows):
        block = jnp.where(at == n, row, block)
    extra[...] = block.astype(BF)
    target = routes[...]
    choose = (lax.broadcasted_iota(jnp.int32, (16, 256), 0) == target).astype(F32)
    before = (
        lax.broadcasted_iota(jnp.int32, (256, 256), 0)
        < lax.broadcasted_iota(jnp.int32, (256, 256), 1)
    ).astype(F32)
    ranked = jnp.dot(choose.astype(BF), before.astype(BF), preferred_element_type=F32)
    rank = jnp.sum(choose * ranked, axis=0, keepdims=True)
    slots[...] = target * SLOT + rank.astype(jnp.int32)


def pack_kernel(quarters, dirs, *outs):
    for k in range(4):
        outs[k][0:256, :] = quarters[k]
        for q in range(4):
            outs[k][256 + 128 * q : 384 + 128 * q, :] = dirs[q]


def spread_kernel(w, extra, out):
    for k in range(16):
        out[k, 0:256, :] = w[...]
        out[k, 256:272, :] = extra[...]


def terms_kernel(s0, s1, s2, s3, other, weights, pay):
    shares = (s0, s1, s2, s3)
    zh, core, sec = (lax.axis_index(name) for name in ("zh", "core", "sec"))
    acc = [jnp.zeros((2, 256), F32) for _ in range(4)]
    for q in range(4):
        mats = [
            jnp.concatenate(
                [weights[handler(zh, 2 * u + h, q), 0:256, :] for h in range(2)], axis=1
            )
            for u in (core, 1 - core)
        ]
        for s, share in enumerate(shares):
            key = lax.dot_general(mats[0], share[0:256, :], NT, preferred_element_type=F32)
            key += lax.dot_general(
                mats[1], other[256 * s : 256 * (s + 1), :], NT, preferred_element_type=F32
            )
            wide = share[256 + 128 * q : 384 + 128 * q, :].astype(F32)
            acc[s] += jnp.concatenate(
                [
                    jnp.sum(wide * key[0:128], axis=0, keepdims=True),
                    jnp.sum(wide * key[128:256], axis=0, keepdims=True),
                ],
                axis=0,
            )
    for s in range(4):
        for p in range(2):
            pay[0:1, 1024 * p + 256 * s : 1024 * p + 256 * (s + 1)] = acc[s][p : p + 1]
    lane = lax.broadcasted_iota(jnp.int32, (16, 128), 1)
    block = jnp.zeros((16, 128), F32)
    for i in range(16):
        block = jnp.where((lane & 15) == i, weights[i, 256:272, :].astype(F32), block)
    fields = [block[0:1] + block[1:2] + block[2:3], block[3:4] + block[4:5] + block[5:6]]
    fields.extend(block[n : n + 1] for n in range(6, 10))
    facts = jnp.zeros((1, 128), F32)
    for n, field in enumerate(fields):
        facts = jnp.where((lane[0:1] >> 4) == n, field, facts)
    pay[0:1, 2048:2176] = facts


def join_kernel(mine, partner, out):
    whole = mine[...] + partner[...]
    for d in range(16):
        out[d] = whole


def grads_kernel(pays, s0, s1, s2, s3, other, old_logp, slots, out, sums, change, coefs):
    shares = (s0, s1, s2, s3)
    zh, core, sec = (lax.axis_index(name) for name in ("zh", "core", "sec"))
    dp = dp_index()
    for s in range(4):
        for p in range(2):
            total = jnp.zeros((1, 256), F32)
            for d in range(16):
                k = (d - s) & 3
                total += pays[d, 0:1, 1024 * p + 256 * k : 1024 * p + 256 * (k + 1)]
            for q in range(2):
                n = 8 * p + 4 * q + s
                sums[n : n + 1, :] = total[:, 128 * q : 128 * (q + 1)]
    tp, tr = sums[0:8, :], sums[8:16, :]
    facts = []
    for s in range(4):
        fact = pays[s, 0:1, 2048:2176]
        for d in range(1, 4):
            fact = fact + pays[4 * d + s, 0:1, 2048:2176]
        facts.append(fact)
    facts = jnp.concatenate(facts + facts, axis=0)
    lane = lax.broadcasted_iota(jnp.int32, (8, 128), 1)
    at = lax.broadcasted_iota(jnp.int32, (8, 128), 0)
    facts = jnp.where(at < 4, facts, pltpu.roll(facts, 112, 1))
    used = lane < 16
    ids = pltpu.roll(facts, 96, 1) * 0.125
    lens = jnp.where(used, pltpu.roll(facts, 64, 1) * 0.125, 1.0)
    reward = facts / jnp.sqrt(lens)
    center = jnp.zeros((8, 128), F32)
    spread = jnp.zeros((8, 128), F32)
    for g in range(NGROUPS):
        member = used & (ids == float(g))
        mine = jnp.where(member, reward, 0.0)
        total = jnp.sum(jnp.sum(mine, axis=0, keepdims=True), axis=1, keepdims=True)
        square = jnp.sum(jnp.sum(mine * mine, axis=0, keepdims=True), axis=1, keepdims=True)
        mid = total / GROUP
        center = jnp.where(member, mid, center)
        spread = jnp.where(member, square / GROUP - mid * mid, spread)
    advantage = ((reward - center) / jnp.sqrt(spread + var_offset)).astype(BF).astype(F32)
    here = lane == dp
    adv = jnp.sum(jnp.where(here, advantage, 0.0), axis=1, keepdims=True)
    length = jnp.sum(jnp.where(here, lens, 0.0), axis=1, keepdims=True)
    valid = (lane.astype(F32) < length).astype(F32)
    coef = valid * (-adv * jnp.exp(tp) + kl_weight * (1.0 - jnp.exp(tr - tp)))
    coefs[...] = coef
    for s in range(4):
        from_sec = (sec - s) & 3
        row = jnp.concatenate(
            [coefs[pl.ds(from_sec, 1), :], coefs[pl.ds(4 + from_sec, 1), :]], axis=1
        )
        for q in range(4):
            change[128 * q : 128 * (q + 1), 256 * s : 256 * (s + 1)] = (
                shares[s][256 + 128 * q : 384 + 128 * q, :].astype(F32) * row
            ).astype(BF)
    grads = [
        jnp.dot(change[:, 0:256], s0[0:256, :], preferred_element_type=F32),
        jnp.dot(change[...], other[...], preferred_element_type=F32),
    ]
    for s in range(1, 4):
        grads[0] += jnp.dot(
            change[:, 256 * s : 256 * (s + 1)], shares[s][0:256, :], preferred_element_type=F32
        )
    for u, grad in ((core, grads[0]), (1 - core, grads[1])):
        grad = grad.astype(BF)
        for h in range(2):
            for q in range(4):
                out[handler(zh, 2 * u + h, q), 0:128, :] = grad[
                    128 * q : 128 * (q + 1), 128 * h : 128 * (h + 1)
                ]
    old = old_logp[...].astype(F32)
    logp = jnp.concatenate(
        [
            old[q : q + 1] + jnp.sum(jnp.where(at == 4 * q + sec, tp, 0.0), axis=0, keepdims=True)
            for q in range(2)
        ],
        axis=1,
    )
    hi, mid, lo = split3(logp)
    rows = jnp.concatenate([hi, mid, lo, jnp.zeros((5, 256), F32)], axis=0).astype(BF)
    place = (lax.broadcasted_iota(jnp.int32, (16 * SLOT, 256), 0) == slots[...]).astype(F32)
    placed = lax.dot_general(rows, place.astype(BF), NT, preferred_element_type=F32)
    for a in range(4):
        tail = placed[:, 128 * a : 128 * (a + 1)].astype(BF)
        for k in range(4):
            out[4 * a + k, 128:136, :] = tail


def finish_kernel(parts, grad, packed):
    dp = dp_index()
    total = parts[0, 0:128, :].astype(F32)
    for i in range(1, 16):
        total = total + parts[i, 0:128, :].astype(F32)
    grad[...] = total.T
    rows = [
        jnp.sum(parts[i, 128:136, :].astype(F32), axis=0, keepdims=True) for i in range(16)
    ]
    table = jnp.concatenate(rows, axis=0)
    pick = jnp.zeros((16, SLOT), F32)
    for a in range(4):
        pick = jnp.where(lax.rem(dp, 4) == a, table[:, SLOT * a : SLOT * (a + 1)], pick)
    packed[...] = jnp.concatenate([pick[i : i + 1, 0:CAP] for i in range(16)], axis=1)


def cost(flops, size):
    return pl.CostEstimate(flops=flops, bytes_accessed=size, transcendentals=0)


def shape(dims, dtype):
    return jax.ShapeDtypeStruct(dims, dtype)


def call(kernel, outs, scratch=(), smem=0, inputs=0, flops=0, size=0, vmem_mib=16):
    vmem = pl.BlockSpec(memory_space=pltpu.VMEM)
    scalar = pl.BlockSpec(memory_space=pltpu.SMEM)
    return pl.pallas_call(
        kernel,
        out_shape=outs,
        in_specs=[scalar] * smem + [vmem] * inputs,
        out_specs=jax.tree.map(lambda _: vmem, outs),
        scratch_shapes=list(scratch),
        cost_estimate=cost(flops, size),
        compiler_params=pltpu.CompilerParams(vmem_limit_bytes=vmem_mib << 20),
    )


def flat(i, zh, core, sec):
    return ((i * 4 + zh) * 2 + core) * 4 + sec


TO_HANDLER = [
    (flat(i, zz, core, sec), flat(handler(i >> 2, i & 3, zz), i >> 2, core, sec))
    for i in range(16)
    for zz in range(4)
    for core in range(2)
    for sec in range(4)
]
TO_OWNER = [(b, a) for a, b in TO_HANDLER]


def ring(step):
    return [(j, (j + step) % 4) for j in range(4)]


def body(
    states, direction, old_logp, lengths, group_ids, routes, reward_head, policy_k, reference_k
):
    dir_t, w_t = call(
        turn_kernel,
        (shape((4, 128, 256), BF), shape((256, 128), BF)),
        inputs=3,
        flops=1 << 16,
        size=1 << 18,
        vmem_mib=60,
    )(direction, policy_k, reference_k)
    w_here = lax.ppermute(w_t, ALL, TO_HANDLER)
    quarters, extra, slots = call(
        prepare_kernel,
        (shape((4, 256, 256), BF), shape((16, 128), BF), shape((1, 256), jnp.int32)),
        smem=2,
        inputs=3,
        flops=8 * 256 * 1024 * 2,
        size=1 << 20,
    )(lengths, group_ids, states, reward_head.reshape(8, 128), routes.reshape(1, 256))
    dirs = lax.all_to_all(dir_t, "zh", 0, 0, tiled=True)
    w_here, dirs = lax.optimization_barrier((w_here, dirs))
    weights = call(
        spread_kernel, shape((16, 272, 128), BF), inputs=2, flops=1 << 10, size=1 << 20
    )(w_here, extra)
    weights = lax.all_to_all(weights, DP, 0, 0, tiled=True)
    packs = call(
        pack_kernel, (shape((768, 256), BF),) * 4, inputs=2, flops=1 << 10, size=3 << 20
    )(quarters, dirs)
    shares = [packs[0]] + [lax.ppermute(packs[k], "sec", ring(k)) for k in (1, 2, 3)]
    other = lax.ppermute(
        jnp.concatenate([share[0:256] for share in shares], axis=0), "core", [(0, 1), (1, 0)]
    )
    pay = call(
        terms_kernel, shape((1, 2176), F32), inputs=6, flops=1 << 30, size=4 << 20
    )(*shares, other, weights)
    pays = call(join_kernel, shape((16, 1, 2176), F32), inputs=2, flops=1 << 12, size=1 << 18)(
        pay, lax.ppermute(pay, "core", [(0, 1), (1, 0)])
    )
    pays = lax.all_to_all(pays, ("zh", "sec"), 0, 0, tiled=True)
    parts = call(
        grads_kernel,
        shape((16, 136, 128), BF),
        scratch=[
            pltpu.VMEM((16, 128), F32),
            pltpu.VMEM((512, 1024), BF),
            pltpu.VMEM((8, 128), F32),
        ],
        inputs=8,
        flops=1 << 29,
        size=4 << 20,
    )(pays, *shares, other, old_logp.reshape(2, 128), slots)
    parts = lax.all_to_all(parts, DP, 0, 0, tiled=True)
    grad, packed = call(
        finish_kernel,
        (shape((128, 128), F32), shape((1, 320), F32)),
        inputs=1,
        flops=1 << 20,
        size=1 << 20,
    )(parts)
    return lax.ppermute(grad, ALL, TO_OWNER), packed.reshape(1, 1, 320)


def solution(mesh):
    fine = Mesh(mesh.devices.reshape(2, 8, 4, 2, 4), ALL)
    rows, cols = ("zl", "y", "sec"), ("zh", "core")
    return jax.shard_map(
        body,
        mesh=fine,
        in_specs=(
            P(rows, cols),
            P(rows, cols),
            P(rows),
            P(rows),
            P(rows),
            P(rows, None),
            P(cols),
            P(rows, cols),
            P(rows, cols),
        ),
        out_specs=(P(rows, cols), P(DP, "sec", None)),
        check_vma=False,
    )
```

```python
import jax
import jax.numpy as jnp
from jax import lax
from jax.experimental import pallas as pl
from jax.experimental.pallas import tpu as pltpu
from jax.sharding import Mesh
from jax.sharding import PartitionSpec as P

GROUP = 8
NGROUPS = 16
CAP = 20
SLOT = 32

kl_weight = 0.4
var_offset = 0.25

DP = ("zl", "y")
ALL = ("zl", "y", "zh", "core", "sec")
BF = jnp.bfloat16
F32 = jnp.float32
NT = (((1,), (1,)), ((), ()))


def split3(x):
    hi = x.astype(BF).astype(F32)
    rest = x - hi
    mid = rest.astype(BF).astype(F32)
    return hi, mid, rest - mid


def dp_index():
    return lax.axis_index("zl") * 8 + lax.axis_index("y")


def handler(zh, block, zz):
    turn = (zz - zh + (zh >> 1)) & 3
    zl = (turn & 1) ^ (turn >> 1)
    near = 4 * (zh & 1)
    y = near + block + (turn >> 1) * (7 - 2 * block)
    return zl * 8 + (y & 7)


def turn_kernel(direction, wp, wr, dir_t, w_t):
    turned = direction[...].astype(F32).T.astype(BF)
    for k in range(4):
        dir_t[k] = turned
    w_t[0:128, :] = wp[...].astype(F32).T.astype(BF)
    w_t[128:256, :] = wr[...].astype(F32).T.astype(BF)


def prepare_kernel(lengths, group_ids, states, head, routes, quarters, extra, slots):
    sec = lax.axis_index("sec")
    for k in range(4):
        to = lax.rem(k - sec + 4, 4)
        quarters[to, :, 0:128] = states[:, 128 * k : 128 * (k + 1)]
        quarters[to, :, 128:256] = states[:, 512 + 128 * k : 512 + 128 * (k + 1)]
    head_rows = head[...].astype(F32)
    wide_head = jnp.concatenate([head_rows[k : k + 1] for k in range(8)], axis=1).astype(BF)
    score = lax.dot_general(
        jnp.broadcast_to(wide_head, (8, 1024)), states[...], NT, preferred_element_type=F32
    )
    lane = lax.broadcasted_iota(jnp.int32, (1, 128), 1)
    rows = []
    for q in range(2):
        valid = (lane < lengths[q]).astype(F32)
        part = jnp.sum(score[0:1, 128 * q : 128 * (q + 1)] * valid, axis=1, keepdims=True)
        rows.extend(split3(part))
    for values in (group_ids, lengths):
        for q in range(2):
            rows.append(jnp.full((1, 1), values[q], jnp.int32).astype(F32))
    at = lax.broadcasted_iota(jnp.int32, (16, 128), 0)
    block = jnp.zeros((16, 128), F32)
    for n, row in enumerate(rows):
        block = jnp.where(at == n, row, block)
    extra[...] = block.astype(BF)
    target = routes[...]
    choose = (lax.broadcasted_iota(jnp.int32, (16, 256), 0) == target).astype(F32)
    before = (
        lax.broadcasted_iota(jnp.int32, (256, 256), 0)
        < lax.broadcasted_iota(jnp.int32, (256, 256), 1)
    ).astype(F32)
    ranked = jnp.dot(choose.astype(BF), before.astype(BF), preferred_element_type=F32)
    rank = jnp.sum(choose * ranked, axis=0, keepdims=True)
    slots[...] = target * SLOT + rank.astype(jnp.int32)


def pack_kernel(quarters, dirs, *outs):
    for k in range(4):
        outs[k][0:256, :] = quarters[k]
        for q in range(4):
            outs[k][256 + 128 * q : 384 + 128 * q, :] = dirs[q]


def spread_kernel(w, extra, out):
    for k in range(16):
        out[k, 0:256, :] = w[...]
        out[k, 256:272, :] = extra[...]


def terms_kernel(s0, s1, s2, s3, other, weights, pay):
    shares = (s0, s1, s2, s3)
    zh, core, sec = (lax.axis_index(name) for name in ("zh", "core", "sec"))
    acc = [jnp.zeros((2, 256), F32) for _ in range(4)]
    for q in range(4):
        mats = [
            jnp.concatenate(
                [weights[handler(zh, 2 * u + h, q), 0:256, :] for h in range(2)], axis=1
            )
            for u in (core, 1 - core)
        ]
        for s, share in enumerate(shares):
            key = lax.dot_general(mats[0], share[0:256, :], NT, preferred_element_type=F32)
            key += lax.dot_general(
                mats[1], other[256 * s : 256 * (s + 1), :], NT, preferred_element_type=F32
            )
            wide = share[256 + 128 * q : 384 + 128 * q, :].astype(F32)
            acc[s] += jnp.concatenate(
                [
                    jnp.sum(wide * key[0:128], axis=0, keepdims=True),
                    jnp.sum(wide * key[128:256], axis=0, keepdims=True),
                ],
                axis=0,
            )
    for s in range(4):
        for p in range(2):
            for q in range(2):
                pay[pl.ds(8 * p + 4 * q + ((sec - s) & 3), 1), :] = acc[s][
                    p : p + 1, 128 * q : 128 * (q + 1)
                ]
    lane = lax.broadcasted_iota(jnp.int32, (16, 128), 1)
    block = jnp.zeros((16, 128), F32)
    for i in range(16):
        block = jnp.where((lane & 15) == i, weights[i, 256:272, :].astype(F32), block)
    fields = [block[0:1] + block[1:2] + block[2:3], block[3:4] + block[4:5] + block[5:6]]
    fields.extend(block[n : n + 1] for n in range(6, 10))
    facts = jnp.zeros((1, 128), F32)
    for n, field in enumerate(fields):
        facts = jnp.where((lane[0:1] >> 4) == n, field, facts)
    pay[16:24, :] = jnp.broadcast_to(facts, (8, 128))


def join_kernel(mine, partner, out):
    whole = mine[...] + partner[...]
    for d in range(16):
        out[d] = whole


def grads_kernel(pays, s0, s1, s2, s3, other, old_logp, slots, out, change, coefs):
    shares = (s0, s1, s2, s3)
    zh, core, sec = (lax.axis_index(name) for name in ("zh", "core", "sec"))
    dp = dp_index()
    sums = pays[0, 0:16, :]
    for d in range(1, 16):
        sums = sums + pays[d, 0:16, :]
    tp, tr = sums[0:8], sums[8:16]
    facts = []
    for s in range(4):
        fact = pays[s, 16:17, :]
        for d in range(1, 4):
            fact = fact + pays[4 * d + s, 16:17, :]
        facts.append(fact)
    facts = jnp.concatenate(facts + facts, axis=0)
    lane = lax.broadcasted_iota(jnp.int32, (8, 128), 1)
    at = lax.broadcasted_iota(jnp.int32, (8, 128), 0)
    facts = jnp.where(at < 4, facts, pltpu.roll(facts, 112, 1))
    used = lane < 16
    ids = pltpu.roll(facts, 96, 1) * 0.125
    lens = jnp.where(used, pltpu.roll(facts, 64, 1) * 0.125, 1.0)
    reward = facts / jnp.sqrt(lens)
    center = jnp.zeros((8, 128), F32)
    spread = jnp.zeros((8, 128), F32)
    for g in range(NGROUPS):
        member = used & (ids == float(g))
        mine = jnp.where(member, reward, 0.0)
        total = jnp.sum(jnp.sum(mine, axis=0, keepdims=True), axis=1, keepdims=True)
        square = jnp.sum(jnp.sum(mine * mine, axis=0, keepdims=True), axis=1, keepdims=True)
        mid = total / GROUP
        center = jnp.where(member, mid, center)
        spread = jnp.where(member, square / GROUP - mid * mid, spread)
    advantage = ((reward - center) / jnp.sqrt(spread + var_offset)).astype(BF).astype(F32)
    here = lane == dp
    adv = jnp.sum(jnp.where(here, advantage, 0.0), axis=1, keepdims=True)
    length = jnp.sum(jnp.where(here, lens, 0.0), axis=1, keepdims=True)
    valid = (lane.astype(F32) < length).astype(F32)
    coef = valid * (-adv * jnp.exp(tp) + kl_weight * (1.0 - jnp.exp(tr - tp)))
    coefs[...] = coef
    for s in range(4):
        from_sec = (sec - s) & 3
        row = jnp.concatenate(
            [coefs[pl.ds(from_sec, 1), :], coefs[pl.ds(4 + from_sec, 1), :]], axis=1
        )
        for q in range(4):
            change[128 * q : 128 * (q + 1), 256 * s : 256 * (s + 1)] = (
                shares[s][256 + 128 * q : 384 + 128 * q, :].astype(F32) * row
            ).astype(BF)
    grads = [
        jnp.dot(change[:, 0:256], s0[0:256, :], preferred_element_type=F32),
        jnp.dot(change[...], other[...], preferred_element_type=F32),
    ]
    for s in range(1, 4):
        grads[0] += jnp.dot(
            change[:, 256 * s : 256 * (s + 1)], shares[s][0:256, :], preferred_element_type=F32
        )
    for u, grad in ((core, grads[0]), (1 - core, grads[1])):
        grad = grad.astype(BF)
        for h in range(2):
            for q in range(4):
                out[handler(zh, 2 * u + h, q), 0:128, :] = grad[
                    128 * q : 128 * (q + 1), 128 * h : 128 * (h + 1)
                ]
    old = old_logp[...].astype(F32)
    logp = jnp.concatenate(
        [
            old[q : q + 1] + jnp.sum(jnp.where(at == 4 * q + sec, tp, 0.0), axis=0, keepdims=True)
            for q in range(2)
        ],
        axis=1,
    )
    hi, mid, lo = split3(logp)
    rows = jnp.concatenate([hi, mid, lo, jnp.zeros((5, 256), F32)], axis=0).astype(BF)
    place = (lax.broadcasted_iota(jnp.int32, (16 * SLOT, 256), 0) == slots[...]).astype(F32)
    placed = lax.dot_general(rows, place.astype(BF), NT, preferred_element_type=F32)
    for a in range(4):
        tail = placed[:, 128 * a : 128 * (a + 1)].astype(BF)
        for k in range(4):
            out[4 * a + k, 128:136, :] = tail


def finish_kernel(parts, grad, packed):
    dp = dp_index()
    total = parts[0, 0:128, :].astype(F32)
    for i in range(1, 16):
        total = total + parts[i, 0:128, :].astype(F32)
    grad[...] = total.T
    rows = [
        jnp.sum(parts[i, 128:136, :].astype(F32), axis=0, keepdims=True) for i in range(16)
    ]
    table = jnp.concatenate(rows, axis=0)
    pick = jnp.zeros((16, SLOT), F32)
    for a in range(4):
        pick = jnp.where(lax.rem(dp, 4) == a, table[:, SLOT * a : SLOT * (a + 1)], pick)
    packed[...] = jnp.concatenate([pick[i : i + 1, 0:CAP] for i in range(16)], axis=1)


def cost(flops, size):
    return pl.CostEstimate(flops=flops, bytes_accessed=size, transcendentals=0)


def shape(dims, dtype):
    return jax.ShapeDtypeStruct(dims, dtype)


def call(kernel, outs, scratch=(), smem=0, inputs=0, flops=0, size=0, vmem_mib=16):
    vmem = pl.BlockSpec(memory_space=pltpu.VMEM)
    scalar = pl.BlockSpec(memory_space=pltpu.SMEM)
    return pl.pallas_call(
        kernel,
        out_shape=outs,
        in_specs=[scalar] * smem + [vmem] * inputs,
        out_specs=jax.tree.map(lambda _: vmem, outs),
        scratch_shapes=list(scratch),
        cost_estimate=cost(flops, size),
        compiler_params=pltpu.CompilerParams(vmem_limit_bytes=vmem_mib << 20),
    )


def flat(i, zh, core, sec):
    return ((i * 4 + zh) * 2 + core) * 4 + sec


TO_HANDLER = [
    (flat(i, zz, core, sec), flat(handler(i >> 2, i & 3, zz), i >> 2, core, sec))
    for i in range(16)
    for zz in range(4)
    for core in range(2)
    for sec in range(4)
]
TO_OWNER = [(b, a) for a, b in TO_HANDLER]


def ring(step):
    return [(j, (j + step) % 4) for j in range(4)]


def body(
    states, direction, old_logp, lengths, group_ids, routes, reward_head, policy_k, reference_k
):
    dir_t, w_t = call(
        turn_kernel,
        (shape((4, 128, 256), BF), shape((256, 128), BF)),
        inputs=3,
        flops=1 << 16,
        size=1 << 18,
        vmem_mib=60,
    )(direction, policy_k, reference_k)
    w_here = lax.ppermute(w_t, ALL, TO_HANDLER)
    quarters, extra, slots = call(
        prepare_kernel,
        (shape((4, 256, 256), BF), shape((16, 128), BF), shape((1, 256), jnp.int32)),
        smem=2,
        inputs=3,
        flops=8 * 256 * 1024 * 2,
        size=1 << 20,
        vmem_mib=60,
    )(lengths, group_ids, states, reward_head.reshape(8, 128), routes.reshape(1, 256))
    dirs = lax.all_to_all(dir_t, "zh", 0, 0, tiled=True)
    w_here, dirs = lax.optimization_barrier((w_here, dirs))
    weights = call(
        spread_kernel, shape((16, 272, 128), BF), inputs=2, flops=1 << 10, size=1 << 20
    )(w_here, extra)
    weights = lax.all_to_all(weights, DP, 0, 0, tiled=True)
    packs = call(
        pack_kernel, (shape((768, 256), BF),) * 4, inputs=2, flops=1 << 10, size=3 << 20
    )(quarters, dirs)
    shares = [packs[0]] + [lax.ppermute(packs[k], "sec", ring(k)) for k in (1, 2, 3)]
    other = lax.ppermute(
        jnp.concatenate([share[0:256] for share in shares], axis=0), "core", [(0, 1), (1, 0)]
    )
    pay = call(
        terms_kernel, shape((24, 128), F32), inputs=6, flops=1 << 30, size=4 << 20
    )(*shares, other, weights)
    pays = call(join_kernel, shape((16, 24, 128), F32), inputs=2, flops=1 << 12, size=1 << 18)(
        pay, lax.ppermute(pay, "core", [(0, 1), (1, 0)])
    )
    pays = lax.all_to_all(pays, ("zh", "sec"), 0, 0, tiled=True)
    parts = call(
        grads_kernel,
        shape((16, 136, 128), BF),
        scratch=[
            pltpu.VMEM((512, 1024), BF),
            pltpu.VMEM((8, 128), F32),
        ],
        inputs=8,
        flops=1 << 29,
        size=4 << 20,
    )(pays, *shares, other, old_logp.reshape(2, 128), slots)
    parts = lax.all_to_all(parts, DP, 0, 0, tiled=True)
    grad, packed = call(
        finish_kernel,
        (shape((128, 128), F32), shape((1, 320), F32)),
        inputs=1,
        flops=1 << 20,
        size=1 << 20,
    )(parts)
    return lax.ppermute(grad, ALL, TO_OWNER), packed.reshape(1, 1, 320)


def solution(mesh):
    fine = Mesh(mesh.devices.reshape(2, 8, 4, 2, 4), ALL)
    rows, cols = ("zl", "y", "sec"), ("zh", "core")
    return jax.shard_map(
        body,
        mesh=fine,
        in_specs=(
            P(rows, cols),
            P(rows, cols),
            P(rows),
            P(rows),
            P(rows),
            P(rows, None),
            P(cols),
            P(rows, cols),
            P(rows, cols),
        ),
        out_specs=(P(rows, cols), P(DP, "sec", None)),
        check_vma=False,
    )
```

```python
import jax
import jax.numpy as jnp
from jax import lax
from jax.experimental import pallas as pl
from jax.experimental.pallas import tpu as pltpu
from jax.sharding import Mesh
from jax.sharding import PartitionSpec as P

GROUP = 8
NGROUPS = 16
CAP = 20
SLOT = 32

kl_weight = 0.4
var_offset = 0.25

DP = ("zl", "y")
ALL = ("zl", "y", "zh", "core", "sec")
BF = jnp.bfloat16
F32 = jnp.float32
NT = (((1,), (1,)), ((), ()))


def split3(x):
    hi = x.astype(BF).astype(F32)
    rest = x - hi
    mid = rest.astype(BF).astype(F32)
    return hi, mid, rest - mid


def dp_index():
    return lax.axis_index("zl") * 8 + lax.axis_index("y")


def handler(zh, block, zz):
    turn = (zz - zh + (zh >> 1)) & 3
    zl = (turn & 1) ^ (turn >> 1)
    near = 4 * (zh & 1)
    y = near + block + (turn >> 1) * (7 - 2 * block)
    return zl * 8 + (y & 7)


def turn_kernel(direction, routes, old_logp, wp, wr, dir_t, w_t):
    dir_t[0:128, :] = direction[...].astype(F32).T.astype(BF)
    at = lax.broadcasted_iota(jnp.int32, (8, 256), 0)
    old = old_logp[...].astype(F32)
    old = jnp.concatenate([old[0:1], old[1:2]], axis=1)
    rows = jnp.where(at == 0, routes[...].astype(F32), jnp.where(at == 1, old, 0.0))
    dir_t[128:136, :] = rows.astype(BF)
    w_t[0:128, :] = wp[...].astype(F32).T.astype(BF)
    w_t[128:256, :] = wr[...].astype(F32).T.astype(BF)


def prepare_kernel(lengths, group_ids, states, head, w_t, w_pack, half0, half1):
    sec, odd = lax.axis_index("sec"), lax.axis_index("y") & 1
    for b, half in enumerate((half0, half1)):
        for k in range(4):
            start = 512 * (b ^ odd) + 128 * ((sec - k) & 3)
            half[:, 128 * k : 128 * (k + 1)] = states[:, pl.ds(pl.multiple_of(start, 128), 128)]
    head_rows = head[...].astype(F32)
    wide_head = jnp.concatenate([head_rows[k : k + 1] for k in range(8)], axis=1).astype(BF)
    score = lax.dot_general(
        jnp.broadcast_to(wide_head, (8, 1024)), states[...], NT, preferred_element_type=F32
    )
    lane = lax.broadcasted_iota(jnp.int32, (1, 128), 1)
    rows = []
    for q in range(2):
        valid = (lane < lengths[q]).astype(F32)
        part = jnp.sum(score[0:1, 128 * q : 128 * (q + 1)] * valid, axis=1, keepdims=True)
        rows.extend(split3(part))
    for values in (group_ids, lengths):
        for q in range(2):
            rows.append(jnp.full((1, 1), values[q], jnp.int32).astype(F32))
    at = lax.broadcasted_iota(jnp.int32, (16, 128), 0)
    block = jnp.zeros((16, 128), F32)
    for n, row in enumerate(rows):
        block = jnp.where(at == n, row, block)
    for z in range(4):
        w_pack[z, 0:256, :] = w_t[...]
        w_pack[z, 256:272, :] = block.astype(BF)


def spread_kernel(block, out):
    for k in range(16):
        out[k] = block[...]


def row_block(n):
    core, odd = lax.axis_index("core"), lax.axis_index("y") & 1
    return 2 * (core ^ (n >> 1)) + ((n & 1) ^ odd)


def terms_kernel(own, other, w0, w1, w2, w3, dirs, pay):
    weights = (w0, w1, w2, w3)
    zh, sec = lax.axis_index("zh"), lax.axis_index("sec")
    acc = [jnp.zeros((2, 256), F32) for _ in range(4)]
    for z in range(4):
        mat = jnp.concatenate([w[z, 0:256, :] for w in weights], axis=1)
        for n in range(4):
            part = (own, other)[n >> 1][256 * (n & 1) : 256 * (n & 1) + 256, :]
            key = lax.dot_general(mat, part, NT, preferred_element_type=F32)
            wide = dirs[handler(zh, row_block(n), z), 0:128, :].astype(F32)
            acc[n] += jnp.concatenate(
                [
                    jnp.sum(wide * key[0:128], axis=0, keepdims=True),
                    jnp.sum(wide * key[128:256], axis=0, keepdims=True),
                ],
                axis=0,
            )
    for n in range(4):
        for p in range(2):
            for q in range(2):
                pay[pl.ds(8 * p + 4 * q + row_block(n), 1), :] = acc[n][
                    p : p + 1, 128 * q : 128 * (q + 1)
                ]
    lane = lax.broadcasted_iota(jnp.int32, (16, 128), 1)
    block = jnp.zeros((16, 128), F32)
    for k, w in enumerate(weights):
        tail = w[0, 256:272, :].astype(F32)
        for z in range(1, 4):
            tail = tail + w[z, 256:272, :].astype(F32)
        block = jnp.where((lane & 15) == ((sec - k) & 3), tail, block)
    fields = [block[0:1] + block[1:2] + block[2:3], block[3:4] + block[4:5] + block[5:6]]
    fields.extend(block[n : n + 1] for n in range(6, 10))
    facts = jnp.zeros((1, 128), F32)
    for n, field in enumerate(fields):
        facts = jnp.where((lane[0:1] >> 4) == n, field, facts)
    pay[16:24, :] = jnp.broadcast_to(facts, (8, 128))


def join_kernel(mine, partner, out):
    whole = mine[...] + partner[...]
    for d in range(16):
        out[d] = whole


def grads_kernel(pays, own, other, dirs, out, change, table, coefs):
    zh, sec, dp = lax.axis_index("zh"), lax.axis_index("sec"), dp_index()
    sums = pays[0, 0:16, :]
    for d in range(1, 16):
        sums = sums + pays[d, 0:16, :]
    tp, tr = sums[0:8], sums[8:16]
    facts = jnp.concatenate([pays[d, 16:17, :] for d in range(16)], axis=0)
    facts = jnp.concatenate([facts, pltpu.roll(facts, 112, 1)], axis=0)
    lane = lax.broadcasted_iota(jnp.int32, (32, 128), 1)
    used = lane < 4
    ids = pltpu.roll(facts, 96, 1) * 0.125
    lens = jnp.where(used, pltpu.roll(facts, 64, 1) * 0.125, 1.0)
    reward = facts / jnp.sqrt(lens)
    center = jnp.zeros((32, 128), F32)
    spread = jnp.zeros((32, 128), F32)
    for g in range(NGROUPS):
        member = used & (ids == float(g))
        mine = jnp.where(member, reward, 0.0)
        total = jnp.sum(jnp.sum(mine, axis=0, keepdims=True), axis=1, keepdims=True)
        square = jnp.sum(jnp.sum(mine * mine, axis=0, keepdims=True), axis=1, keepdims=True)
        mid = total / GROUP
        center = jnp.where(member, mid, center)
        spread = jnp.where(member, square / GROUP - mid * mid, spread)
    advantage = ((reward - center) / jnp.sqrt(spread + var_offset)).astype(BF).astype(F32)
    here = lane == sec
    picked = []
    for values in (advantage, lens):
        column = jnp.sum(jnp.where(here, values, 0.0), axis=1, keepdims=True)
        table[...] = jnp.broadcast_to(column, (32, 128))
        picked.append(
            jnp.concatenate(
                [table[pl.ds(16 * q + 4 * zh + a, 1), :] for q in range(2) for a in range(4)],
                axis=0,
            )
        )
    adv, length = picked
    valid = (lane[0:8].astype(F32) < length).astype(F32)
    coefs[...] = valid * (-adv * jnp.exp(tp) + kl_weight * (1.0 - jnp.exp(tr - tp)))
    for n in range(4):
        a = row_block(n)
        row = jnp.concatenate([coefs[pl.ds(a, 1), :], coefs[pl.ds(4 + a, 1), :]], axis=1)
        for z in range(4):
            change[128 * z : 128 * (z + 1), 256 * n : 256 * (n + 1)] = (
                dirs[handler(zh, a, z), 0:128, :].astype(F32) * row
            ).astype(BF)
    grad = jnp.dot(change[:, 0:512], own[...], preferred_element_type=F32)
    grad += jnp.dot(change[:, 512:1024], other[...], preferred_element_type=F32)
    grad = grad.astype(BF)
    for z in range(4):
        for k in range(4):
            out[4 * z + ((sec - k) & 3), 0:128, :] = grad[
                128 * z : 128 * (z + 1), 128 * k : 128 * (k + 1)
            ]
    marks, logps = [], []
    for a in range(4):
        facts = dirs[handler(zh, a, 0), 128:136, :].astype(F32)
        marks.append((facts[0:1] == dp.astype(F32)).astype(F32))
        logps.append(facts[1:2] + jnp.concatenate([tp[a : a + 1], tp[4 + a : 5 + a]], axis=1))
    zeros = jnp.zeros((4, 256), F32)
    before = (
        lax.broadcasted_iota(jnp.int32, (256, 256), 0)
        < lax.broadcasted_iota(jnp.int32, (256, 256), 1)
    ).astype(F32)
    ranks = jnp.dot(
        jnp.concatenate(marks + [zeros], axis=0).astype(BF),
        before.astype(BF),
        preferred_element_type=F32,
    )
    slot = lax.broadcasted_iota(jnp.int32, (SLOT, 256), 0).astype(F32)
    tails = []
    for a in range(4):
        place = jnp.where(slot == ranks[a : a + 1], marks[a], 0.0).astype(BF)
        hi, mid, lo = split3(logps[a])
        rows = jnp.concatenate([hi, mid, lo, zeros, zeros[0:1]], axis=0).astype(BF)
        tails.append(lax.dot_general(rows, place, NT, preferred_element_type=F32))
    tail = jnp.concatenate(tails, axis=1).astype(BF)
    for d in range(16):
        out[d, 128:136, :] = tail


def finish_kernel(parts, grad, packed):
    sec = lax.axis_index("sec")
    total = parts[0, 0:128, :].astype(F32)
    for d in range(1, 16):
        total = total + parts[d, 0:128, :].astype(F32)
    grad[...] = total.T
    pieces = []
    for z in range(4):
        row = jnp.sum(parts[4 * z + sec, 128:136, :].astype(F32), axis=0, keepdims=True)
        pieces.extend(row[:, SLOT * a : SLOT * a + CAP] for a in range(4))
    packed[...] = jnp.concatenate(pieces, axis=1)


def cost(flops, size):
    return pl.CostEstimate(flops=flops, bytes_accessed=size, transcendentals=0)


def shape(dims, dtype):
    return jax.ShapeDtypeStruct(dims, dtype)


def call(kernel, outs, scratch=(), smem=0, inputs=0, flops=0, size=0, vmem_mib=16):
    vmem = pl.BlockSpec(memory_space=pltpu.VMEM)
    scalar = pl.BlockSpec(memory_space=pltpu.SMEM)
    return pl.pallas_call(
        kernel,
        out_shape=outs,
        in_specs=[scalar] * smem + [vmem] * inputs,
        out_specs=jax.tree.map(lambda _: vmem, outs),
        scratch_shapes=list(scratch),
        cost_estimate=cost(flops, size),
        compiler_params=pltpu.CompilerParams(vmem_limit_bytes=vmem_mib << 20),
    )


def flat(i, zh, core, sec):
    return ((i * 4 + zh) * 2 + core) * 4 + sec


PLACES = [
    (i, zh, core, sec)
    for i in range(16)
    for zh in range(4)
    for core in range(2)
    for sec in range(4)
]
TO_HANDLER = [
    (flat(i, zz, core, sec), flat(handler(i >> 2, i & 3, zz), i >> 2, core, sec))
    for i, zz, core, sec in PLACES
]
TO_POOL = [
    [
        (
            flat(i, zh, core, sec),
            flat(4 * zh + 2 * core + (b ^ (i & 1)), i >> 2, (i >> 1) & 1, sec),
        )
        for i, zh, core, sec in PLACES
    ]
    for b in range(2)
]


def ring(step):
    return [(j, (j + step) % 4) for j in range(4)]


def swap(x):
    return lax.ppermute(x, "core", [(0, 1), (1, 0)])


def body(
    states, direction, old_logp, lengths, group_ids, routes, reward_head, policy_k, reference_k
):
    dir_t, w_t = call(
        turn_kernel,
        (shape((136, 256), BF), shape((256, 128), BF)),
        inputs=5,
        flops=1 << 16,
        size=1 << 18,
        vmem_mib=60,
    )(direction, routes.reshape(1, 256), old_logp.reshape(2, 128), policy_k, reference_k)
    dir_here = lax.ppermute(dir_t, ALL, TO_HANDLER)
    w_pack, half0, half1 = call(
        prepare_kernel,
        (shape((4, 272, 128), BF), shape((256, 512), BF), shape((256, 512), BF)),
        smem=2,
        inputs=3,
        flops=8 * 256 * 1024 * 2,
        size=1 << 20,
        vmem_mib=60,
    )(lengths, group_ids, states, reward_head.reshape(8, 128), w_t)
    w_cols = lax.all_to_all(w_pack, "zh", 0, 0, tiled=True)
    dir_here, w_cols = lax.optimization_barrier((dir_here, w_cols))
    dirs = call(spread_kernel, shape((16, 136, 256), BF), inputs=1, flops=1 << 10, size=1 << 20)(
        dir_here
    )
    dirs = lax.all_to_all(dirs, DP, 0, 0, tiled=True)
    weights = [w_cols] + [lax.ppermute(w_cols, "sec", ring(k)) for k in (1, 2, 3)]
    own = jnp.concatenate(
        [lax.ppermute(half0, ALL, TO_POOL[0]), lax.ppermute(half1, ALL, TO_POOL[1])], axis=0
    )
    other = swap(own)
    pay = call(terms_kernel, shape((24, 128), F32), inputs=7, flops=1 << 30, size=4 << 20)(
        own, other, *weights, dirs
    )
    pays = call(join_kernel, shape((16, 24, 128), F32), inputs=2, flops=1 << 12, size=1 << 18)(
        pay, swap(pay)
    )
    pays = lax.all_to_all(pays, DP, 0, 0, tiled=True)
    parts = call(
        grads_kernel,
        shape((16, 136, 128), BF),
        scratch=[
            pltpu.VMEM((512, 1024), BF),
            pltpu.VMEM((32, 128), F32),
            pltpu.VMEM((8, 128), F32),
        ],
        inputs=4,
        flops=1 << 29,
        size=4 << 20,
    )(pays, own, other, dirs)
    parts = lax.all_to_all(parts, ("zh", "sec"), 0, 0, tiled=True)
    grad, packed = call(
        finish_kernel,
        (shape((128, 128), F32), shape((1, 320), F32)),
        inputs=1,
        flops=1 << 20,
        size=1 << 20,
    )(parts)
    return grad, packed.reshape(1, 1, 320)


def solution(mesh):
    fine = Mesh(mesh.devices.reshape(2, 8, 4, 2, 4), ALL)
    rows, cols = ("zl", "y", "sec"), ("zh", "core")
    return jax.shard_map(
        body,
        mesh=fine,
        in_specs=(
            P(rows, cols),
            P(rows, cols),
            P(rows),
            P(rows),
            P(rows),
            P(rows, None),
            P(cols),
            P(rows, cols),
            P(rows, cols),
        ),
        out_specs=(P(rows, cols), P(DP, "sec", None)),
        check_vma=False,
    )
```

```python
import jax
import jax.numpy as jnp
from jax import lax
from jax.experimental import pallas as pl
from jax.experimental.pallas import tpu as pltpu
from jax.sharding import Mesh
from jax.sharding import PartitionSpec as P

GROUP = 8
NGROUPS = 16
CAP = 20
SLOT = 32

kl_weight = 0.4
var_offset = 0.25

DP = ("zl", "y")
ALL = ("zl", "y", "zh", "core", "sec")
BF = jnp.bfloat16
F32 = jnp.float32
NT = (((1,), (1,)), ((), ()))


def split3(x):
    hi = x.astype(BF).astype(F32)
    rest = x - hi
    mid = rest.astype(BF).astype(F32)
    return hi, mid, rest - mid


def dp_index():
    return lax.axis_index("zl") * 8 + lax.axis_index("y")


def handler(zh, block, zz):
    turn = (zz - zh + (zh >> 1)) & 3
    zl = (turn & 1) ^ (turn >> 1)
    near = 4 * (zh & 1)
    y = near + block + (1 - (turn >> 1)) * (7 - 2 * block)
    return zl * 8 + (y & 7)


def turn_kernel(direction, wp, wr, dir_t, w_t):
    turned = direction[...].astype(F32).T.astype(BF)
    for k in range(4):
        dir_t[k] = turned
    w_t[0:128, :] = wp[...].astype(F32).T.astype(BF)
    w_t[128:256, :] = wr[...].astype(F32).T.astype(BF)


def prepare_kernel(lengths, group_ids, states, head, routes, quarters, extra, slots):
    sec = lax.axis_index("sec")
    for k in range(4):
        to = lax.rem(k - sec + 4, 4)
        quarters[to, :, 0:128] = states[:, 128 * k : 128 * (k + 1)]
        quarters[to, :, 128:256] = states[:, 512 + 128 * k : 512 + 128 * (k + 1)]
    head_rows = head[...].astype(F32)
    wide_head = jnp.concatenate([head_rows[k : k + 1] for k in range(8)], axis=1).astype(BF)
    score = lax.dot_general(
        jnp.broadcast_to(wide_head, (8, 1024)), states[...], NT, preferred_element_type=F32
    )
    lane = lax.broadcasted_iota(jnp.int32, (1, 128), 1)
    rows = []
    for q in range(2):
        valid = (lane < lengths[q]).astype(F32)
        part = jnp.sum(score[0:1, 128 * q : 128 * (q + 1)] * valid, axis=1, keepdims=True)
        rows.extend(split3(part))
    for values in (group_ids, lengths):
        for q in range(2):
            rows.append(jnp.full((1, 1), values[q], jnp.int32).astype(F32))
    at = lax.broadcasted_iota(jnp.int32, (16, 128), 0)
    block = jnp.zeros((16, 128), F32)
    for n, row in enumerate(rows):
        block = jnp.where(at == n, row, block)
    extra[...] = block.astype(BF)
    target = routes[...]
    choose = (lax.broadcasted_iota(jnp.int32, (16, 256), 0) == target).astype(F32)
    before = (
        lax.broadcasted_iota(jnp.int32, (256, 256), 0)
        < lax.broadcasted_iota(jnp.int32, (256, 256), 1)
    ).astype(F32)
    ranked = jnp.dot(choose.astype(BF), before.astype(BF), preferred_element_type=F32)
    rank = jnp.sum(choose * ranked, axis=0, keepdims=True)
    slots[...] = target * SLOT + rank.astype(jnp.int32)


def pack_kernel(quarters, dirs, *outs):
    for k in range(4):
        outs[k][0:256, :] = quarters[k]
        for q in range(4):
            outs[k][256 + 128 * q : 384 + 128 * q, :] = dirs[q]


def spread_kernel(w, extra, out):
    for k in range(16):
        out[k, 0:256, :] = w[...]
        out[k, 256:272, :] = extra[...]


def terms_kernel(s0, s1, s2, s3, other, weights, pay):
    shares = (s0, s1, s2, s3)
    zh, core, sec = (lax.axis_index(name) for name in ("zh", "core", "sec"))
    acc = [jnp.zeros((2, 256), F32) for _ in range(4)]
    for q in range(4):
        mats = [
            jnp.concatenate(
                [weights[handler(zh, 2 * u + h, q), 0:256, :] for h in range(2)], axis=1
            )
            for u in (core, 1 - core)
        ]
        for s, share in enumerate(shares):
            key = lax.dot_general(mats[0], share[0:256, :], NT, preferred_element_type=F32)
            key += lax.dot_general(
                mats[1], other[256 * s : 256 * (s + 1), :], NT, preferred_element_type=F32
            )
            wide = share[256 + 128 * q : 384 + 128 * q, :].astype(F32)
            acc[s] += jnp.concatenate(
                [
                    jnp.sum(wide * key[0:128], axis=0, keepdims=True),
                    jnp.sum(wide * key[128:256], axis=0, keepdims=True),
                ],
                axis=0,
            )
    for s in range(4):
        for p in range(2):
            for q in range(2):
                pay[pl.ds(8 * p + 4 * q + ((sec - s) & 3), 1), :] = acc[s][
                    p : p + 1, 128 * q : 128 * (q + 1)
                ]
    lane = lax.broadcasted_iota(jnp.int32, (16, 128), 1)
    block = jnp.zeros((16, 128), F32)
    for i in range(16):
        block = jnp.where((lane & 15) == i, weights[i, 256:272, :].astype(F32), block)
    fields = [block[0:1] + block[1:2] + block[2:3], block[3:4] + block[4:5] + block[5:6]]
    fields.extend(block[n : n + 1] for n in range(6, 10))
    facts = jnp.zeros((1, 128), F32)
    for n, field in enumerate(fields):
        facts = jnp.where((lane[0:1] >> 4) == n, field, facts)
    pay[16:24, :] = jnp.broadcast_to(facts, (8, 128))


def join_kernel(mine, partner, out):
    whole = mine[...] + partner[...]
    for d in range(16):
        out[d] = whole


def grads_kernel(pays, s0, s1, s2, s3, other, old_logp, slots, out, change, coefs):
    shares = (s0, s1, s2, s3)
    zh, core, sec = (lax.axis_index(name) for name in ("zh", "core", "sec"))
    dp = dp_index()
    sums = pays[0, 0:16, :]
    for d in range(1, 16):
        sums = sums + pays[d, 0:16, :]
    tp, tr = sums[0:8], sums[8:16]
    facts = []
    for s in range(4):
        fact = pays[s, 16:17, :]
        for d in range(1, 4):
            fact = fact + pays[4 * d + s, 16:17, :]
        facts.append(fact)
    facts = jnp.concatenate(facts + facts, axis=0)
    lane = lax.broadcasted_iota(jnp.int32, (8, 128), 1)
    at = lax.broadcasted_iota(jnp.int32, (8, 128), 0)
    facts = jnp.where(at < 4, facts, pltpu.roll(facts, 112, 1))
    used = lane < 16
    ids = pltpu.roll(facts, 96, 1) * 0.125
    lens = jnp.where(used, pltpu.roll(facts, 64, 1) * 0.125, 1.0)
    reward = facts / jnp.sqrt(lens)
    center = jnp.zeros((8, 128), F32)
    spread = jnp.zeros((8, 128), F32)
    for g in range(NGROUPS):
        member = used & (ids == float(g))
        mine = jnp.where(member, reward, 0.0)
        total = jnp.sum(jnp.sum(mine, axis=0, keepdims=True), axis=1, keepdims=True)
        square = jnp.sum(jnp.sum(mine * mine, axis=0, keepdims=True), axis=1, keepdims=True)
        mid = total / GROUP
        center = jnp.where(member, mid, center)
        spread = jnp.where(member, square / GROUP - mid * mid, spread)
    advantage = ((reward - center) / jnp.sqrt(spread + var_offset)).astype(BF).astype(F32)
    here = lane == dp
    adv = jnp.sum(jnp.where(here, advantage, 0.0), axis=1, keepdims=True)
    length = jnp.sum(jnp.where(here, lens, 0.0), axis=1, keepdims=True)
    valid = (lane.astype(F32) < length).astype(F32)
    coef = valid * (-adv * jnp.exp(tp) + kl_weight * (1.0 - jnp.exp(tr - tp)))
    coefs[...] = coef
    for s in range(4):
        from_sec = (sec - s) & 3
        row = jnp.concatenate(
            [coefs[pl.ds(from_sec, 1), :], coefs[pl.ds(4 + from_sec, 1), :]], axis=1
        )
        for q in range(4):
            change[128 * q : 128 * (q + 1), 256 * s : 256 * (s + 1)] = (
                shares[s][256 + 128 * q : 384 + 128 * q, :].astype(F32) * row
            ).astype(BF)
    grads = [
        jnp.dot(change[:, 0:256], s0[0:256, :], preferred_element_type=F32),
        jnp.dot(change[...], other[...], preferred_element_type=F32),
    ]
    for s in range(1, 4):
        grads[0] += jnp.dot(
            change[:, 256 * s : 256 * (s + 1)], shares[s][0:256, :], preferred_element_type=F32
        )
    for u, grad in ((core, grads[0]), (1 - core, grads[1])):
        grad = grad.astype(BF)
        for h in range(2):
            for q in range(4):
                out[handler(zh, 2 * u + h, q), 0:128, :] = grad[
                    128 * q : 128 * (q + 1), 128 * h : 128 * (h + 1)
                ]
    old = old_logp[...].astype(F32)
    logp = jnp.concatenate(
        [
            old[q : q + 1] + jnp.sum(jnp.where(at == 4 * q + sec, tp, 0.0), axis=0, keepdims=True)
            for q in range(2)
        ],
        axis=1,
    )
    hi, mid, lo = split3(logp)
    rows = jnp.concatenate([hi, mid, lo, jnp.zeros((5, 256), F32)], axis=0).astype(BF)
    place = (lax.broadcasted_iota(jnp.int32, (16 * SLOT, 256), 0) == slots[...]).astype(F32)
    placed = lax.dot_general(rows, place.astype(BF), NT, preferred_element_type=F32)
    for a in range(4):
        tail = placed[:, 128 * a : 128 * (a + 1)].astype(BF)
        for k in range(4):
            out[4 * a + k, 128:136, :] = tail
            out[4 * a + k, 136:144, :] = jnp.zeros((8, 128), BF)


def finish_kernel(parts, grad, packed):
    dp = dp_index()
    total = parts[0, 0:128, :].astype(F32)
    for i in range(1, 16):
        total = total + parts[i, 0:128, :].astype(F32)
    grad[...] = total.T
    rows = [
        jnp.sum(parts[i, 128:136, :].astype(F32), axis=0, keepdims=True) for i in range(16)
    ]
    table = jnp.concatenate(rows, axis=0)
    pick = jnp.zeros((16, SLOT), F32)
    for a in range(4):
        pick = jnp.where(lax.rem(dp, 4) == a, table[:, SLOT * a : SLOT * (a + 1)], pick)
    packed[...] = jnp.concatenate([pick[i : i + 1, 0:CAP] for i in range(16)], axis=1)


def cost(flops, size):
    return pl.CostEstimate(flops=flops, bytes_accessed=size, transcendentals=0)


def shape(dims, dtype):
    return jax.ShapeDtypeStruct(dims, dtype)


def call(kernel, outs, scratch=(), smem=0, inputs=0, flops=0, size=0, vmem_mib=16):
    vmem = pl.BlockSpec(memory_space=pltpu.VMEM)
    scalar = pl.BlockSpec(memory_space=pltpu.SMEM)
    return pl.pallas_call(
        kernel,
        out_shape=outs,
        in_specs=[scalar] * smem + [vmem] * inputs,
        out_specs=jax.tree.map(lambda _: vmem, outs),
        scratch_shapes=list(scratch),
        cost_estimate=cost(flops, size),
        compiler_params=pltpu.CompilerParams(vmem_limit_bytes=vmem_mib << 20),
    )


def flat(i, zh, core, sec):
    return ((i * 4 + zh) * 2 + core) * 4 + sec


TO_HANDLER = [
    (flat(i, zz, core, sec), flat(handler(i >> 2, i & 3, zz), i >> 2, core, sec))
    for i in range(16)
    for zz in range(4)
    for core in range(2)
    for sec in range(4)
]
TO_OWNER = [(b, a) for a, b in TO_HANDLER]


def ring(step):
    return [(j, (j + step) % 4) for j in range(4)]


def body(
    states, direction, old_logp, lengths, group_ids, routes, reward_head, policy_k, reference_k
):
    dir_t, w_t = call(
        turn_kernel,
        (shape((4, 128, 256), BF), shape((256, 128), BF)),
        inputs=3,
        flops=1 << 16,
        size=1 << 18,
        vmem_mib=60,
    )(direction, policy_k, reference_k)
    w_here = lax.ppermute(w_t, ALL, TO_HANDLER)
    quarters, extra, slots = call(
        prepare_kernel,
        (shape((4, 256, 256), BF), shape((16, 128), BF), shape((1, 256), jnp.int32)),
        smem=2,
        inputs=3,
        flops=8 * 256 * 1024 * 2,
        size=1 << 20,
        vmem_mib=60,
    )(lengths, group_ids, states, reward_head.reshape(8, 128), routes.reshape(1, 256))
    dirs = lax.all_to_all(dir_t, "zh", 0, 0, tiled=True)
    weights = call(
        spread_kernel, shape((16, 272, 128), BF), inputs=2, flops=1 << 10, size=1 << 20
    )(w_here, extra)
    weights = lax.all_to_all(weights, DP, 0, 0, tiled=True)
    packs = call(
        pack_kernel, (shape((768, 256), BF),) * 4, inputs=2, flops=1 << 10, size=3 << 20
    )(quarters, dirs)
    shares = [packs[0]] + [lax.ppermute(packs[k], "sec", ring(k)) for k in (1, 2, 3)]
    other = lax.ppermute(
        jnp.concatenate([share[0:256] for share in shares], axis=0), "core", [(0, 1), (1, 0)]
    )
    pay = call(
        terms_kernel, shape((24, 128), F32), inputs=6, flops=1 << 30, size=4 << 20
    )(*shares, other, weights)
    pays = call(join_kernel, shape((16, 24, 128), F32), inputs=2, flops=1 << 12, size=1 << 18)(
        pay, lax.ppermute(pay, "core", [(0, 1), (1, 0)])
    )
    pays = lax.all_to_all(pays, ("zh", "sec"), 0, 0, tiled=True)
    parts = call(
        grads_kernel,
        shape((16, 144, 128), BF),
        scratch=[
            pltpu.VMEM((512, 1024), BF),
            pltpu.VMEM((8, 128), F32),
        ],
        inputs=8,
        flops=1 << 29,
        size=4 << 20,
    )(pays, *shares, other, old_logp.reshape(2, 128), slots)
    parts = lax.all_to_all(parts, DP, 0, 0, tiled=True)
    grad, packed = call(
        finish_kernel,
        (shape((128, 128), F32), shape((1, 320), F32)),
        inputs=1,
        flops=1 << 20,
        size=1 << 20,
    )(parts)
    return lax.ppermute(grad, ALL, TO_OWNER), packed.reshape(1, 1, 320)


def solution(mesh):
    fine = Mesh(mesh.devices.reshape(2, 8, 4, 2, 4), ALL)
    rows, cols = ("zl", "y", "sec"), ("zh", "core")
    return jax.shard_map(
        body,
        mesh=fine,
        in_specs=(
            P(rows, cols),
            P(rows, cols),
            P(rows),
            P(rows),
            P(rows),
            P(rows, None),
            P(cols),
            P(rows, cols),
            P(rows, cols),
        ),
        out_specs=(P(rows, cols), P(DP, "sec", None)),
        check_vma=False,
    )
```

```python
import jax
import jax.numpy as jnp
from jax import lax
from jax.experimental import pallas as pl
from jax.experimental.pallas import tpu as pltpu
from jax.sharding import Mesh
from jax.sharding import PartitionSpec as P

GROUP = 8
NGROUPS = 16
CAP = 20
SLOT = 32

kl_weight = 0.4
var_offset = 0.25

DP = ("zl", "y")
ALL = ("zl", "y", "zh", "core", "sec")
BF = jnp.bfloat16
F32 = jnp.float32
NT = (((1,), (1,)), ((), ()))


def split3(x):
    hi = x.astype(BF).astype(F32)
    rest = x - hi
    mid = rest.astype(BF).astype(F32)
    return hi, mid, rest - mid


def dp_index():
    return lax.axis_index("zl") * 8 + lax.axis_index("y")


def handler(zh, block, zz):
    turn = (zz - zh + (zh >> 1)) & 3
    zl = (turn & 1) ^ (turn >> 1)
    near = 4 * (zh & 1)
    y = near + block + (1 - (turn >> 1)) * (7 - 2 * block)
    return zl * 8 + (y & 7)


def turn_kernel(direction, wp, wr, dir_t, w_t):
    turned = direction[...].astype(F32).T.astype(BF)
    for k in range(4):
        dir_t[k] = turned
    w_t[0:128, :] = wp[...].astype(F32).T.astype(BF)
    w_t[128:256, :] = wr[...].astype(F32).T.astype(BF)


def prepare_kernel(lengths, group_ids, states, head, routes, quarters, extra, slots):
    sec = lax.axis_index("sec")
    for k in range(4):
        to = lax.rem(k - sec + 4, 4)
        quarters[to, :, 0:128] = states[:, 128 * k : 128 * (k + 1)]
        quarters[to, :, 128:256] = states[:, 512 + 128 * k : 512 + 128 * (k + 1)]
    head_rows = head[...].astype(F32)
    wide_head = jnp.concatenate([head_rows[k : k + 1] for k in range(8)], axis=1).astype(BF)
    score = lax.dot_general(
        jnp.broadcast_to(wide_head, (8, 1024)), states[...], NT, preferred_element_type=F32
    )
    lane = lax.broadcasted_iota(jnp.int32, (1, 128), 1)
    rows = []
    for q in range(2):
        valid = (lane < lengths[q]).astype(F32)
        part = jnp.sum(score[0:1, 128 * q : 128 * (q + 1)] * valid, axis=1, keepdims=True)
        rows.extend(split3(part))
    for values in (group_ids, lengths):
        for q in range(2):
            rows.append(jnp.full((1, 1), values[q], jnp.int32).astype(F32))
    at = lax.broadcasted_iota(jnp.int32, (16, 128), 0)
    block = jnp.zeros((16, 128), F32)
    for n, row in enumerate(rows):
        block = jnp.where(at == n, row, block)
    extra[...] = block.astype(BF)
    target = routes[...]
    choose = (lax.broadcasted_iota(jnp.int32, (16, 256), 0) == target).astype(F32)
    before = (
        lax.broadcasted_iota(jnp.int32, (256, 256), 0)
        < lax.broadcasted_iota(jnp.int32, (256, 256), 1)
    ).astype(F32)
    ranked = jnp.dot(choose.astype(BF), before.astype(BF), preferred_element_type=F32)
    rank = jnp.sum(choose * ranked, axis=0, keepdims=True)
    slots[...] = target * SLOT + rank.astype(jnp.int32)


def pack_kernel(quarters, dirs, *outs):
    for k in range(4):
        outs[k][0:256, :] = quarters[k]
        for q in range(4):
            outs[k][256 + 128 * q : 384 + 128 * q, :] = dirs[q]


def spread_kernel(w, extra, out, sems):
    copies = []
    for k in range(16):
        copies.append(pltpu.make_async_copy(w, out.at[k, 0:256, :], sems.at[k]))
        copies.append(pltpu.make_async_copy(extra, out.at[k, 256:272, :], sems.at[16 + k]))
    for copy in copies:
        copy.start()
    for copy in copies:
        copy.wait()


def terms_kernel(s0, s1, s2, s3, other, weights, pay):
    shares = (s0, s1, s2, s3)
    zh, core, sec = (lax.axis_index(name) for name in ("zh", "core", "sec"))
    acc = [jnp.zeros((2, 256), F32) for _ in range(4)]
    for q in range(4):
        mats = [
            jnp.concatenate(
                [weights[handler(zh, 2 * u + h, q), 0:256, :] for h in range(2)], axis=1
            )
            for u in (core, 1 - core)
        ]
        for s, share in enumerate(shares):
            key = lax.dot_general(mats[0], share[0:256, :], NT, preferred_element_type=F32)
            key += lax.dot_general(
                mats[1], other[256 * s : 256 * (s + 1), :], NT, preferred_element_type=F32
            )
            wide = share[256 + 128 * q : 384 + 128 * q, :].astype(F32)
            acc[s] += jnp.concatenate(
                [
                    jnp.sum(wide * key[0:128], axis=0, keepdims=True),
                    jnp.sum(wide * key[128:256], axis=0, keepdims=True),
                ],
                axis=0,
            )
    for s in range(4):
        for p in range(2):
            for q in range(2):
                pay[pl.ds(8 * p + 4 * q + ((sec - s) & 3), 1), :] = acc[s][
                    p : p + 1, 128 * q : 128 * (q + 1)
                ]
    lane = lax.broadcasted_iota(jnp.int32, (16, 128), 1)
    block = jnp.zeros((16, 128), F32)
    for i in range(16):
        block = jnp.where((lane & 15) == i, weights[i, 256:272, :].astype(F32), block)
    fields = [block[0:1] + block[1:2] + block[2:3], block[3:4] + block[4:5] + block[5:6]]
    fields.extend(block[n : n + 1] for n in range(6, 10))
    facts = jnp.zeros((1, 128), F32)
    for n, field in enumerate(fields):
        facts = jnp.where((lane[0:1] >> 4) == n, field, facts)
    pay[16:24, :] = jnp.broadcast_to(facts, (8, 128))


def join_kernel(mine, partner, out):
    whole = mine[...] + partner[...]
    for d in range(16):
        out[d] = whole


def grads_kernel(pays, s0, s1, s2, s3, other, old_logp, slots, out, change, coefs):
    shares = (s0, s1, s2, s3)
    zh, core, sec = (lax.axis_index(name) for name in ("zh", "core", "sec"))
    dp = dp_index()
    sums = pays[0, 0:16, :]
    for d in range(1, 16):
        sums = sums + pays[d, 0:16, :]
    tp, tr = sums[0:8], sums[8:16]
    facts = []
    for s in range(4):
        fact = pays[s, 16:17, :]
        for d in range(1, 4):
            fact = fact + pays[4 * d + s, 16:17, :]
        facts.append(fact)
    facts = jnp.concatenate(facts + facts, axis=0)
    lane = lax.broadcasted_iota(jnp.int32, (8, 128), 1)
    at = lax.broadcasted_iota(jnp.int32, (8, 128), 0)
    facts = jnp.where(at < 4, facts, pltpu.roll(facts, 112, 1))
    used = lane < 16
    ids = pltpu.roll(facts, 96, 1) * 0.125
    lens = jnp.where(used, pltpu.roll(facts, 64, 1) * 0.125, 1.0)
    reward = facts / jnp.sqrt(lens)
    center = jnp.zeros((8, 128), F32)
    spread = jnp.zeros((8, 128), F32)
    for g in range(NGROUPS):
        member = used & (ids == float(g))
        mine = jnp.where(member, reward, 0.0)
        total = jnp.sum(jnp.sum(mine, axis=0, keepdims=True), axis=1, keepdims=True)
        square = jnp.sum(jnp.sum(mine * mine, axis=0, keepdims=True), axis=1, keepdims=True)
        mid = total / GROUP
        center = jnp.where(member, mid, center)
        spread = jnp.where(member, square / GROUP - mid * mid, spread)
    advantage = ((reward - center) / jnp.sqrt(spread + var_offset)).astype(BF).astype(F32)
    here = lane == dp
    adv = jnp.sum(jnp.where(here, advantage, 0.0), axis=1, keepdims=True)
    length = jnp.sum(jnp.where(here, lens, 0.0), axis=1, keepdims=True)
    valid = (lane.astype(F32) < length).astype(F32)
    coef = valid * (-adv * jnp.exp(tp) + kl_weight * (1.0 - jnp.exp(tr - tp)))
    coefs[...] = coef
    for s in range(4):
        from_sec = (sec - s) & 3
        row = jnp.concatenate(
            [coefs[pl.ds(from_sec, 1), :], coefs[pl.ds(4 + from_sec, 1), :]], axis=1
        )
        for q in range(4):
            change[128 * q : 128 * (q + 1), 256 * s : 256 * (s + 1)] = (
                shares[s][256 + 128 * q : 384 + 128 * q, :].astype(F32) * row
            ).astype(BF)
    grads = [
        jnp.dot(change[:, 0:256], s0[0:256, :], preferred_element_type=F32),
        jnp.dot(change[...], other[...], preferred_element_type=F32),
    ]
    for s in range(1, 4):
        grads[0] += jnp.dot(
            change[:, 256 * s : 256 * (s + 1)], shares[s][0:256, :], preferred_element_type=F32
        )
    for u, grad in ((core, grads[0]), (1 - core, grads[1])):
        grad = grad.astype(BF)
        for h in range(2):
            for q in range(4):
                out[handler(zh, 2 * u + h, q), 0:128, :] = grad[
                    128 * q : 128 * (q + 1), 128 * h : 128 * (h + 1)
                ]
    old = old_logp[...].astype(F32)
    logp = jnp.concatenate(
        [
            old[q : q + 1] + jnp.sum(jnp.where(at == 4 * q + sec, tp, 0.0), axis=0, keepdims=True)
            for q in range(2)
        ],
        axis=1,
    )
    hi, mid, lo = split3(logp)
    rows = jnp.concatenate([hi, mid, lo, jnp.zeros((5, 256), F32)], axis=0).astype(BF)
    place = (lax.broadcasted_iota(jnp.int32, (16 * SLOT, 256), 0) == slots[...]).astype(F32)
    placed = lax.dot_general(rows, place.astype(BF), NT, preferred_element_type=F32)
    for a in range(4):
        tail = placed[:, 128 * a : 128 * (a + 1)].astype(BF)
        for k in range(4):
            out[4 * a + k, 128:136, :] = tail


def finish_kernel(parts, grad, packed):
    dp = dp_index()
    total = parts[0, 0:128, :].astype(F32)
    for i in range(1, 16):
        total = total + parts[i, 0:128, :].astype(F32)
    grad[...] = total.T
    rows = [
        jnp.sum(parts[i, 128:136, :].astype(F32), axis=0, keepdims=True) for i in range(16)
    ]
    table = jnp.concatenate(rows, axis=0)
    pick = jnp.zeros((16, SLOT), F32)
    for a in range(4):
        pick = jnp.where(lax.rem(dp, 4) == a, table[:, SLOT * a : SLOT * (a + 1)], pick)
    packed[...] = jnp.concatenate([pick[i : i + 1, 0:CAP] for i in range(16)], axis=1)


def cost(flops, size):
    return pl.CostEstimate(flops=flops, bytes_accessed=size, transcendentals=0)


def shape(dims, dtype):
    return jax.ShapeDtypeStruct(dims, dtype)


def call(kernel, outs, scratch=(), smem=0, inputs=0, flops=0, size=0, vmem_mib=16):
    vmem = pl.BlockSpec(memory_space=pltpu.VMEM)
    scalar = pl.BlockSpec(memory_space=pltpu.SMEM)
    return pl.pallas_call(
        kernel,
        out_shape=outs,
        in_specs=[scalar] * smem + [vmem] * inputs,
        out_specs=jax.tree.map(lambda _: vmem, outs),
        scratch_shapes=list(scratch),
        cost_estimate=cost(flops, size),
        compiler_params=pltpu.CompilerParams(vmem_limit_bytes=vmem_mib << 20),
    )


def flat(i, zh, core, sec):
    return ((i * 4 + zh) * 2 + core) * 4 + sec


TO_HANDLER = [
    (flat(i, zz, core, sec), flat(handler(i >> 2, i & 3, zz), i >> 2, core, sec))
    for i in range(16)
    for zz in range(4)
    for core in range(2)
    for sec in range(4)
]
TO_OWNER = [(b, a) for a, b in TO_HANDLER]


def ring(step):
    return [(j, (j + step) % 4) for j in range(4)]


def body(
    states, direction, old_logp, lengths, group_ids, routes, reward_head, policy_k, reference_k
):
    dir_t, w_t = call(
        turn_kernel,
        (shape((4, 128, 256), BF), shape((256, 128), BF)),
        inputs=3,
        flops=1 << 16,
        size=1 << 18,
        vmem_mib=60,
    )(direction, policy_k, reference_k)
    w_here = lax.ppermute(w_t, ALL, TO_HANDLER)
    quarters, extra, slots = call(
        prepare_kernel,
        (shape((4, 256, 256), BF), shape((16, 128), BF), shape((1, 256), jnp.int32)),
        smem=2,
        inputs=3,
        flops=8 * 256 * 1024 * 2,
        size=1 << 20,
        vmem_mib=60,
    )(lengths, group_ids, states, reward_head.reshape(8, 128), routes.reshape(1, 256))
    dirs = lax.all_to_all(dir_t, "zh", 0, 0, tiled=True)
    anywhere = pl.BlockSpec(memory_space=pl.ANY)
    weights = pl.pallas_call(
        spread_kernel,
        out_shape=shape((16, 272, 128), BF),
        in_specs=[anywhere, pl.BlockSpec(memory_space=pltpu.HBM)],
        out_specs=anywhere,
        scratch_shapes=[pltpu.SemaphoreType.DMA((32,))],
        cost_estimate=cost(1 << 10, 1 << 20),
        compiler_params=pltpu.CompilerParams(vmem_limit_bytes=16 << 20),
    )(w_here, extra)
    weights = lax.all_to_all(weights, DP, 0, 0, tiled=True)
    packs = call(
        pack_kernel, (shape((768, 256), BF),) * 4, inputs=2, flops=1 << 10, size=3 << 20
    )(quarters, dirs)
    shares = [packs[0]] + [lax.ppermute(packs[k], "sec", ring(k)) for k in (1, 2, 3)]
    other = lax.ppermute(
        jnp.concatenate([share[0:256] for share in shares], axis=0), "core", [(0, 1), (1, 0)]
    )
    pay = call(
        terms_kernel, shape((24, 128), F32), inputs=6, flops=1 << 30, size=4 << 20
    )(*shares, other, weights)
    pays = call(join_kernel, shape((16, 24, 128), F32), inputs=2, flops=1 << 12, size=1 << 18)(
        pay, lax.ppermute(pay, "core", [(0, 1), (1, 0)])
    )
    pays = lax.all_to_all(pays, ("zh", "sec"), 0, 0, tiled=True)
    parts = call(
        grads_kernel,
        shape((16, 136, 128), BF),
        scratch=[
            pltpu.VMEM((512, 1024), BF),
            pltpu.VMEM((8, 128), F32),
        ],
        inputs=8,
        flops=1 << 29,
        size=4 << 20,
    )(pays, *shares, other, old_logp.reshape(2, 128), slots)
    parts = lax.all_to_all(parts, DP, 0, 0, tiled=True)
    grad, packed = call(
        finish_kernel,
        (shape((128, 128), F32), shape((1, 320), F32)),
        inputs=1,
        flops=1 << 20,
        size=1 << 20,
    )(parts)
    return lax.ppermute(grad, ALL, TO_OWNER), packed.reshape(1, 1, 320)


def solution(mesh):
    fine = Mesh(mesh.devices.reshape(2, 8, 4, 2, 4), ALL)
    rows, cols = ("zl", "y", "sec"), ("zh", "core")
    return jax.shard_map(
        body,
        mesh=fine,
        in_specs=(
            P(rows, cols),
            P(rows, cols),
            P(rows),
            P(rows),
            P(rows),
            P(rows, None),
            P(cols),
            P(rows, cols),
            P(rows, cols),
        ),
        out_specs=(P(rows, cols), P(DP, "sec", None)),
        check_vma=False,
    )
```

```python
import jax
import jax.numpy as jnp
from jax import lax
from jax.experimental import pallas as pl
from jax.experimental.pallas import tpu as pltpu
from jax.sharding import Mesh
from jax.sharding import PartitionSpec as P

GROUP = 8
NGROUPS = 16
CAP = 20
SLOT = 32

STEPS = (0, 2, 1, 3)

kl_weight = 0.4
var_offset = 0.25

DP = ("zl", "y")
ALL = ("zl", "y", "zh", "core", "sec")
BF = jnp.bfloat16
F32 = jnp.float32
NT = (((1,), (1,)), ((), ()))


def split3(x):
    hi = x.astype(BF).astype(F32)
    rest = x - hi
    mid = rest.astype(BF).astype(F32)
    return hi, mid, rest - mid


def dp_index():
    return lax.axis_index("zl") * 8 + lax.axis_index("y")


def handler(zh, block, zz):
    turn = (zz - zh + (zh >> 1)) & 3
    zl = (turn & 1) ^ (turn >> 1)
    near = 4 * (zh & 1)
    y = near + block + (1 - (turn >> 1)) * (7 - 2 * block)
    return zl * 8 + (y & 7)


def turn_kernel(direction, wp, wr, dir_t, w_t):
    turned = direction[...].astype(F32).T.astype(BF)
    for k in range(4):
        dir_t[k] = turned
    w_t[0:128, :] = wp[...].astype(F32).T.astype(BF)
    w_t[128:256, :] = wr[...].astype(F32).T.astype(BF)


def prepare_kernel(lengths, group_ids, states, head, routes, quarters, extra, slots):
    sec = lax.axis_index("sec")
    for k in range(4):
        to = lax.rem(k - sec + 4, 4)
        quarters[to, :, 0:128] = states[:, 128 * k : 128 * (k + 1)]
        quarters[to, :, 128:256] = states[:, 512 + 128 * k : 512 + 128 * (k + 1)]
    head_rows = head[...].astype(F32)
    wide_head = jnp.concatenate([head_rows[k : k + 1] for k in range(8)], axis=1).astype(BF)
    score = lax.dot_general(
        jnp.broadcast_to(wide_head, (8, 1024)), states[...], NT, preferred_element_type=F32
    )
    lane = lax.broadcasted_iota(jnp.int32, (1, 128), 1)
    rows = []
    for q in range(2):
        valid = (lane < lengths[q]).astype(F32)
        part = jnp.sum(score[0:1, 128 * q : 128 * (q + 1)] * valid, axis=1, keepdims=True)
        rows.extend(split3(part))
    for values in (group_ids, lengths):
        for q in range(2):
            rows.append(jnp.full((1, 1), values[q], jnp.int32).astype(F32))
    at = lax.broadcasted_iota(jnp.int32, (16, 128), 0)
    block = jnp.zeros((16, 128), F32)
    for n, row in enumerate(rows):
        block = jnp.where(at == n, row, block)
    extra[...] = block.astype(BF)
    target = routes[...]
    choose = (lax.broadcasted_iota(jnp.int32, (16, 256), 0) == target).astype(F32)
    before = (
        lax.broadcasted_iota(jnp.int32, (256, 256), 0)
        < lax.broadcasted_iota(jnp.int32, (256, 256), 1)
    ).astype(F32)
    ranked = jnp.dot(choose.astype(BF), before.astype(BF), preferred_element_type=F32)
    rank = jnp.sum(choose * ranked, axis=0, keepdims=True)
    slots[...] = target * SLOT + rank.astype(jnp.int32)


def pack_kernel(quarters, dirs, *outs):
    for k in range(4):
        outs[k][0:256, :] = quarters[STEPS[k]]
        for q in range(4):
            outs[k][256 + 128 * q : 384 + 128 * q, :] = dirs[q]


def spread_kernel(w, extra, out, sems):
    copies = []
    for k in range(16):
        copies.append(pltpu.make_async_copy(w, out.at[k, 0:256, :], sems.at[k]))
        copies.append(pltpu.make_async_copy(extra, out.at[k, 256:272, :], sems.at[16 + k]))
    for copy in copies:
        copy.start()
    for copy in copies:
        copy.wait()


def terms_kernel(s0, s1, s2, s3, other, weights, pay):
    shares = (s0, s1, s2, s3)
    zh, core, sec = (lax.axis_index(name) for name in ("zh", "core", "sec"))
    acc = [jnp.zeros((2, 256), F32) for _ in range(4)]
    for q in range(4):
        mats = [
            jnp.concatenate(
                [weights[handler(zh, 2 * u + h, q), 0:256, :] for h in range(2)], axis=1
            )
            for u in (core, 1 - core)
        ]
        for s, share in enumerate(shares):
            key = lax.dot_general(mats[0], share[0:256, :], NT, preferred_element_type=F32)
            key += lax.dot_general(
                mats[1], other[256 * s : 256 * (s + 1), :], NT, preferred_element_type=F32
            )
            wide = share[256 + 128 * q : 384 + 128 * q, :].astype(F32)
            acc[s] += jnp.concatenate(
                [
                    jnp.sum(wide * key[0:128], axis=0, keepdims=True),
                    jnp.sum(wide * key[128:256], axis=0, keepdims=True),
                ],
                axis=0,
            )
    for s in range(4):
        for p in range(2):
            for q in range(2):
                pay[pl.ds(8 * p + 4 * q + ((sec - STEPS[s]) & 3), 1), :] = acc[s][
                    p : p + 1, 128 * q : 128 * (q + 1)
                ]
    lane = lax.broadcasted_iota(jnp.int32, (16, 128), 1)
    block = jnp.zeros((16, 128), F32)
    for i in range(16):
        block = jnp.where((lane & 15) == i, weights[i, 256:272, :].astype(F32), block)
    fields = [block[0:1] + block[1:2] + block[2:3], block[3:4] + block[4:5] + block[5:6]]
    fields.extend(block[n : n + 1] for n in range(6, 10))
    facts = jnp.zeros((1, 128), F32)
    for n, field in enumerate(fields):
        facts = jnp.where((lane[0:1] >> 4) == n, field, facts)
    pay[16:24, :] = jnp.broadcast_to(facts, (8, 128))


def join_kernel(mine, partner, out):
    whole = mine[...] + partner[...]
    for d in range(16):
        out[d] = whole


def grads_kernel(pays, s0, s1, s2, s3, other, old_logp, slots, out, change, coefs):
    shares = (s0, s1, s2, s3)
    zh, core, sec = (lax.axis_index(name) for name in ("zh", "core", "sec"))
    dp = dp_index()
    sums = pays[0, 0:16, :]
    for d in range(1, 16):
        sums = sums + pays[d, 0:16, :]
    tp, tr = sums[0:8], sums[8:16]
    facts = []
    for s in range(4):
        fact = pays[s, 16:17, :]
        for d in range(1, 4):
            fact = fact + pays[4 * d + s, 16:17, :]
        facts.append(fact)
    facts = jnp.concatenate(facts + facts, axis=0)
    lane = lax.broadcasted_iota(jnp.int32, (8, 128), 1)
    at = lax.broadcasted_iota(jnp.int32, (8, 128), 0)
    facts = jnp.where(at < 4, facts, pltpu.roll(facts, 112, 1))
    used = lane < 16
    ids = pltpu.roll(facts, 96, 1) * 0.125
    lens = jnp.where(used, pltpu.roll(facts, 64, 1) * 0.125, 1.0)
    reward = facts / jnp.sqrt(lens)
    center = jnp.zeros((8, 128), F32)
    spread = jnp.zeros((8, 128), F32)
    for g in range(NGROUPS):
        member = used & (ids == float(g))
        mine = jnp.where(member, reward, 0.0)
        total = jnp.sum(jnp.sum(mine, axis=0, keepdims=True), axis=1, keepdims=True)
        square = jnp.sum(jnp.sum(mine * mine, axis=0, keepdims=True), axis=1, keepdims=True)
        mid = total / GROUP
        center = jnp.where(member, mid, center)
        spread = jnp.where(member, square / GROUP - mid * mid, spread)
    advantage = ((reward - center) / jnp.sqrt(spread + var_offset)).astype(BF).astype(F32)
    here = lane == dp
    adv = jnp.sum(jnp.where(here, advantage, 0.0), axis=1, keepdims=True)
    length = jnp.sum(jnp.where(here, lens, 0.0), axis=1, keepdims=True)
    valid = (lane.astype(F32) < length).astype(F32)
    coef = valid * (-adv * jnp.exp(tp) + kl_weight * (1.0 - jnp.exp(tr - tp)))
    coefs[...] = coef
    for s in range(4):
        from_sec = (sec - STEPS[s]) & 3
        row = jnp.concatenate(
            [coefs[pl.ds(from_sec, 1), :], coefs[pl.ds(4 + from_sec, 1), :]], axis=1
        )
        for q in range(4):
            change[128 * q : 128 * (q + 1), 256 * s : 256 * (s + 1)] = (
                shares[s][256 + 128 * q : 384 + 128 * q, :].astype(F32) * row
            ).astype(BF)
    grads = [
        jnp.dot(change[:, 0:256], s0[0:256, :], preferred_element_type=F32),
        jnp.dot(change[...], other[...], preferred_element_type=F32),
    ]
    for s in range(1, 4):
        grads[0] += jnp.dot(
            change[:, 256 * s : 256 * (s + 1)], shares[s][0:256, :], preferred_element_type=F32
        )
    for u, grad in ((core, grads[0]), (1 - core, grads[1])):
        grad = grad.astype(BF)
        for h in range(2):
            for q in range(4):
                out[handler(zh, 2 * u + h, q), 0:128, :] = grad[
                    128 * q : 128 * (q + 1), 128 * h : 128 * (h + 1)
                ]
    old = old_logp[...].astype(F32)
    logp = jnp.concatenate(
        [
            old[q : q + 1] + jnp.sum(jnp.where(at == 4 * q + sec, tp, 0.0), axis=0, keepdims=True)
            for q in range(2)
        ],
        axis=1,
    )
    hi, mid, lo = split3(logp)
    rows = jnp.concatenate([hi, mid, lo, jnp.zeros((5, 256), F32)], axis=0).astype(BF)
    place = (lax.broadcasted_iota(jnp.int32, (16 * SLOT, 256), 0) == slots[...]).astype(F32)
    placed = lax.dot_general(rows, place.astype(BF), NT, preferred_element_type=F32)
    for a in range(4):
        tail = placed[:, 128 * a : 128 * (a + 1)].astype(BF)
        for k in range(4):
            out[4 * a + k, 128:136, :] = tail


def finish_kernel(parts, grad, packed):
    dp = dp_index()
    total = parts[0, 0:128, :].astype(F32)
    for i in range(1, 16):
        total = total + parts[i, 0:128, :].astype(F32)
    grad[...] = total.T
    rows = [
        jnp.sum(parts[i, 128:136, :].astype(F32), axis=0, keepdims=True) for i in range(16)
    ]
    table = jnp.concatenate(rows, axis=0)
    pick = jnp.zeros((16, SLOT), F32)
    for a in range(4):
        pick = jnp.where(lax.rem(dp, 4) == a, table[:, SLOT * a : SLOT * (a + 1)], pick)
    packed[...] = jnp.concatenate([pick[i : i + 1, 0:CAP] for i in range(16)], axis=1)


def cost(flops, size):
    return pl.CostEstimate(flops=flops, bytes_accessed=size, transcendentals=0)


def shape(dims, dtype):
    return jax.ShapeDtypeStruct(dims, dtype)


def call(kernel, outs, scratch=(), smem=0, inputs=0, flops=0, size=0, vmem_mib=16):
    vmem = pl.BlockSpec(memory_space=pltpu.VMEM)
    scalar = pl.BlockSpec(memory_space=pltpu.SMEM)
    return pl.pallas_call(
        kernel,
        out_shape=outs,
        in_specs=[scalar] * smem + [vmem] * inputs,
        out_specs=jax.tree.map(lambda _: vmem, outs),
        scratch_shapes=list(scratch),
        cost_estimate=cost(flops, size),
        compiler_params=pltpu.CompilerParams(vmem_limit_bytes=vmem_mib << 20),
    )


def flat(i, zh, core, sec):
    return ((i * 4 + zh) * 2 + core) * 4 + sec


TO_HANDLER = [
    (flat(i, zz, core, sec), flat(handler(i >> 2, i & 3, zz), i >> 2, core, sec))
    for i in range(16)
    for zz in range(4)
    for core in range(2)
    for sec in range(4)
]
TO_OWNER = [(b, a) for a, b in TO_HANDLER]


def ring(step):
    return [(j, (j + step) % 4) for j in range(4)]


def body(
    states, direction, old_logp, lengths, group_ids, routes, reward_head, policy_k, reference_k
):
    dir_t, w_t = call(
        turn_kernel,
        (shape((4, 128, 256), BF), shape((256, 128), BF)),
        inputs=3,
        flops=1 << 16,
        size=1 << 18,
        vmem_mib=60,
    )(direction, policy_k, reference_k)
    w_here = lax.ppermute(w_t, ALL, TO_HANDLER)
    quarters, extra, slots = call(
        prepare_kernel,
        (shape((4, 256, 256), BF), shape((16, 128), BF), shape((1, 256), jnp.int32)),
        smem=2,
        inputs=3,
        flops=8 * 256 * 1024 * 2,
        size=1 << 20,
        vmem_mib=60,
    )(lengths, group_ids, states, reward_head.reshape(8, 128), routes.reshape(1, 256))
    dirs = lax.all_to_all(dir_t, "zh", 0, 0, tiled=True)
    anywhere = pl.BlockSpec(memory_space=pl.ANY)
    weights = pl.pallas_call(
        spread_kernel,
        out_shape=shape((16, 272, 128), BF),
        in_specs=[anywhere, pl.BlockSpec(memory_space=pltpu.HBM)],
        out_specs=anywhere,
        scratch_shapes=[pltpu.SemaphoreType.DMA((32,))],
        cost_estimate=cost(1 << 10, 1 << 20),
        compiler_params=pltpu.CompilerParams(vmem_limit_bytes=16 << 20),
    )(w_here, extra)
    weights = lax.all_to_all(weights, DP, 0, 0, tiled=True)
    packs = call(
        pack_kernel, (shape((768, 256), BF),) * 4, inputs=2, flops=1 << 10, size=3 << 20
    )(quarters, dirs)
    shares = [packs[0]] + [lax.ppermute(packs[n], "sec", ring(STEPS[n])) for n in (1, 2, 3)]
    other = lax.ppermute(
        jnp.concatenate([share[0:256] for share in shares], axis=0), "core", [(0, 1), (1, 0)]
    )
    pay = call(
        terms_kernel, shape((24, 128), F32), inputs=6, flops=1 << 30, size=4 << 20
    )(*shares, other, weights)
    pays = call(join_kernel, shape((16, 24, 128), F32), inputs=2, flops=1 << 12, size=1 << 18)(
        pay, lax.ppermute(pay, "core", [(0, 1), (1, 0)])
    )
    pays = lax.all_to_all(pays, ("zh", "sec"), 0, 0, tiled=True)
    parts = call(
        grads_kernel,
        shape((16, 136, 128), BF),
        scratch=[
            pltpu.VMEM((512, 1024), BF),
            pltpu.VMEM((8, 128), F32),
        ],
        inputs=8,
        flops=1 << 29,
        size=4 << 20,
    )(pays, *shares, other, old_logp.reshape(2, 128), slots)
    parts = lax.all_to_all(parts, DP, 0, 0, tiled=True)
    grad, packed = call(
        finish_kernel,
        (shape((128, 128), F32), shape((1, 320), F32)),
        inputs=1,
        flops=1 << 20,
        size=1 << 20,
    )(parts)
    return lax.ppermute(grad, ALL, TO_OWNER), packed.reshape(1, 1, 320)


def solution(mesh):
    fine = Mesh(mesh.devices.reshape(2, 8, 4, 2, 4), ALL)
    rows, cols = ("zl", "y", "sec"), ("zh", "core")
    return jax.shard_map(
        body,
        mesh=fine,
        in_specs=(
            P(rows, cols),
            P(rows, cols),
            P(rows),
            P(rows),
            P(rows),
            P(rows, None),
            P(cols),
            P(rows, cols),
            P(rows, cols),
        ),
        out_specs=(P(rows, cols), P(DP, "sec", None)),
        check_vma=False,
    )
```

```python
import jax
import jax.numpy as jnp
from jax import lax
from jax.experimental import pallas as pl
from jax.experimental.pallas import tpu as pltpu
from jax.sharding import Mesh
from jax.sharding import PartitionSpec as P

GROUP = 8
NGROUPS = 16
CAP = 20
SLOT = 32

STEPS = (0, 2, 1, 3)

kl_weight = 0.4
var_offset = 0.25

DP = ("zl", "y")
ALL = ("zl", "y", "zh", "core", "sec")
BF = jnp.bfloat16
F32 = jnp.float32
NT = (((1,), (1,)), ((), ()))


def split3(x):
    hi = x.astype(BF).astype(F32)
    rest = x - hi
    mid = rest.astype(BF).astype(F32)
    return hi, mid, rest - mid


def dp_index():
    return lax.axis_index("zl") * 8 + lax.axis_index("y")


def handler(zh, block, zz):
    turn = (zz - zh + (zh >> 1)) & 3
    zl = (turn & 1) ^ (turn >> 1)
    near = 4 * (zh & 1)
    y = near + block + (1 - (turn >> 1)) * (7 - 2 * block)
    return zl * 8 + (y & 7)


def turn_kernel(direction, wp, wr, dir_t, w_t):
    turned = direction[...].astype(F32).T.astype(BF)
    for k in range(4):
        dir_t[k] = turned
    w_t[0:128, :] = wp[...].astype(F32).T.astype(BF)
    w_t[128:256, :] = wr[...].astype(F32).T.astype(BF)


def prepare_kernel(lengths, group_ids, states, head, routes, quarters, extra, slots):
    sec = lax.axis_index("sec")
    for k in range(4):
        to = lax.rem(k - sec + 4, 4)
        quarters[to, :, 0:128] = states[:, 128 * k : 128 * (k + 1)]
        quarters[to, :, 128:256] = states[:, 512 + 128 * k : 512 + 128 * (k + 1)]
    head_rows = head[...].astype(F32)
    wide_head = jnp.concatenate([head_rows[k : k + 1] for k in range(8)], axis=1).astype(BF)
    score = lax.dot_general(
        jnp.broadcast_to(wide_head, (8, 1024)), states[...], NT, preferred_element_type=F32
    )
    lane = lax.broadcasted_iota(jnp.int32, (1, 128), 1)
    rows = []
    for q in range(2):
        valid = (lane < lengths[q]).astype(F32)
        part = jnp.sum(score[0:1, 128 * q : 128 * (q + 1)] * valid, axis=1, keepdims=True)
        rows.extend(split3(part))
    for values in (group_ids, lengths):
        for q in range(2):
            rows.append(jnp.full((1, 1), values[q], jnp.int32).astype(F32))
    at = lax.broadcasted_iota(jnp.int32, (16, 128), 0)
    block = jnp.zeros((16, 128), F32)
    for n, row in enumerate(rows):
        block = jnp.where(at == n, row, block)
    extra[...] = block.astype(BF)
    target = routes[...]
    choose = (lax.broadcasted_iota(jnp.int32, (16, 256), 0) == target).astype(F32)
    before = (
        lax.broadcasted_iota(jnp.int32, (256, 256), 0)
        < lax.broadcasted_iota(jnp.int32, (256, 256), 1)
    ).astype(F32)
    ranked = jnp.dot(choose.astype(BF), before.astype(BF), preferred_element_type=F32)
    rank = jnp.sum(choose * ranked, axis=0, keepdims=True)
    slots[...] = target * SLOT + rank.astype(jnp.int32)


def pack_kernel(quarters, dirs, *outs):
    for k in range(4):
        outs[k][0:256, :] = quarters[STEPS[k]]
        for q in range(4):
            outs[k][256 + 128 * q : 384 + 128 * q, :] = dirs[q]


def spread_kernel(w, extra, out, sems):
    copies = []
    for k in range(16):
        copies.append(pltpu.make_async_copy(w, out.at[k, 0:256, :], sems.at[k]))
        copies.append(pltpu.make_async_copy(extra, out.at[k, 256:272, :], sems.at[16 + k]))
    for copy in copies:
        copy.start()
    for copy in copies:
        copy.wait()


def terms_kernel(s0, s1, s2, s3, o0, o1, weights, pay):
    shares = (s0, s1, s2, s3)
    zh, core, sec = (lax.axis_index(name) for name in ("zh", "core", "sec"))
    acc = [jnp.zeros((2, 256), F32) for _ in range(4)]
    for q in range(4):
        mats = [
            jnp.concatenate(
                [weights[handler(zh, 2 * u + h, q), 0:256, :] for h in range(2)], axis=1
            )
            for u in (core, 1 - core)
        ]
        for s, share in enumerate(shares):
            key = lax.dot_general(mats[0], share[0:256, :], NT, preferred_element_type=F32)
            key += lax.dot_general(
                mats[1],
                (o0, o1)[s >> 1][256 * (s & 1) : 256 * (s & 1) + 256, :],
                NT, preferred_element_type=F32
            )
            wide = share[256 + 128 * q : 384 + 128 * q, :].astype(F32)
            acc[s] += jnp.concatenate(
                [
                    jnp.sum(wide * key[0:128], axis=0, keepdims=True),
                    jnp.sum(wide * key[128:256], axis=0, keepdims=True),
                ],
                axis=0,
            )
    for s in range(4):
        for p in range(2):
            for q in range(2):
                pay[pl.ds(8 * p + 4 * q + ((sec - STEPS[s]) & 3), 1), :] = acc[s][
                    p : p + 1, 128 * q : 128 * (q + 1)
                ]
    lane = lax.broadcasted_iota(jnp.int32, (16, 128), 1)
    block = jnp.zeros((16, 128), F32)
    for i in range(16):
        block = jnp.where((lane & 15) == i, weights[i, 256:272, :].astype(F32), block)
    fields = [block[0:1] + block[1:2] + block[2:3], block[3:4] + block[4:5] + block[5:6]]
    fields.extend(block[n : n + 1] for n in range(6, 10))
    facts = jnp.zeros((1, 128), F32)
    for n, field in enumerate(fields):
        facts = jnp.where((lane[0:1] >> 4) == n, field, facts)
    pay[16:24, :] = jnp.broadcast_to(facts, (8, 128))


def join_kernel(mine, partner, out):
    whole = mine[...] + partner[...]
    for d in range(16):
        out[d] = whole


def grads_kernel(pays, s0, s1, s2, s3, o0, o1, old_logp, slots, out, change, coefs):
    shares = (s0, s1, s2, s3)
    zh, core, sec = (lax.axis_index(name) for name in ("zh", "core", "sec"))
    dp = dp_index()
    sums = pays[0, 0:16, :]
    for d in range(1, 16):
        sums = sums + pays[d, 0:16, :]
    tp, tr = sums[0:8], sums[8:16]
    facts = []
    for s in range(4):
        fact = pays[s, 16:17, :]
        for d in range(1, 4):
            fact = fact + pays[4 * d + s, 16:17, :]
        facts.append(fact)
    facts = jnp.concatenate(facts + facts, axis=0)
    lane = lax.broadcasted_iota(jnp.int32, (8, 128), 1)
    at = lax.broadcasted_iota(jnp.int32, (8, 128), 0)
    facts = jnp.where(at < 4, facts, pltpu.roll(facts, 112, 1))
    used = lane < 16
    ids = pltpu.roll(facts, 96, 1) * 0.125
    lens = jnp.where(used, pltpu.roll(facts, 64, 1) * 0.125, 1.0)
    reward = facts / jnp.sqrt(lens)
    center = jnp.zeros((8, 128), F32)
    spread = jnp.zeros((8, 128), F32)
    for g in range(NGROUPS):
        member = used & (ids == float(g))
        mine = jnp.where(member, reward, 0.0)
        total = jnp.sum(jnp.sum(mine, axis=0, keepdims=True), axis=1, keepdims=True)
        square = jnp.sum(jnp.sum(mine * mine, axis=0, keepdims=True), axis=1, keepdims=True)
        mid = total / GROUP
        center = jnp.where(member, mid, center)
        spread = jnp.where(member, square / GROUP - mid * mid, spread)
    advantage = ((reward - center) / jnp.sqrt(spread + var_offset)).astype(BF).astype(F32)
    here = lane == dp
    adv = jnp.sum(jnp.where(here, advantage, 0.0), axis=1, keepdims=True)
    length = jnp.sum(jnp.where(here, lens, 0.0), axis=1, keepdims=True)
    valid = (lane.astype(F32) < length).astype(F32)
    coef = valid * (-adv * jnp.exp(tp) + kl_weight * (1.0 - jnp.exp(tr - tp)))
    coefs[...] = coef
    for s in range(4):
        from_sec = (sec - STEPS[s]) & 3
        row = jnp.concatenate(
            [coefs[pl.ds(from_sec, 1), :], coefs[pl.ds(4 + from_sec, 1), :]], axis=1
        )
        for q in range(4):
            change[128 * q : 128 * (q + 1), 256 * s : 256 * (s + 1)] = (
                shares[s][256 + 128 * q : 384 + 128 * q, :].astype(F32) * row
            ).astype(BF)
    grads = [
        jnp.dot(change[:, 0:256], s0[0:256, :], preferred_element_type=F32),
        jnp.dot(change[:, 0:512], o0[...], preferred_element_type=F32),
    ]
    grads[1] += jnp.dot(change[:, 512:1024], o1[...], preferred_element_type=F32)
    for s in range(1, 4):
        grads[0] += jnp.dot(
            change[:, 256 * s : 256 * (s + 1)], shares[s][0:256, :], preferred_element_type=F32
        )
    for u, grad in ((core, grads[0]), (1 - core, grads[1])):
        grad = grad.astype(BF)
        for h in range(2):
            for q in range(4):
                out[handler(zh, 2 * u + h, q), 0:128, :] = grad[
                    128 * q : 128 * (q + 1), 128 * h : 128 * (h + 1)
                ]
    old = old_logp[...].astype(F32)
    logp = jnp.concatenate(
        [
            old[q : q + 1] + jnp.sum(jnp.where(at == 4 * q + sec, tp, 0.0), axis=0, keepdims=True)
            for q in range(2)
        ],
        axis=1,
    )
    hi, mid, lo = split3(logp)
    rows = jnp.concatenate([hi, mid, lo, jnp.zeros((5, 256), F32)], axis=0).astype(BF)
    place = (lax.broadcasted_iota(jnp.int32, (16 * SLOT, 256), 0) == slots[...]).astype(F32)
    placed = lax.dot_general(rows, place.astype(BF), NT, preferred_element_type=F32)
    for a in range(4):
        tail = placed[:, 128 * a : 128 * (a + 1)].astype(BF)
        for k in range(4):
            out[4 * a + k, 128:136, :] = tail


def finish_kernel(parts, grad, packed):
    dp = dp_index()
    total = parts[0, 0:128, :].astype(F32)
    for i in range(1, 16):
        total = total + parts[i, 0:128, :].astype(F32)
    grad[...] = total.T
    rows = [
        jnp.sum(parts[i, 128:136, :].astype(F32), axis=0, keepdims=True) for i in range(16)
    ]
    table = jnp.concatenate(rows, axis=0)
    pick = jnp.zeros((16, SLOT), F32)
    for a in range(4):
        pick = jnp.where(lax.rem(dp, 4) == a, table[:, SLOT * a : SLOT * (a + 1)], pick)
    packed[...] = jnp.concatenate([pick[i : i + 1, 0:CAP] for i in range(16)], axis=1)


def cost(flops, size):
    return pl.CostEstimate(flops=flops, bytes_accessed=size, transcendentals=0)


def shape(dims, dtype):
    return jax.ShapeDtypeStruct(dims, dtype)


def call(kernel, outs, scratch=(), smem=0, inputs=0, flops=0, size=0, vmem_mib=16):
    vmem = pl.BlockSpec(memory_space=pltpu.VMEM)
    scalar = pl.BlockSpec(memory_space=pltpu.SMEM)
    return pl.pallas_call(
        kernel,
        out_shape=outs,
        in_specs=[scalar] * smem + [vmem] * inputs,
        out_specs=jax.tree.map(lambda _: vmem, outs),
        scratch_shapes=list(scratch),
        cost_estimate=cost(flops, size),
        compiler_params=pltpu.CompilerParams(vmem_limit_bytes=vmem_mib << 20),
    )


def flat(i, zh, core, sec):
    return ((i * 4 + zh) * 2 + core) * 4 + sec


TO_HANDLER = [
    (flat(i, zz, core, sec), flat(handler(i >> 2, i & 3, zz), i >> 2, core, sec))
    for i in range(16)
    for zz in range(4)
    for core in range(2)
    for sec in range(4)
]
TO_OWNER = [(b, a) for a, b in TO_HANDLER]


def ring(step):
    return [(j, (j + step) % 4) for j in range(4)]


def body(
    states, direction, old_logp, lengths, group_ids, routes, reward_head, policy_k, reference_k
):
    dir_t, w_t = call(
        turn_kernel,
        (shape((4, 128, 256), BF), shape((256, 128), BF)),
        inputs=3,
        flops=1 << 16,
        size=1 << 18,
        vmem_mib=60,
    )(direction, policy_k, reference_k)
    w_here = lax.ppermute(w_t, ALL, TO_HANDLER)
    quarters, extra, slots = call(
        prepare_kernel,
        (shape((4, 256, 256), BF), shape((16, 128), BF), shape((1, 256), jnp.int32)),
        smem=2,
        inputs=3,
        flops=8 * 256 * 1024 * 2,
        size=1 << 20,
    )(lengths, group_ids, states, reward_head.reshape(8, 128), routes.reshape(1, 256))
    dirs = lax.all_to_all(dir_t, "zh", 0, 0, tiled=True)
    anywhere = pl.BlockSpec(memory_space=pl.ANY)
    weights = pl.pallas_call(
        spread_kernel,
        out_shape=shape((16, 272, 128), BF),
        in_specs=[anywhere, pl.BlockSpec(memory_space=pltpu.HBM)],
        out_specs=anywhere,
        scratch_shapes=[pltpu.SemaphoreType.DMA((32,))],
        cost_estimate=cost(1 << 10, 1 << 20),
        compiler_params=pltpu.CompilerParams(vmem_limit_bytes=16 << 20),
    )(w_here, extra)
    weights = lax.all_to_all(weights, DP, 0, 0, tiled=True)
    packs = call(
        pack_kernel, (shape((768, 256), BF),) * 4, inputs=2, flops=1 << 10, size=3 << 20
    )(quarters, dirs)
    shares = [packs[0]] + [lax.ppermute(packs[n], "sec", ring(STEPS[n])) for n in (1, 2, 3)]
    others = [
        lax.ppermute(
            jnp.concatenate([share[0:256] for share in pair], axis=0), "core", [(0, 1), (1, 0)]
        )
        for pair in (shares[0:2], shares[2:4])
    ]
    pay = call(
        terms_kernel, shape((24, 128), F32), inputs=7, flops=1 << 30, size=4 << 20
    )(*shares, *others, weights)
    pays = call(join_kernel, shape((16, 24, 128), F32), inputs=2, flops=1 << 12, size=1 << 18)(
        pay, lax.ppermute(pay, "core", [(0, 1), (1, 0)])
    )
    pays = lax.all_to_all(pays, ("zh", "sec"), 0, 0, tiled=True)
    parts = call(
        grads_kernel,
        shape((16, 136, 128), BF),
        scratch=[
            pltpu.VMEM((512, 1024), BF),
            pltpu.VMEM((8, 128), F32),
        ],
        inputs=9,
        flops=1 << 29,
        size=4 << 20,
    )(pays, *shares, *others, old_logp.reshape(2, 128), slots)
    parts = lax.all_to_all(parts, DP, 0, 0, tiled=True)
    grad, packed = call(
        finish_kernel,
        (shape((128, 128), F32), shape((1, 320), F32)),
        inputs=1,
        flops=1 << 20,
        size=1 << 20,
    )(parts)
    return lax.ppermute(grad, ALL, TO_OWNER), packed.reshape(1, 1, 320)


def solution(mesh):
    fine = Mesh(mesh.devices.reshape(2, 8, 4, 2, 4), ALL)
    rows, cols = ("zl", "y", "sec"), ("zh", "core")
    return jax.shard_map(
        body,
        mesh=fine,
        in_specs=(
            P(rows, cols),
            P(rows, cols),
            P(rows),
            P(rows),
            P(rows),
            P(rows, None),
            P(cols),
            P(rows, cols),
            P(rows, cols),
        ),
        out_specs=(P(rows, cols), P(DP, "sec", None)),
        check_vma=False,
    )
```

```python
import jax
import jax.numpy as jnp
from jax import lax
from jax.experimental import pallas as pl
from jax.experimental.pallas import tpu as pltpu
from jax.sharding import Mesh
from jax.sharding import PartitionSpec as P

GROUP = 8
NGROUPS = 16
CAP = 20
SLOT = 32

STEPS = (0, 2, 1, 3)

kl_weight = 0.4
var_offset = 0.25

DP = ("zl", "y")
ALL = ("zl", "y", "zh", "core", "sec")
BF = jnp.bfloat16
F32 = jnp.float32
NT = (((1,), (1,)), ((), ()))


def split3(x):
    hi = x.astype(BF).astype(F32)
    rest = x - hi
    mid = rest.astype(BF).astype(F32)
    return hi, mid, rest - mid


def dp_index():
    return lax.axis_index("zl") * 8 + lax.axis_index("y")


def handler(zh, block, zz):
    turn = (zz - zh + (zh >> 1)) & 3
    zl = (turn & 1) ^ (turn >> 1)
    near = 4 * (zh & 1)
    y = near + block + (1 - (turn >> 1)) * (7 - 2 * block)
    return zl * 8 + (y & 7)


def turn_kernel(direction, wp, wr, dir_t, w_t):
    turned = direction[...].T
    for k in range(4):
        dir_t[k] = turned
    w_t[0:128, :] = wp[...].T
    w_t[128:256, :] = wr[...].T


def prepare_kernel(lengths, group_ids, states, head, routes, quarters, extra, slots):
    sec = lax.axis_index("sec")
    for k in range(4):
        to = lax.rem(k - sec + 4, 4)
        quarters[to, :, 0:128] = states[:, 128 * k : 128 * (k + 1)]
        quarters[to, :, 128:256] = states[:, 512 + 128 * k : 512 + 128 * (k + 1)]
    head_rows = head[...].astype(F32)
    wide_head = jnp.concatenate([head_rows[k : k + 1] for k in range(8)], axis=1).astype(BF)
    score = lax.dot_general(
        jnp.broadcast_to(wide_head, (8, 1024)), states[...], NT, preferred_element_type=F32
    )
    lane = lax.broadcasted_iota(jnp.int32, (1, 128), 1)
    parts = []
    for q in range(2):
        valid = (lane < lengths[q]).astype(F32)
        part = jnp.sum(score[0:1, 128 * q : 128 * (q + 1)] * valid, axis=1, keepdims=True)
        numbers = [jnp.full((1, 1), n[q], jnp.int32).astype(F32) for n in (group_ids, lengths)]
        parts.append([*split3(part), *numbers])
    at = lax.broadcasted_iota(jnp.int32, (8, 128), 0)
    block = jnp.zeros((8, 128), F32)
    for n in range(5):
        block = jnp.where(at == n, jnp.where(lane < 64, parts[0][n], parts[1][n]), block)
    extra[...] = block.astype(BF)
    target = routes[...]
    choose = (lax.broadcasted_iota(jnp.int32, (16, 256), 0) == target).astype(F32)
    before = (
        lax.broadcasted_iota(jnp.int32, (256, 256), 0)
        < lax.broadcasted_iota(jnp.int32, (256, 256), 1)
    ).astype(F32)
    ranked = jnp.dot(choose.astype(BF), before.astype(BF), preferred_element_type=F32)
    rank = jnp.sum(choose * ranked, axis=0, keepdims=True)
    slots[...] = target * SLOT + rank.astype(jnp.int32)


def pack_kernel(quarters, dirs, *outs):
    for k in range(4):
        outs[k][0:256, :] = quarters[STEPS[k]]
        for q in range(4):
            outs[k][256 + 128 * q : 384 + 128 * q, :] = dirs[q]


def spread_kernel(w, extra, out, sems):
    copies = []
    for k in range(16):
        copies.append(pltpu.make_async_copy(w, out.at[k, 0:256, :], sems.at[k]))
        copies.append(pltpu.make_async_copy(extra, out.at[k, 256:264, :], sems.at[16 + k]))
    for copy in copies:
        copy.start()
    for copy in copies:
        copy.wait()


def terms_kernel(s0, s1, s2, s3, o0, o1, weights, pay):
    shares = (s0, s1, s2, s3)
    zh, core, sec = (lax.axis_index(name) for name in ("zh", "core", "sec"))
    acc = [jnp.zeros((2, 256), F32) for _ in range(4)]
    for q in range(4):
        mats = [
            jnp.concatenate(
                [weights[handler(zh, 2 * u + h, q), 0:256, :] for h in range(2)], axis=1
            )
            for u in (core, 1 - core)
        ]
        for s, share in enumerate(shares):
            key = lax.dot_general(mats[0], share[0:256, :], NT, preferred_element_type=F32)
            key += lax.dot_general(
                mats[1],
                (o0, o1)[s >> 1][256 * (s & 1) : 256 * (s & 1) + 256, :],
                NT, preferred_element_type=F32
            )
            wide = share[256 + 128 * q : 384 + 128 * q, :].astype(F32)
            acc[s] += jnp.concatenate(
                [
                    jnp.sum(wide * key[0:128], axis=0, keepdims=True),
                    jnp.sum(wide * key[128:256], axis=0, keepdims=True),
                ],
                axis=0,
            )
    for s in range(4):
        for p in range(2):
            for q in range(2):
                pay[pl.ds(8 * p + 4 * q + ((sec - STEPS[s]) & 3), 1), :] = acc[s][
                    p : p + 1, 128 * q : 128 * (q + 1)
                ]
    lane = lax.broadcasted_iota(jnp.int32, (8, 128), 1)
    block = jnp.zeros((8, 128), F32)
    for i in range(16):
        block = jnp.where((lane & 15) == i, weights[i, 256:264, :].astype(F32), block)
    field = (lane[0:1] >> 4) & 3
    facts = jnp.where(field == 0, block[0:1] + block[1:2] + block[2:3], 0.0)
    facts = jnp.where(field == 1, block[3:4], facts)
    facts = jnp.where(field == 2, block[4:5], facts)
    pay[16:24, :] = jnp.broadcast_to(facts, (8, 128))


def join_kernel(mine, partner, out):
    whole = mine[...] + partner[...]
    for d in range(16):
        out[d] = whole


def grads_kernel(pays, s0, s1, s2, s3, o0, o1, old_logp, slots, out, change, coefs):
    shares = (s0, s1, s2, s3)
    zh, core, sec = (lax.axis_index(name) for name in ("zh", "core", "sec"))
    dp = dp_index()
    sums = pays[0, 0:16, :]
    for d in range(1, 16):
        sums = sums + pays[d, 0:16, :]
    tp, tr = sums[0:8], sums[8:16]
    facts = []
    for s in range(4):
        fact = pays[s, 16:17, :]
        for d in range(1, 4):
            fact = fact + pays[4 * d + s, 16:17, :]
        facts.append(fact)
    facts = jnp.concatenate(facts + facts, axis=0)
    lane = lax.broadcasted_iota(jnp.int32, (8, 128), 1)
    at = lax.broadcasted_iota(jnp.int32, (8, 128), 0)
    facts = jnp.where(at < 4, facts, pltpu.roll(facts, 64, 1))
    used = lane < 16
    ids = pltpu.roll(facts, 112, 1) * 0.125
    lens = jnp.where(used, pltpu.roll(facts, 96, 1) * 0.125, 1.0)
    reward = facts / jnp.sqrt(lens)
    center = jnp.zeros((8, 128), F32)
    spread = jnp.zeros((8, 128), F32)
    for g in range(NGROUPS):
        member = used & (ids == float(g))
        mine = jnp.where(member, reward, 0.0)
        total = jnp.sum(jnp.sum(mine, axis=0, keepdims=True), axis=1, keepdims=True)
        square = jnp.sum(jnp.sum(mine * mine, axis=0, keepdims=True), axis=1, keepdims=True)
        mid = total / GROUP
        center = jnp.where(member, mid, center)
        spread = jnp.where(member, square / GROUP - mid * mid, spread)
    advantage = ((reward - center) / jnp.sqrt(spread + var_offset)).astype(BF).astype(F32)
    here = lane == dp
    adv = jnp.sum(jnp.where(here, advantage, 0.0), axis=1, keepdims=True)
    length = jnp.sum(jnp.where(here, lens, 0.0), axis=1, keepdims=True)
    valid = (lane.astype(F32) < length).astype(F32)
    coef = valid * (-adv * jnp.exp(tp) + kl_weight * (1.0 - jnp.exp(tr - tp)))
    coefs[...] = coef
    for s in range(4):
        from_sec = (sec - STEPS[s]) & 3
        row = jnp.concatenate(
            [coefs[pl.ds(from_sec, 1), :], coefs[pl.ds(4 + from_sec, 1), :]], axis=1
        )
        for q in range(4):
            change[128 * q : 128 * (q + 1), 256 * s : 256 * (s + 1)] = (
                shares[s][256 + 128 * q : 384 + 128 * q, :].astype(F32) * row
            ).astype(BF)
    grads = [
        jnp.dot(change[:, 0:256], s0[0:256, :], preferred_element_type=F32),
        jnp.dot(change[:, 0:512], o0[...], preferred_element_type=F32),
    ]
    grads[1] += jnp.dot(change[:, 512:1024], o1[...], preferred_element_type=F32)
    for s in range(1, 4):
        grads[0] += jnp.dot(
            change[:, 256 * s : 256 * (s + 1)], shares[s][0:256, :], preferred_element_type=F32
        )
    for u, grad in ((core, grads[0]), (1 - core, grads[1])):
        grad = grad.astype(BF)
        for h in range(2):
            for q in range(4):
                out[handler(zh, 2 * u + h, q), 0:128, :] = grad[
                    128 * q : 128 * (q + 1), 128 * h : 128 * (h + 1)
                ]
    old = old_logp[...].astype(F32)
    logp = jnp.concatenate(
        [
            old[q : q + 1] + jnp.sum(jnp.where(at == 4 * q + sec, tp, 0.0), axis=0, keepdims=True)
            for q in range(2)
        ],
        axis=1,
    )
    hi, mid, lo = split3(logp)
    rows = jnp.concatenate([hi, mid, lo, jnp.zeros((5, 256), F32)], axis=0).astype(BF)
    place = (lax.broadcasted_iota(jnp.int32, (16 * SLOT, 256), 0) == slots[...]).astype(F32)
    placed = lax.dot_general(rows, place.astype(BF), NT, preferred_element_type=F32)
    for a in range(4):
        tail = placed[:, 128 * a : 128 * (a + 1)].astype(BF)
        for k in range(4):
            out[4 * a + k, 128:136, :] = tail


def finish_kernel(parts, grad):
    total = parts[0, 0:128, :].astype(F32)
    for i in range(1, 16):
        total = total + parts[i, 0:128, :].astype(F32)
    grad[...] = total.T


def pick_kernel(parts, packed):
    dp = dp_index()
    rows = [
        jnp.sum(parts[i, 128:136, :].astype(F32), axis=0, keepdims=True) for i in range(16)
    ]
    table = jnp.concatenate(rows, axis=0)
    pick = jnp.zeros((16, SLOT), F32)
    for a in range(4):
        pick = jnp.where(lax.rem(dp, 4) == a, table[:, SLOT * a : SLOT * (a + 1)], pick)
    packed[...] = jnp.concatenate([pick[i : i + 1, 0:CAP] for i in range(16)], axis=1)


def cost(flops, size):
    return pl.CostEstimate(flops=flops, bytes_accessed=size, transcendentals=0)


def shape(dims, dtype):
    return jax.ShapeDtypeStruct(dims, dtype)


def call(kernel, outs, scratch=(), smem=0, inputs=0, flops=0, size=0, vmem_mib=16):
    vmem = pl.BlockSpec(memory_space=pltpu.VMEM)
    scalar = pl.BlockSpec(memory_space=pltpu.SMEM)
    return pl.pallas_call(
        kernel,
        out_shape=outs,
        in_specs=[scalar] * smem + [vmem] * inputs,
        out_specs=jax.tree.map(lambda _: vmem, outs),
        scratch_shapes=list(scratch),
        cost_estimate=cost(flops, size),
        compiler_params=pltpu.CompilerParams(vmem_limit_bytes=vmem_mib << 20),
    )


def flat(i, zh, core, sec):
    return ((i * 4 + zh) * 2 + core) * 4 + sec


TO_HANDLER = [
    (flat(i, zz, core, sec), flat(handler(i >> 2, i & 3, zz), i >> 2, core, sec))
    for i in range(16)
    for zz in range(4)
    for core in range(2)
    for sec in range(4)
]
TO_OWNER = [(b, a) for a, b in TO_HANDLER]


def ring(step):
    return [(j, (j + step) % 4) for j in range(4)]


def body(
    states, direction, old_logp, lengths, group_ids, routes, reward_head, policy_k, reference_k
):
    dir_t, w_t = call(
        turn_kernel,
        (shape((4, 128, 256), BF), shape((256, 128), BF)),
        inputs=3,
        flops=1 << 16,
        size=1 << 18,
        vmem_mib=60,
    )(direction, policy_k, reference_k)
    w_here = lax.ppermute(w_t, ALL, TO_HANDLER)
    quarters, extra, slots = call(
        prepare_kernel,
        (shape((4, 256, 256), BF), shape((8, 128), BF), shape((1, 256), jnp.int32)),
        smem=2,
        inputs=3,
        flops=8 * 256 * 1024 * 2,
        size=1 << 20,
    )(lengths, group_ids, states, reward_head.reshape(8, 128), routes.reshape(1, 256))
    dirs = lax.all_to_all(dir_t, "zh", 0, 0, tiled=True)
    anywhere = pl.BlockSpec(memory_space=pl.ANY)
    weights = pl.pallas_call(
        spread_kernel,
        out_shape=shape((16, 264, 128), BF),
        in_specs=[anywhere, pl.BlockSpec(memory_space=pltpu.HBM)],
        out_specs=anywhere,
        scratch_shapes=[pltpu.SemaphoreType.DMA((32,))],
        cost_estimate=cost(1 << 10, 1 << 20),
        compiler_params=pltpu.CompilerParams(vmem_limit_bytes=16 << 20),
    )(w_here, extra)
    weights = lax.all_to_all(weights, DP, 0, 0, tiled=True)
    packs = call(
        pack_kernel, (shape((768, 256), BF),) * 4, inputs=2, flops=1 << 10, size=3 << 20
    )(quarters, dirs)
    shares = [packs[0]] + [lax.ppermute(packs[n], "sec", ring(STEPS[n])) for n in (1, 2, 3)]
    others = [
        lax.ppermute(
            jnp.concatenate([share[0:256] for share in pair], axis=0), "core", [(0, 1), (1, 0)]
        )
        for pair in (shares[0:2], shares[2:4])
    ]
    pay = call(
        terms_kernel, shape((24, 128), F32), inputs=7, flops=1 << 30, size=4 << 20
    )(*shares, *others, weights)
    pays = call(join_kernel, shape((16, 24, 128), F32), inputs=2, flops=1 << 12, size=1 << 18)(
        pay, lax.ppermute(pay, "core", [(0, 1), (1, 0)])
    )
    pays = lax.all_to_all(pays, ("zh", "sec"), 0, 0, tiled=True)
    parts = call(
        grads_kernel,
        shape((16, 136, 128), BF),
        scratch=[
            pltpu.VMEM((512, 1024), BF),
            pltpu.VMEM((8, 128), F32),
        ],
        inputs=9,
        flops=1 << 29,
        size=4 << 20,
    )(pays, *shares, *others, old_logp.reshape(2, 128), slots)
    parts = lax.all_to_all(parts, DP, 0, 0, tiled=True)
    grad = call(
        finish_kernel, shape((128, 128), F32), inputs=1, flops=1 << 20, size=1 << 20
    )(parts)
    packed = call(pick_kernel, shape((1, 320), F32), inputs=1, flops=1 << 10, size=1 << 16)(parts)
    return lax.ppermute(grad, ALL, TO_OWNER), packed.reshape(1, 1, 320)


def solution(mesh):
    fine = Mesh(mesh.devices.reshape(2, 8, 4, 2, 4), ALL)
    rows, cols = ("zl", "y", "sec"), ("zh", "core")
    return jax.shard_map(
        body,
        mesh=fine,
        in_specs=(
            P(rows, cols),
            P(rows, cols),
            P(rows),
            P(rows),
            P(rows),
            P(rows, None),
            P(cols),
            P(rows, cols),
            P(rows, cols),
        ),
        out_specs=(P(rows, cols), P(DP, "sec", None)),
        check_vma=False,
    )
```

```python
import jax
import jax.numpy as jnp
from jax import lax
from jax.experimental import pallas as pl
from jax.experimental.pallas import tpu as pltpu
from jax.sharding import Mesh
from jax.sharding import PartitionSpec as P

GROUP = 8
NGROUPS = 16
CAP = 20
SLOT = 32

STEPS = (0, 2, 1, 3)

kl_weight = 0.4
var_offset = 0.25

DP = ("zl", "y")
ALL = ("zl", "y", "zh", "core", "sec")
BF = jnp.bfloat16
F32 = jnp.float32
NT = (((1,), (1,)), ((), ()))


def split3(x):
    hi = x.astype(BF).astype(F32)
    rest = x - hi
    mid = rest.astype(BF).astype(F32)
    return hi, mid, rest - mid


def dp_index():
    return lax.axis_index("zl") * 8 + lax.axis_index("y")


def handler(zh, block, zz):
    turn = (zz - zh + (zh >> 1)) & 3
    zl = (turn & 1) ^ (turn >> 1)
    near = 4 * (zh & 1)
    y = near + block + (1 - (turn >> 1)) * (7 - 2 * block)
    return zl * 8 + (y & 7)


def turn_kernel(direction, wp, wr, dir_t, w_t):
    turned = direction[...].T
    for k in range(4):
        dir_t[k] = turned
    w_t[0:128, :] = wp[...].T
    w_t[128:256, :] = wr[...].T


def prepare_kernel(lengths, group_ids, states, head, routes, quarters, extra, slots):
    sec = lax.axis_index("sec")
    for k in range(4):
        to = lax.rem(k - sec + 4, 4)
        quarters[to, :, 0:128] = states[:, 128 * k : 128 * (k + 1)]
        quarters[to, :, 128:256] = states[:, 512 + 128 * k : 512 + 128 * (k + 1)]
    head_rows = head[...].astype(F32)
    wide_head = jnp.concatenate([head_rows[k : k + 1] for k in range(8)], axis=1).astype(BF)
    score = lax.dot_general(
        jnp.broadcast_to(wide_head, (8, 1024)), states[...], NT, preferred_element_type=F32
    )
    lane = lax.broadcasted_iota(jnp.int32, (1, 128), 1)
    parts = []
    for q in range(2):
        valid = (lane < lengths[q]).astype(F32)
        part = jnp.sum(score[0:1, 128 * q : 128 * (q + 1)] * valid, axis=1, keepdims=True)
        numbers = [jnp.full((1, 1), n[q], jnp.int32).astype(F32) for n in (group_ids, lengths)]
        parts.append([*split3(part), *numbers])
    at = lax.broadcasted_iota(jnp.int32, (8, 128), 0)
    block = jnp.zeros((8, 128), F32)
    for n in range(5):
        block = jnp.where(at == n, jnp.where(lane < 64, parts[0][n], parts[1][n]), block)
    extra[...] = block.astype(BF)
    target = routes[...]
    choose = (lax.broadcasted_iota(jnp.int32, (16, 256), 0) == target).astype(F32)
    before = (
        lax.broadcasted_iota(jnp.int32, (256, 256), 0)
        < lax.broadcasted_iota(jnp.int32, (256, 256), 1)
    ).astype(F32)
    ranked = jnp.dot(choose.astype(BF), before.astype(BF), preferred_element_type=F32)
    rank = jnp.sum(choose * ranked, axis=0, keepdims=True)
    slots[...] = target * SLOT + rank.astype(jnp.int32)


def pack_kernel(quarters, dirs, *outs):
    for k in range(4):
        outs[k][0:256, :] = quarters[STEPS[k]]
        for q in range(4):
            outs[k][256 + 128 * q : 384 + 128 * q, :] = dirs[q]


def spread_kernel(w, extra, out, block, sems):
    block[0:256, :] = w[...]
    block[256:264, :] = extra[...]
    copies = [pltpu.make_async_copy(block, out.at[k], sems.at[k]) for k in range(16)]
    for copy in copies:
        copy.start()
    for copy in copies:
        copy.wait()


def terms_kernel(s0, s1, s2, s3, o0, o1, weights, pay):
    shares = (s0, s1, s2, s3)
    zh, core, sec = (lax.axis_index(name) for name in ("zh", "core", "sec"))
    acc = [jnp.zeros((2, 256), F32) for _ in range(4)]
    for q in range(4):
        mats = [
            jnp.concatenate(
                [weights[handler(zh, 2 * u + h, q), 0:256, :] for h in range(2)], axis=1
            )
            for u in (core, 1 - core)
        ]
        for s, share in enumerate(shares):
            key = lax.dot_general(mats[0], share[0:256, :], NT, preferred_element_type=F32)
            key += lax.dot_general(
                mats[1],
                (o0, o1)[s >> 1][256 * (s & 1) : 256 * (s & 1) + 256, :],
                NT, preferred_element_type=F32
            )
            wide = share[256 + 128 * q : 384 + 128 * q, :].astype(F32)
            acc[s] += jnp.concatenate(
                [
                    jnp.sum(wide * key[0:128], axis=0, keepdims=True),
                    jnp.sum(wide * key[128:256], axis=0, keepdims=True),
                ],
                axis=0,
            )
    for s in range(4):
        for p in range(2):
            for q in range(2):
                pay[pl.ds(8 * p + 4 * q + ((sec - STEPS[s]) & 3), 1), :] = acc[s][
                    p : p + 1, 128 * q : 128 * (q + 1)
                ]
    lane = lax.broadcasted_iota(jnp.int32, (8, 128), 1)
    block = jnp.zeros((8, 128), F32)
    for i in range(16):
        block = jnp.where((lane & 15) == i, weights[i, 256:264, :].astype(F32), block)
    field = (lane[0:1] >> 4) & 3
    facts = jnp.where(field == 0, block[0:1] + block[1:2] + block[2:3], 0.0)
    facts = jnp.where(field == 1, block[3:4], facts)
    facts = jnp.where(field == 2, block[4:5], facts)
    pay[16:24, :] = jnp.broadcast_to(facts, (8, 128))


def join_kernel(mine, partner, out):
    whole = mine[...] + partner[...]
    for d in range(16):
        out[d] = whole


def grads_kernel(pays, s0, s1, s2, s3, o0, o1, old_logp, slots, out, change, coefs):
    shares = (s0, s1, s2, s3)
    zh, core, sec = (lax.axis_index(name) for name in ("zh", "core", "sec"))
    dp = dp_index()
    sums = pays[0, 0:16, :]
    for d in range(1, 16):
        sums = sums + pays[d, 0:16, :]
    tp, tr = sums[0:8], sums[8:16]
    facts = []
    for s in range(4):
        fact = pays[s, 16:17, :]
        for d in range(1, 4):
            fact = fact + pays[4 * d + s, 16:17, :]
        facts.append(fact)
    facts = jnp.concatenate(facts + facts, axis=0)
    lane = lax.broadcasted_iota(jnp.int32, (8, 128), 1)
    at = lax.broadcasted_iota(jnp.int32, (8, 128), 0)
    facts = jnp.where(at < 4, facts, pltpu.roll(facts, 64, 1))
    used = lane < 16
    ids = pltpu.roll(facts, 112, 1) * 0.125
    lens = jnp.where(used, pltpu.roll(facts, 96, 1) * 0.125, 1.0)
    reward = facts / jnp.sqrt(lens)
    center = jnp.zeros((8, 128), F32)
    spread = jnp.zeros((8, 128), F32)
    for g in range(NGROUPS):
        member = used & (ids == float(g))
        mine = jnp.where(member, reward, 0.0)
        total = jnp.sum(jnp.sum(mine, axis=0, keepdims=True), axis=1, keepdims=True)
        square = jnp.sum(jnp.sum(mine * mine, axis=0, keepdims=True), axis=1, keepdims=True)
        mid = total / GROUP
        center = jnp.where(member, mid, center)
        spread = jnp.where(member, square / GROUP - mid * mid, spread)
    advantage = ((reward - center) / jnp.sqrt(spread + var_offset)).astype(BF).astype(F32)
    here = lane == dp
    adv = jnp.sum(jnp.where(here, advantage, 0.0), axis=1, keepdims=True)
    length = jnp.sum(jnp.where(here, lens, 0.0), axis=1, keepdims=True)
    valid = (lane.astype(F32) < length).astype(F32)
    coef = valid * (-adv * jnp.exp(tp) + kl_weight * (1.0 - jnp.exp(tr - tp)))
    coefs[...] = coef
    for s in range(4):
        from_sec = (sec - STEPS[s]) & 3
        row = jnp.concatenate(
            [coefs[pl.ds(from_sec, 1), :], coefs[pl.ds(4 + from_sec, 1), :]], axis=1
        )
        for q in range(4):
            change[128 * q : 128 * (q + 1), 256 * s : 256 * (s + 1)] = (
                shares[s][256 + 128 * q : 384 + 128 * q, :].astype(F32) * row
            ).astype(BF)
    grads = [
        jnp.dot(change[:, 0:256], s0[0:256, :], preferred_element_type=F32),
        jnp.dot(change[:, 0:512], o0[...], preferred_element_type=F32),
    ]
    grads[1] += jnp.dot(change[:, 512:1024], o1[...], preferred_element_type=F32)
    for s in range(1, 4):
        grads[0] += jnp.dot(
            change[:, 256 * s : 256 * (s + 1)], shares[s][0:256, :], preferred_element_type=F32
        )
    for u, grad in ((core, grads[0]), (1 - core, grads[1])):
        grad = grad.astype(BF)
        for h in range(2):
            for q in range(4):
                out[handler(zh, 2 * u + h, q), 0:128, :] = grad[
                    128 * q : 128 * (q + 1), 128 * h : 128 * (h + 1)
                ]
    old = old_logp[...].astype(F32)
    logp = jnp.concatenate(
        [
            old[q : q + 1] + jnp.sum(jnp.where(at == 4 * q + sec, tp, 0.0), axis=0, keepdims=True)
            for q in range(2)
        ],
        axis=1,
    )
    hi, mid, lo = split3(logp)
    rows = jnp.concatenate([hi, mid, lo, jnp.zeros((5, 256), F32)], axis=0).astype(BF)
    place = (lax.broadcasted_iota(jnp.int32, (16 * SLOT, 256), 0) == slots[...]).astype(F32)
    placed = lax.dot_general(rows, place.astype(BF), NT, preferred_element_type=F32)
    for a in range(4):
        tail = placed[:, 128 * a : 128 * (a + 1)].astype(BF)
        for k in range(4):
            out[4 * a + k, 128:136, :] = tail


def finish_kernel(parts, grad):
    total = parts[0, 0:128, :].astype(F32)
    for i in range(1, 16):
        total = total + parts[i, 0:128, :].astype(F32)
    grad[...] = total.T


def pick_kernel(parts, packed):
    dp = dp_index()
    rows = [
        jnp.sum(parts[i, 128:136, :].astype(F32), axis=0, keepdims=True) for i in range(16)
    ]
    table = jnp.concatenate(rows, axis=0)
    pick = jnp.zeros((16, SLOT), F32)
    for a in range(4):
        pick = jnp.where(lax.rem(dp, 4) == a, table[:, SLOT * a : SLOT * (a + 1)], pick)
    packed[...] = jnp.concatenate([pick[i : i + 1, 0:CAP] for i in range(16)], axis=1)


def cost(flops, size):
    return pl.CostEstimate(flops=flops, bytes_accessed=size, transcendentals=0)


def shape(dims, dtype):
    return jax.ShapeDtypeStruct(dims, dtype)


def call(kernel, outs, scratch=(), smem=0, inputs=0, flops=0, size=0, vmem_mib=16):
    vmem = pl.BlockSpec(memory_space=pltpu.VMEM)
    scalar = pl.BlockSpec(memory_space=pltpu.SMEM)
    return pl.pallas_call(
        kernel,
        out_shape=outs,
        in_specs=[scalar] * smem + [vmem] * inputs,
        out_specs=jax.tree.map(lambda _: vmem, outs),
        scratch_shapes=list(scratch),
        cost_estimate=cost(flops, size),
        compiler_params=pltpu.CompilerParams(vmem_limit_bytes=vmem_mib << 20),
    )


def flat(i, zh, core, sec):
    return ((i * 4 + zh) * 2 + core) * 4 + sec


TO_HANDLER = [
    (flat(i, zz, core, sec), flat(handler(i >> 2, i & 3, zz), i >> 2, core, sec))
    for i in range(16)
    for zz in range(4)
    for core in range(2)
    for sec in range(4)
]
TO_OWNER = [(b, a) for a, b in TO_HANDLER]


def ring(step):
    return [(j, (j + step) % 4) for j in range(4)]


def body(
    states, direction, old_logp, lengths, group_ids, routes, reward_head, policy_k, reference_k
):
    dir_t, w_t = call(
        turn_kernel,
        (shape((4, 128, 256), BF), shape((256, 128), BF)),
        inputs=3,
        flops=1 << 16,
        size=1 << 18,
        vmem_mib=60,
    )(direction, policy_k, reference_k)
    w_here = lax.ppermute(w_t, ALL, TO_HANDLER)
    quarters, extra, slots = call(
        prepare_kernel,
        (shape((4, 256, 256), BF), shape((8, 128), BF), shape((1, 256), jnp.int32)),
        smem=2,
        inputs=3,
        flops=8 * 256 * 1024 * 2,
        size=1 << 20,
    )(lengths, group_ids, states, reward_head.reshape(8, 128), routes.reshape(1, 256))
    dirs = lax.all_to_all(dir_t, "zh", 0, 0, tiled=True)
    anywhere = pl.BlockSpec(memory_space=pl.ANY)
    weights = pl.pallas_call(
        spread_kernel,
        out_shape=shape((16, 264, 128), BF),
        in_specs=[pl.BlockSpec(memory_space=pltpu.VMEM)] * 2,
        out_specs=anywhere,
        scratch_shapes=[pltpu.VMEM((264, 128), BF), pltpu.SemaphoreType.DMA((16,))],
        cost_estimate=cost(1 << 10, 1 << 20),
        compiler_params=pltpu.CompilerParams(vmem_limit_bytes=16 << 20),
    )(w_here, extra)
    weights = lax.all_to_all(weights, DP, 0, 0, tiled=True)
    packs = call(
        pack_kernel, (shape((768, 256), BF),) * 4, inputs=2, flops=1 << 10, size=3 << 20
    )(quarters, dirs)
    shares = [packs[0]] + [lax.ppermute(packs[n], "sec", ring(STEPS[n])) for n in (1, 2, 3)]
    others = [
        lax.ppermute(
            jnp.concatenate([share[0:256] for share in pair], axis=0), "core", [(0, 1), (1, 0)]
        )
        for pair in (shares[0:2], shares[2:4])
    ]
    pay = call(
        terms_kernel, shape((24, 128), F32), inputs=7, flops=1 << 30, size=4 << 20
    )(*shares, *others, weights)
    pays = call(join_kernel, shape((16, 24, 128), F32), inputs=2, flops=1 << 12, size=1 << 18)(
        pay, lax.ppermute(pay, "core", [(0, 1), (1, 0)])
    )
    pays = lax.all_to_all(pays, ("zh", "sec"), 0, 0, tiled=True)
    parts = call(
        grads_kernel,
        shape((16, 136, 128), BF),
        scratch=[
            pltpu.VMEM((512, 1024), BF),
            pltpu.VMEM((8, 128), F32),
        ],
        inputs=9,
        flops=1 << 29,
        size=4 << 20,
    )(pays, *shares, *others, old_logp.reshape(2, 128), slots)
    parts = lax.all_to_all(parts, DP, 0, 0, tiled=True)
    grad = call(
        finish_kernel, shape((128, 128), F32), inputs=1, flops=1 << 20, size=1 << 20
    )(parts)
    packed = call(pick_kernel, shape((1, 320), F32), inputs=1, flops=1 << 10, size=1 << 16)(parts)
    return lax.ppermute(grad, ALL, TO_OWNER), packed.reshape(1, 1, 320)


def solution(mesh):
    fine = Mesh(mesh.devices.reshape(2, 8, 4, 2, 4), ALL)
    rows, cols = ("zl", "y", "sec"), ("zh", "core")
    return jax.shard_map(
        body,
        mesh=fine,
        in_specs=(
            P(rows, cols),
            P(rows, cols),
            P(rows),
            P(rows),
            P(rows),
            P(rows, None),
            P(cols),
            P(rows, cols),
            P(rows, cols),
        ),
        out_specs=(P(rows, cols), P(DP, "sec", None)),
        check_vma=False,
    )
```

```python
import jax
import jax.numpy as jnp
from jax import lax
from jax.experimental import pallas as pl
from jax.experimental.pallas import tpu as pltpu
from jax.sharding import Mesh
from jax.sharding import PartitionSpec as P

GROUP = 8
NGROUPS = 16
CAP = 20
SLOT = 32

STEPS = (0, 2, 1, 3)

kl_weight = 0.4
var_offset = 0.25

DP = ("zl", "y")
ALL = ("zl", "y", "zh", "core", "sec")
BF = jnp.bfloat16
F32 = jnp.float32
NT = (((1,), (1,)), ((), ()))


def split3(x):
    hi = x.astype(BF).astype(F32)
    rest = x - hi
    mid = rest.astype(BF).astype(F32)
    return hi, mid, rest - mid


def dp_index():
    return lax.axis_index("zl") * 8 + lax.axis_index("y")


def handler(zh, block, zz):
    turn = (zz - zh + (zh >> 1)) & 3
    zl = (turn & 1) ^ (turn >> 1)
    near = 4 * (zh & 1)
    y = near + block + (1 - (turn >> 1)) * (7 - 2 * block)
    return zl * 8 + (y & 7)


def turn_kernel(direction, wp, wr, dir_t, w_t):
    turned = direction[...].T
    for k in range(4):
        dir_t[k] = turned
    w_t[0:128, :] = wp[...].T
    w_t[128:256, :] = wr[...].T


def prepare_kernel(lengths, group_ids, states, head, quarters, extra):
    sec = lax.axis_index("sec")
    for k in range(4):
        to = lax.rem(k - sec + 4, 4)
        quarters[to, :, 0:128] = states[:, 128 * k : 128 * (k + 1)]
        quarters[to, :, 128:256] = states[:, 512 + 128 * k : 512 + 128 * (k + 1)]
    head_rows = head[...].astype(F32)
    wide_head = jnp.concatenate([head_rows[k : k + 1] for k in range(8)], axis=1).astype(BF)
    score = lax.dot_general(
        jnp.broadcast_to(wide_head, (8, 1024)), states[...], NT, preferred_element_type=F32
    )
    lane = lax.broadcasted_iota(jnp.int32, (1, 128), 1)
    parts = []
    for q in range(2):
        valid = (lane < lengths[q]).astype(F32)
        part = jnp.sum(score[0:1, 128 * q : 128 * (q + 1)] * valid, axis=1, keepdims=True)
        numbers = [jnp.full((1, 1), n[q], jnp.int32).astype(F32) for n in (group_ids, lengths)]
        parts.append([*split3(part), *numbers])
    at = lax.broadcasted_iota(jnp.int32, (8, 128), 0)
    block = jnp.zeros((8, 128), F32)
    for n in range(5):
        block = jnp.where(at == n, jnp.where(lane < 64, parts[0][n], parts[1][n]), block)
    extra[...] = block.astype(BF)


def pack_kernel(quarters, dirs, *outs):
    for k in range(4):
        outs[k][0:256, :] = quarters[STEPS[k]]
        for q in range(4):
            outs[k][256 + 128 * q : 384 + 128 * q, :] = dirs[q]


def spread_kernel(w, extra, out, block, sems):
    block[0:256, :] = w[...]
    block[256:264, :] = extra[...]
    copies = [pltpu.make_async_copy(block, out.at[k], sems.at[k]) for k in range(16)]
    for copy in copies:
        copy.start()
    for copy in copies:
        copy.wait()


def terms_kernel(s0, s1, s2, s3, o0, o1, weights, pay):
    shares = (s0, s1, s2, s3)
    zh, core, sec = (lax.axis_index(name) for name in ("zh", "core", "sec"))
    acc = [jnp.zeros((2, 256), F32) for _ in range(4)]
    for q in range(4):
        mats = [
            jnp.concatenate(
                [weights[handler(zh, 2 * u + h, q), 0:256, :] for h in range(2)], axis=1
            )
            for u in (core, 1 - core)
        ]
        for s, share in enumerate(shares):
            key = lax.dot_general(mats[0], share[0:256, :], NT, preferred_element_type=F32)
            key += lax.dot_general(
                mats[1],
                (o0, o1)[s >> 1][256 * (s & 1) : 256 * (s & 1) + 256, :],
                NT, preferred_element_type=F32
            )
            wide = share[256 + 128 * q : 384 + 128 * q, :].astype(F32)
            acc[s] += jnp.concatenate(
                [
                    jnp.sum(wide * key[0:128], axis=0, keepdims=True),
                    jnp.sum(wide * key[128:256], axis=0, keepdims=True),
                ],
                axis=0,
            )
    for s in range(4):
        for p in range(2):
            for q in range(2):
                pay[pl.ds(8 * p + 4 * q + ((sec - STEPS[s]) & 3), 1), :] = acc[s][
                    p : p + 1, 128 * q : 128 * (q + 1)
                ]
    lane = lax.broadcasted_iota(jnp.int32, (8, 128), 1)
    block = jnp.zeros((8, 128), F32)
    for i in range(16):
        block = jnp.where((lane & 15) == i, weights[i, 256:264, :].astype(F32), block)
    field = (lane[0:1] >> 4) & 3
    facts = jnp.where(field == 0, block[0:1] + block[1:2] + block[2:3], 0.0)
    facts = jnp.where(field == 1, block[3:4], facts)
    facts = jnp.where(field == 2, block[4:5], facts)
    pay[16:24, :] = jnp.broadcast_to(facts, (8, 128))


def join_kernel(mine, partner, out):
    whole = mine[...] + partner[...]
    for d in range(16):
        out[d] = whole


def grads_kernel(pays, s0, s1, s2, s3, o0, o1, old_logp, routes, out, change, coefs):
    shares = (s0, s1, s2, s3)
    zh, core, sec = (lax.axis_index(name) for name in ("zh", "core", "sec"))
    dp = dp_index()
    sums = pays[0, 0:16, :]
    for d in range(1, 16):
        sums = sums + pays[d, 0:16, :]
    tp, tr = sums[0:8], sums[8:16]
    facts = []
    for s in range(4):
        fact = pays[s, 16:17, :]
        for d in range(1, 4):
            fact = fact + pays[4 * d + s, 16:17, :]
        facts.append(fact)
    facts = jnp.concatenate(facts + facts, axis=0)
    lane = lax.broadcasted_iota(jnp.int32, (8, 128), 1)
    at = lax.broadcasted_iota(jnp.int32, (8, 128), 0)
    facts = jnp.where(at < 4, facts, pltpu.roll(facts, 64, 1))
    used = lane < 16
    ids = pltpu.roll(facts, 112, 1) * 0.125
    lens = jnp.where(used, pltpu.roll(facts, 96, 1) * 0.125, 1.0)
    reward = facts / jnp.sqrt(lens)
    center = jnp.zeros((8, 128), F32)
    spread = jnp.zeros((8, 128), F32)
    for g in range(NGROUPS):
        member = used & (ids == float(g))
        mine = jnp.where(member, reward, 0.0)
        total = jnp.sum(jnp.sum(mine, axis=0, keepdims=True), axis=1, keepdims=True)
        square = jnp.sum(jnp.sum(mine * mine, axis=0, keepdims=True), axis=1, keepdims=True)
        mid = total / GROUP
        center = jnp.where(member, mid, center)
        spread = jnp.where(member, square / GROUP - mid * mid, spread)
    advantage = ((reward - center) / jnp.sqrt(spread + var_offset)).astype(BF).astype(F32)
    here = lane == dp
    adv = jnp.sum(jnp.where(here, advantage, 0.0), axis=1, keepdims=True)
    length = jnp.sum(jnp.where(here, lens, 0.0), axis=1, keepdims=True)
    valid = (lane.astype(F32) < length).astype(F32)
    coef = valid * (-adv * jnp.exp(tp) + kl_weight * (1.0 - jnp.exp(tr - tp)))
    coefs[...] = coef
    for s in range(4):
        from_sec = (sec - STEPS[s]) & 3
        row = jnp.concatenate(
            [coefs[pl.ds(from_sec, 1), :], coefs[pl.ds(4 + from_sec, 1), :]], axis=1
        )
        for q in range(4):
            change[128 * q : 128 * (q + 1), 256 * s : 256 * (s + 1)] = (
                shares[s][256 + 128 * q : 384 + 128 * q, :].astype(F32) * row
            ).astype(BF)
    grads = [
        jnp.dot(change[:, 0:256], s0[0:256, :], preferred_element_type=F32),
        jnp.dot(change[:, 0:512], o0[...], preferred_element_type=F32),
    ]
    grads[1] += jnp.dot(change[:, 512:1024], o1[...], preferred_element_type=F32)
    for s in range(1, 4):
        grads[0] += jnp.dot(
            change[:, 256 * s : 256 * (s + 1)], shares[s][0:256, :], preferred_element_type=F32
        )
    for u, grad in ((core, grads[0]), (1 - core, grads[1])):
        grad = grad.astype(BF)
        for h in range(2):
            for q in range(4):
                out[handler(zh, 2 * u + h, q), 0:128, :] = grad[
                    128 * q : 128 * (q + 1), 128 * h : 128 * (h + 1)
                ]
    old = old_logp[...].astype(F32)
    logp = jnp.concatenate(
        [
            old[q : q + 1] + jnp.sum(jnp.where(at == 4 * q + sec, tp, 0.0), axis=0, keepdims=True)
            for q in range(2)
        ],
        axis=1,
    )
    hi, mid, lo = split3(logp)
    rows = jnp.concatenate([hi, mid, lo, jnp.zeros((5, 256), F32)], axis=0).astype(BF)
    target = routes[...]
    choose = (lax.broadcasted_iota(jnp.int32, (16, 256), 0) == target).astype(F32)
    before = (
        lax.broadcasted_iota(jnp.int32, (256, 256), 0)
        < lax.broadcasted_iota(jnp.int32, (256, 256), 1)
    ).astype(F32)
    ranked = jnp.dot(choose.astype(BF), before.astype(BF), preferred_element_type=F32)
    rank = jnp.sum(choose * ranked, axis=0, keepdims=True)
    slots = target * SLOT + rank.astype(jnp.int32)
    place = (lax.broadcasted_iota(jnp.int32, (16 * SLOT, 256), 0) == slots).astype(F32)
    placed = lax.dot_general(rows, place.astype(BF), NT, preferred_element_type=F32)
    for a in range(4):
        tail = placed[:, 128 * a : 128 * (a + 1)].astype(BF)
        for k in range(4):
            out[4 * a + k, 128:136, :] = tail


def finish_kernel(parts, grad):
    total = parts[0, 0:128, :].astype(F32)
    for i in range(1, 16):
        total = total + parts[i, 0:128, :].astype(F32)
    grad[...] = total.T


def pick_kernel(parts, packed):
    dp = dp_index()
    rows = [
        jnp.sum(parts[i, 128:136, :].astype(F32), axis=0, keepdims=True) for i in range(16)
    ]
    table = jnp.concatenate(rows, axis=0)
    pick = jnp.zeros((16, SLOT), F32)
    for a in range(4):
        pick = jnp.where(lax.rem(dp, 4) == a, table[:, SLOT * a : SLOT * (a + 1)], pick)
    packed[...] = jnp.concatenate([pick[i : i + 1, 0:CAP] for i in range(16)], axis=1)


def cost(flops, size):
    return pl.CostEstimate(flops=flops, bytes_accessed=size, transcendentals=0)


def shape(dims, dtype):
    return jax.ShapeDtypeStruct(dims, dtype)


def call(kernel, outs, scratch=(), smem=0, inputs=0, flops=0, size=0, vmem_mib=16):
    vmem = pl.BlockSpec(memory_space=pltpu.VMEM)
    scalar = pl.BlockSpec(memory_space=pltpu.SMEM)
    return pl.pallas_call(
        kernel,
        out_shape=outs,
        in_specs=[scalar] * smem + [vmem] * inputs,
        out_specs=jax.tree.map(lambda _: vmem, outs),
        scratch_shapes=list(scratch),
        cost_estimate=cost(flops, size),
        compiler_params=pltpu.CompilerParams(vmem_limit_bytes=vmem_mib << 20),
    )


def flat(i, zh, core, sec):
    return ((i * 4 + zh) * 2 + core) * 4 + sec


TO_HANDLER = [
    (flat(i, zz, core, sec), flat(handler(i >> 2, i & 3, zz), i >> 2, core, sec))
    for i in range(16)
    for zz in range(4)
    for core in range(2)
    for sec in range(4)
]
TO_OWNER = [(b, a) for a, b in TO_HANDLER]


def ring(step):
    return [(j, (j + step) % 4) for j in range(4)]


def body(
    states, direction, old_logp, lengths, group_ids, routes, reward_head, policy_k, reference_k
):
    dir_t, w_t = call(
        turn_kernel,
        (shape((4, 128, 256), BF), shape((256, 128), BF)),
        inputs=3,
        flops=1 << 16,
        size=1 << 18,
        vmem_mib=60,
    )(direction, policy_k, reference_k)
    w_here = lax.ppermute(w_t, ALL, TO_HANDLER)
    quarters, extra = call(
        prepare_kernel,
        (shape((4, 256, 256), BF), shape((8, 128), BF)),
        smem=2,
        inputs=2,
        flops=8 * 256 * 1024 * 2,
        size=1 << 20,
    )(lengths, group_ids, states, reward_head.reshape(8, 128))
    dirs = lax.all_to_all(dir_t, "zh", 0, 0, tiled=True)
    anywhere = pl.BlockSpec(memory_space=pl.ANY)
    weights = pl.pallas_call(
        spread_kernel,
        out_shape=shape((16, 264, 128), BF),
        in_specs=[pl.BlockSpec(memory_space=pltpu.VMEM)] * 2,
        out_specs=anywhere,
        scratch_shapes=[pltpu.VMEM((264, 128), BF), pltpu.SemaphoreType.DMA((16,))],
        cost_estimate=cost(1 << 10, 1 << 20),
        compiler_params=pltpu.CompilerParams(vmem_limit_bytes=16 << 20),
    )(w_here, extra)
    weights = lax.all_to_all(weights, DP, 0, 0, tiled=True)
    packs = call(
        pack_kernel, (shape((768, 256), BF),) * 4, inputs=2, flops=1 << 10, size=3 << 20
    )(quarters, dirs)
    shares = [packs[0]] + [lax.ppermute(packs[n], "sec", ring(STEPS[n])) for n in (1, 2, 3)]
    others = [
        lax.ppermute(
            jnp.concatenate([share[0:256] for share in pair], axis=0), "core", [(0, 1), (1, 0)]
        )
        for pair in (shares[0:2], shares[2:4])
    ]
    pay = call(
        terms_kernel, shape((24, 128), F32), inputs=7, flops=1 << 30, size=4 << 20
    )(*shares, *others, weights)
    pays = call(join_kernel, shape((16, 24, 128), F32), inputs=2, flops=1 << 12, size=1 << 18)(
        pay, lax.ppermute(pay, "core", [(0, 1), (1, 0)])
    )
    pays = lax.all_to_all(pays, ("zh", "sec"), 0, 0, tiled=True)
    parts = call(
        grads_kernel,
        shape((16, 136, 128), BF),
        scratch=[
            pltpu.VMEM((512, 1024), BF),
            pltpu.VMEM((8, 128), F32),
        ],
        inputs=9,
        flops=1 << 29,
        size=4 << 20,
    )(pays, *shares, *others, old_logp.reshape(2, 128), routes.reshape(1, 256))
    parts = lax.all_to_all(parts, DP, 0, 0, tiled=True)
    grad = call(
        finish_kernel, shape((128, 128), F32), inputs=1, flops=1 << 20, size=1 << 20
    )(parts)
    packed = call(pick_kernel, shape((1, 320), F32), inputs=1, flops=1 << 10, size=1 << 16)(parts)
    return lax.ppermute(grad, ALL, TO_OWNER), packed.reshape(1, 1, 320)


def solution(mesh):
    fine = Mesh(mesh.devices.reshape(2, 8, 4, 2, 4), ALL)
    rows, cols = ("zl", "y", "sec"), ("zh", "core")
    return jax.shard_map(
        body,
        mesh=fine,
        in_specs=(
            P(rows, cols),
            P(rows, cols),
            P(rows),
            P(rows),
            P(rows),
            P(rows, None),
            P(cols),
            P(rows, cols),
            P(rows, cols),
        ),
        out_specs=(P(rows, cols), P(DP, "sec", None)),
        check_vma=False,
    )
```

```python
import jax
import jax.numpy as jnp
from jax import lax
from jax.experimental import pallas as pl
from jax.experimental.pallas import tpu as pltpu
from jax.sharding import Mesh
from jax.sharding import PartitionSpec as P

GROUP = 8
NGROUPS = 16
CAP = 20
SLOT = 32

STEPS = (0, 2, 3, 1)

kl_weight = 0.4
var_offset = 0.25

DP = ("zl", "y")
ALL = ("zl", "y", "zh", "core", "sec")
BF = jnp.bfloat16
F32 = jnp.float32
NT = (((1,), (1,)), ((), ()))


def split3(x):
    hi = x.astype(BF).astype(F32)
    rest = x - hi
    mid = rest.astype(BF).astype(F32)
    return hi, mid, rest - mid


def dp_index():
    return lax.axis_index("zl") * 8 + lax.axis_index("y")


def handler(zh, block, zz):
    turn = (zz - zh + (zh >> 1)) & 3
    zl = (turn & 1) ^ (turn >> 1)
    near = 4 * (zh & 1)
    y = near + block + (1 - (turn >> 1)) * (7 - 2 * block)
    return zl * 8 + (y & 7)


def turn_kernel(direction, wp, wr, dir_t, w_t):
    turned = direction[...].T
    for k in range(4):
        dir_t[k] = turned
    w_t[0:128, :] = wp[...].T
    w_t[128:256, :] = wr[...].T


def prepare_kernel(lengths, group_ids, states, head, routes, quarters, extra, slots):
    sec = lax.axis_index("sec")
    for k in range(4):
        to = lax.rem(k - sec + 4, 4)
        quarters[to, :, 0:128] = states[:, 128 * k : 128 * (k + 1)]
        quarters[to, :, 128:256] = states[:, 512 + 128 * k : 512 + 128 * (k + 1)]
    head_rows = head[...].astype(F32)
    wide_head = jnp.concatenate([head_rows[k : k + 1] for k in range(8)], axis=1).astype(BF)
    score = lax.dot_general(
        jnp.broadcast_to(wide_head, (8, 1024)), states[...], NT, preferred_element_type=F32
    )
    lane = lax.broadcasted_iota(jnp.int32, (1, 128), 1)
    parts = []
    for q in range(2):
        valid = (lane < lengths[q]).astype(F32)
        part = jnp.sum(score[0:1, 128 * q : 128 * (q + 1)] * valid, axis=1, keepdims=True)
        numbers = [jnp.full((1, 1), n[q], jnp.int32).astype(F32) for n in (group_ids, lengths)]
        parts.append([*split3(part), *numbers])
    at = lax.broadcasted_iota(jnp.int32, (8, 128), 0)
    block = jnp.zeros((8, 128), F32)
    for n in range(5):
        block = jnp.where(at == n, jnp.where(lane < 64, parts[0][n], parts[1][n]), block)
    extra[...] = block.astype(BF)
    target = routes[...]
    choose = (lax.broadcasted_iota(jnp.int32, (16, 256), 0) == target).astype(F32)
    before = (
        lax.broadcasted_iota(jnp.int32, (256, 256), 0)
        < lax.broadcasted_iota(jnp.int32, (256, 256), 1)
    ).astype(F32)
    ranked = jnp.dot(choose.astype(BF), before.astype(BF), preferred_element_type=F32)
    rank = jnp.sum(choose * ranked, axis=0, keepdims=True)
    slots[...] = target * SLOT + rank.astype(jnp.int32)


def pack_kernel(quarters, dirs, *outs):
    for k in range(4):
        outs[k][0:256, :] = quarters[STEPS[k]]
        for q in range(4):
            outs[k][256 + 128 * q : 384 + 128 * q, :] = dirs[q]


def spread_kernel(w, extra, out, block, sems):
    block[0:256, :] = w[...]
    block[256:264, :] = extra[...]
    copies = [pltpu.make_async_copy(block, out.at[k], sems.at[k]) for k in range(16)]
    for copy in copies:
        copy.start()
    for copy in copies:
        copy.wait()


def terms_kernel(s0, s1, s2, s3, o0, o1, weights, pay):
    shares = (s0, s1, s2, s3)
    zh, core, sec = (lax.axis_index(name) for name in ("zh", "core", "sec"))
    acc = [jnp.zeros((2, 256), F32) for _ in range(4)]
    for q in range(4):
        mats = [
            jnp.concatenate(
                [weights[handler(zh, 2 * u + h, q), 0:256, :] for h in range(2)], axis=1
            )
            for u in (core, 1 - core)
        ]
        for s, share in enumerate(shares):
            key = lax.dot_general(mats[0], share[0:256, :], NT, preferred_element_type=F32)
            key += lax.dot_general(
                mats[1],
                (o0, o1)[s >> 1][256 * (s & 1) : 256 * (s & 1) + 256, :],
                NT, preferred_element_type=F32
            )
            wide = share[256 + 128 * q : 384 + 128 * q, :].astype(F32)
            acc[s] += jnp.concatenate(
                [
                    jnp.sum(wide * key[0:128], axis=0, keepdims=True),
                    jnp.sum(wide * key[128:256], axis=0, keepdims=True),
                ],
                axis=0,
            )
    for s in range(4):
        for p in range(2):
            for q in range(2):
                pay[pl.ds(8 * p + 4 * q + ((sec - STEPS[s]) & 3), 1), :] = acc[s][
                    p : p + 1, 128 * q : 128 * (q + 1)
                ]
    lane = lax.broadcasted_iota(jnp.int32, (8, 128), 1)
    block = jnp.zeros((8, 128), F32)
    for i in range(16):
        block = jnp.where((lane & 15) == i, weights[i, 256:264, :].astype(F32), block)
    field = (lane[0:1] >> 4) & 3
    facts = jnp.where(field == 0, block[0:1] + block[1:2] + block[2:3], 0.0)
    facts = jnp.where(field == 1, block[3:4], facts)
    facts = jnp.where(field == 2, block[4:5], facts)
    pay[16:24, :] = jnp.broadcast_to(facts, (8, 128))


def join_kernel(mine, partner, out):
    whole = mine[...] + partner[...]
    for d in range(16):
        out[d] = whole


def grads_kernel(pays, s0, s1, s2, s3, o0, o1, old_logp, slots, out, change, coefs):
    shares = (s0, s1, s2, s3)
    zh, core, sec = (lax.axis_index(name) for name in ("zh", "core", "sec"))
    dp = dp_index()
    sums = pays[0, 0:16, :]
    for d in range(1, 16):
        sums = sums + pays[d, 0:16, :]
    tp, tr = sums[0:8], sums[8:16]
    facts = []
    for s in range(4):
        fact = pays[s, 16:17, :]
        for d in range(1, 4):
            fact = fact + pays[4 * d + s, 16:17, :]
        facts.append(fact)
    facts = jnp.concatenate(facts + facts, axis=0)
    lane = lax.broadcasted_iota(jnp.int32, (8, 128), 1)
    at = lax.broadcasted_iota(jnp.int32, (8, 128), 0)
    facts = jnp.where(at < 4, facts, pltpu.roll(facts, 64, 1))
    used = lane < 16
    ids = pltpu.roll(facts, 112, 1) * 0.125
    lens = jnp.where(used, pltpu.roll(facts, 96, 1) * 0.125, 1.0)
    reward = facts / jnp.sqrt(lens)
    center = jnp.zeros((8, 128), F32)
    spread = jnp.zeros((8, 128), F32)
    for g in range(NGROUPS):
        member = used & (ids == float(g))
        mine = jnp.where(member, reward, 0.0)
        total = jnp.sum(jnp.sum(mine, axis=0, keepdims=True), axis=1, keepdims=True)
        square = jnp.sum(jnp.sum(mine * mine, axis=0, keepdims=True), axis=1, keepdims=True)
        mid = total / GROUP
        center = jnp.where(member, mid, center)
        spread = jnp.where(member, square / GROUP - mid * mid, spread)
    advantage = ((reward - center) / jnp.sqrt(spread + var_offset)).astype(BF).astype(F32)
    here = lane == dp
    adv = jnp.sum(jnp.where(here, advantage, 0.0), axis=1, keepdims=True)
    length = jnp.sum(jnp.where(here, lens, 0.0), axis=1, keepdims=True)
    valid = (lane.astype(F32) < length).astype(F32)
    coef = valid * (-adv * jnp.exp(tp) + kl_weight * (1.0 - jnp.exp(tr - tp)))
    coefs[...] = coef
    for s in range(4):
        from_sec = (sec - STEPS[s]) & 3
        row = jnp.concatenate(
            [coefs[pl.ds(from_sec, 1), :], coefs[pl.ds(4 + from_sec, 1), :]], axis=1
        )
        for q in range(4):
            change[128 * q : 128 * (q + 1), 256 * s : 256 * (s + 1)] = (
                shares[s][256 + 128 * q : 384 + 128 * q, :].astype(F32) * row
            ).astype(BF)
    grads = [
        jnp.dot(change[:, 0:256], s0[0:256, :], preferred_element_type=F32),
        jnp.dot(change[:, 0:512], o0[...], preferred_element_type=F32),
    ]
    grads[1] += jnp.dot(change[:, 512:1024], o1[...], preferred_element_type=F32)
    for s in range(1, 4):
        grads[0] += jnp.dot(
            change[:, 256 * s : 256 * (s + 1)], shares[s][0:256, :], preferred_element_type=F32
        )
    for u, grad in ((core, grads[0]), (1 - core, grads[1])):
        grad = grad.astype(BF)
        for h in range(2):
            for q in range(4):
                out[handler(zh, 2 * u + h, q), 0:128, :] = grad[
                    128 * q : 128 * (q + 1), 128 * h : 128 * (h + 1)
                ]
    old = old_logp[...].astype(F32)
    logp = jnp.concatenate(
        [
            old[q : q + 1] + jnp.sum(jnp.where(at == 4 * q + sec, tp, 0.0), axis=0, keepdims=True)
            for q in range(2)
        ],
        axis=1,
    )
    hi, mid, lo = split3(logp)
    rows = jnp.concatenate([hi, mid, lo, jnp.zeros((5, 256), F32)], axis=0).astype(BF)
    place = (lax.broadcasted_iota(jnp.int32, (16 * SLOT, 256), 0) == slots[...]).astype(F32)
    placed = lax.dot_general(rows, place.astype(BF), NT, preferred_element_type=F32)
    for a in range(4):
        tail = placed[:, 128 * a : 128 * (a + 1)].astype(BF)
        for k in range(4):
            out[4 * a + k, 128:136, :] = tail


def finish_kernel(parts, grad):
    total = parts[0, 0:128, :].astype(F32)
    for i in range(1, 16):
        total = total + parts[i, 0:128, :].astype(F32)
    grad[...] = total.T


def pick_kernel(parts, packed):
    dp = dp_index()
    rows = [
        jnp.sum(parts[i, 128:136, :].astype(F32), axis=0, keepdims=True) for i in range(16)
    ]
    table = jnp.concatenate(rows, axis=0)
    pick = jnp.zeros((16, SLOT), F32)
    for a in range(4):
        pick = jnp.where(lax.rem(dp, 4) == a, table[:, SLOT * a : SLOT * (a + 1)], pick)
    packed[...] = jnp.concatenate([pick[i : i + 1, 0:CAP] for i in range(16)], axis=1)


def cost(flops, size):
    return pl.CostEstimate(flops=flops, bytes_accessed=size, transcendentals=0)


def shape(dims, dtype):
    return jax.ShapeDtypeStruct(dims, dtype)


def call(kernel, outs, scratch=(), smem=0, inputs=0, flops=0, size=0, vmem_mib=16):
    vmem = pl.BlockSpec(memory_space=pltpu.VMEM)
    scalar = pl.BlockSpec(memory_space=pltpu.SMEM)
    return pl.pallas_call(
        kernel,
        out_shape=outs,
        in_specs=[scalar] * smem + [vmem] * inputs,
        out_specs=jax.tree.map(lambda _: vmem, outs),
        scratch_shapes=list(scratch),
        cost_estimate=cost(flops, size),
        compiler_params=pltpu.CompilerParams(vmem_limit_bytes=vmem_mib << 20),
    )


def flat(i, zh, core, sec):
    return ((i * 4 + zh) * 2 + core) * 4 + sec


TO_HANDLER = [
    (flat(i, zz, core, sec), flat(handler(i >> 2, i & 3, zz), i >> 2, core, sec))
    for i in range(16)
    for zz in range(4)
    for core in range(2)
    for sec in range(4)
]
TO_OWNER = [(b, a) for a, b in TO_HANDLER]


def ring(step):
    return [(j, (j + step) % 4) for j in range(4)]


def body(
    states, direction, old_logp, lengths, group_ids, routes, reward_head, policy_k, reference_k
):
    dir_t, w_t = call(
        turn_kernel,
        (shape((4, 128, 256), BF), shape((256, 128), BF)),
        inputs=3,
        flops=1 << 16,
        size=1 << 18,
        vmem_mib=60,
    )(direction, policy_k, reference_k)
    w_here = lax.ppermute(w_t, ALL, TO_HANDLER)
    quarters, extra, slots = call(
        prepare_kernel,
        (shape((4, 256, 256), BF), shape((8, 128), BF), shape((1, 256), jnp.int32)),
        smem=2,
        inputs=3,
        flops=8 * 256 * 1024 * 2,
        size=1 << 20,
    )(lengths, group_ids, states, reward_head.reshape(8, 128), routes.reshape(1, 256))
    dirs = lax.all_to_all(dir_t, "zh", 0, 0, tiled=True)
    anywhere = pl.BlockSpec(memory_space=pl.ANY)
    weights = pl.pallas_call(
        spread_kernel,
        out_shape=shape((16, 264, 128), BF),
        in_specs=[pl.BlockSpec(memory_space=pltpu.VMEM)] * 2,
        out_specs=anywhere,
        scratch_shapes=[pltpu.VMEM((264, 128), BF), pltpu.SemaphoreType.DMA((16,))],
        cost_estimate=cost(1 << 10, 1 << 20),
        compiler_params=pltpu.CompilerParams(vmem_limit_bytes=16 << 20),
    )(w_here, extra)
    weights = lax.all_to_all(weights, DP, 0, 0, tiled=True)
    packs = call(
        pack_kernel, (shape((768, 256), BF),) * 4, inputs=2, flops=1 << 10, size=3 << 20
    )(quarters, dirs)
    shares = [packs[0]] + [lax.ppermute(packs[n], "sec", ring(STEPS[n])) for n in (1, 2, 3)]
    others = [
        lax.ppermute(
            jnp.concatenate([share[0:256] for share in pair], axis=0), "core", [(0, 1), (1, 0)]
        )
        for pair in (shares[0:2], shares[2:4])
    ]
    pay = call(
        terms_kernel, shape((24, 128), F32), inputs=7, flops=1 << 30, size=4 << 20
    )(*shares, *others, weights)
    pays = call(join_kernel, shape((16, 24, 128), F32), inputs=2, flops=1 << 12, size=1 << 18)(
        pay, lax.ppermute(pay, "core", [(0, 1), (1, 0)])
    )
    pays = lax.all_to_all(pays, ("zh", "sec"), 0, 0, tiled=True)
    parts = call(
        grads_kernel,
        shape((16, 136, 128), BF),
        scratch=[
            pltpu.VMEM((512, 1024), BF),
            pltpu.VMEM((8, 128), F32),
        ],
        inputs=9,
        flops=1 << 29,
        size=4 << 20,
    )(pays, *shares, *others, old_logp.reshape(2, 128), slots)
    parts = lax.all_to_all(parts, DP, 0, 0, tiled=True)
    grad = call(
        finish_kernel, shape((128, 128), F32), inputs=1, flops=1 << 20, size=1 << 20
    )(parts)
    packed = call(pick_kernel, shape((1, 320), F32), inputs=1, flops=1 << 10, size=1 << 16)(parts)
    return lax.ppermute(grad, ALL, TO_OWNER), packed.reshape(1, 1, 320)


def solution(mesh):
    fine = Mesh(mesh.devices.reshape(2, 8, 4, 2, 4), ALL)
    rows, cols = ("zl", "y", "sec"), ("zh", "core")
    return jax.shard_map(
        body,
        mesh=fine,
        in_specs=(
            P(rows, cols),
            P(rows, cols),
            P(rows),
            P(rows),
            P(rows),
            P(rows, None),
            P(cols),
            P(rows, cols),
            P(rows, cols),
        ),
        out_specs=(P(rows, cols), P(DP, "sec", None)),
        check_vma=False,
    )
```
